32 devices in a mesh: ctx: 8 (over y, x, core), tp: 4 (over z).
Axes of the slice: x: 2, y: 2, z: 4, core: 2. Of those that a mesh axis runs over, the one named last changes fastest.
Arguments:
- tokens: bfloat16 [4096, 2048], P('ctx'), may hold values from -6 to 6
- cotangent: bfloat16 [4096, 2048], P('ctx'), may hold values from -6 to 6
- w_qkv: float32 [3, 2048, 2048], P(None, 'ctx', 'tp'), may hold values from -0.125 to 0.125
- w_out: float32 [2048, 2048], P('tp', 'ctx'), may hold values from -0.75 to 0.75
- w_up: float32 [2048, 8192], P('ctx', 'tp'), may hold values from -0.125 to 0.125
- w_down: float32 [8192, 2048], P('tp', 'ctx'), may hold values from -0.0625 to 0.0625
- norm_gains: float32 [2, 2048], P(None, 'ctx'), may hold values from 0.25 to 1.75
- norm_biases: float32 [2, 2048], P(None, 'ctx'), may hold values from -3 to 3
- m_qkv: float32 [3, 2048, 2048], P(None, 'ctx', 'tp'), may hold values from -0.00024414062 to 0.00024414062
- m_out: float32 [2048, 2048], P('tp', 'ctx'), may hold values from -0.00024414062 to 0.00024414062
- m_up: float32 [2048, 8192], P('ctx', 'tp'), may hold values from -0.00024414062 to 0.00024414062
- m_down: float32 [8192, 2048], P('tp', 'ctx'), may hold values from -0.00024414062 to 0.00024414062
- m_gains: float32 [2, 2048], P(None, 'ctx'), may hold values from -0.00024414062 to 0.00024414062
- m_biases: float32 [2, 2048], P(None, 'ctx'), may hold values from -0.00024414062 to 0.00024414062
- v_qkv: float32 [3, 2048, 2048], P(None, 'ctx', 'tp'), may hold values from 3.9729964e-10 to 3.9729965e-08
- v_out: float32 [2048, 2048], P('tp', 'ctx'), may hold values from 3.9729964e-10 to 3.9729965e-08
- v_up: float32 [2048, 8192], P('ctx', 'tp'), may hold values from 3.9729964e-10 to 3.9729965e-08
- v_down: float32 [8192, 2048], P('tp', 'ctx'), may hold values from 3.9729964e-10 to 3.9729965e-08
- v_gains: float32 [2, 2048], P(None, 'ctx'), may hold values from 3.9729964e-10 to 3.9729965e-08
- v_biases: float32 [2, 2048], P(None, 'ctx'), may hold values from 3.9729964e-10 to 3.9729965e-08
- seq_lengths: int32 [4], replicated, may hold values from 1 to 2048, 4096 in all
- decay_mask: int32 [6], replicated, may hold values 0 or 1
Outputs:
- block_out: bfloat16 [4096, 2048], P('ctx')
- grad_tokens: bfloat16 [4096, 2048], P('ctx')
- grad_norm: float32 [], replicated
- grad_qkv: float32 [3, 2048, 2048], P(None, 'ctx', 'tp')
- grad_out: float32 [2048, 2048], P('tp', 'ctx')
- grad_up: float32 [2048, 8192], P('ctx', 'tp')
- grad_down: float32 [8192, 2048], P('tp', 'ctx')
- grad_gains: float32 [2, 2048], P(None, 'ctx')
- grad_biases: float32 [2, 2048], P(None, 'ctx')
- step_qkv: float32 [3, 2048, 2048], P(None, 'ctx', 'tp')
- step_out: float32 [2048, 2048], P('tp', 'ctx')
- step_up: float32 [2048, 8192], P('ctx', 'tp')
- step_down: float32 [8192, 2048], P('tp', 'ctx')
- step_gains: float32 [2, 2048], P(None, 'ctx')
- step_biases: float32 [2, 2048], P(None, 'ctx')
- first_qkv: float32 [3, 2048, 2048], P(None, 'ctx', 'tp')
- first_out: float32 [2048, 2048], P('tp', 'ctx')
- first_up: float32 [2048, 8192], P('ctx', 'tp')
- first_down: float32 [8192, 2048], P('tp', 'ctx')
- first_gains: float32 [2, 2048], P(None, 'ctx')
- first_biases: float32 [2, 2048], P(None, 'ctx')
- second_qkv: float32 [3, 2048, 2048], P(None, 'ctx', 'tp')
- second_out: float32 [2048, 2048], P('tp', 'ctx')
- second_up: float32 [2048, 8192], P('ctx', 'tp')
- second_down: float32 [8192, 2048], P('tp', 'ctx')
- second_gains: float32 [2, 2048], P(None, 'ctx')
- second_biases: float32 [2, 2048], P(None, 'ctx')
The draws below stay inside these ranges and needn't reach their ends.
Inputs may be any that keep to these rules, and one draw needn't show every extreme that they name: `seq_lengths`: the lengths sum to 4096.
All inputs are finite; a program needn't handle non-finite values.
Results may differ from the reference program's by a relative error of at most 0.012.
Values may be sent and summed in bfloat16 or wider, within the bound.
No kernel may reach another device: no remote copies, remote signals or barrier semaphores. Data moves between devices by JAX's collectives and lax.ppermute only.
A program may use at most 256 MiB of HBM per device.

```python
import math
import jax
import jax.numpy as jnp
import numpy as np
from jax import lax

D = 2048
FF = 8192
HEADS = 16
SEQ_MAX = 2048
BLOCK = 256
TOKENS = 4096
SEQS = 4


def set_ends(result, own_key, least, largest):
    longest = result.shape.index(max(result.shape))
    spots = []
    for shift in (0, 1):
        where = [jax.random.randint(jax.random.fold_in(own_key, axis), (), 0, length) for axis, length in enumerate(result.shape)]
        where[longest] = (where[longest] + shift) % result.shape[longest]
        spots.append(tuple(where))
    return result.at[spots[0]].set(least).at[spots[1]].set(largest)


def shard_levels(own_key, shape, shards, smallest, high):
    level, own = 1.0, jax.random.fold_in(own_key, 6)
    for position, blocks in shards:
        draws = jnp.exp(jax.random.uniform(jax.random.fold_in(own, position), (blocks,), jnp.float32, smallest / len(shards), high / len(shards)))
        level = level * jnp.repeat(draws, shape[position] // blocks).reshape([-1 if axis == position else 1 for axis in range(len(shape))])
    return level


def profile(number_of, total, limit, skew):
    portions = [(1 << 20) // math.isqrt(standing ** skew) + 1 for standing in range(2, number_of + 1)]
    rest, holding = total - limit - (number_of - 1), [1] * (number_of - 1)
    while rest > 0:
        free = [i for i in range(number_of - 1) if holding[i] < limit]
        mass, left = sum([portions[i] for i in free]), rest
        for i in free:
            addition = min(limit - holding[i], max(1, left * portions[i] // mass), rest)
            holding[i] = holding[i] + addition
            rest = rest - addition
    return np.array([limit] + holding)


def ragged_sizes(stream_key, count, total, limit, skew):
    if count == 2:
        one = jax.random.randint(stream_key, (), max(1, total - limit), min(limit, total - 1) + 1)
        return jnp.stack([one, total - one])
    sizes = jnp.asarray(profile(count, total, limit, skew), jnp.int32)
    pairs = (count - 1) // 2
    giver, sink = sizes[1:1 + 2 * pairs:2], sizes[2:2 + 2 * pairs:2]
    margin = jnp.minimum(giver - 1, limit - sink)
    passed = jax.random.randint(jax.random.fold_in(stream_key, 1), (pairs,), 0, 1 << 20) % (margin + 1)
    sizes = sizes.at[1:1 + 2 * pairs:2].set(giver - passed).at[2:2 + 2 * pairs:2].set(sink + passed)
    return sizes[jax.random.permutation(jax.random.fold_in(stream_key, 2), count)]


def noise(rng, extent, spread, most, split=(), kind=jnp.bfloat16):
    level = shard_levels(rng, extent, split, -0.22, 0.18) if split else 1.0
    array = jax.random.normal(rng, extent, jnp.float32) * spread * level
    return jnp.minimum(jnp.maximum(array, -most), most).astype(kind)


def setup_inputs(seed: int = 0) -> dict:
    arg_keys = jax.random.split(jax.random.key(seed), 23)
    tokens = noise(arg_keys[0], (TOKENS, D), 1.0, 6.0, ((0, 8),))
    cotangent = noise(arg_keys[1], (TOKENS, D), 1.0, 6.0, ((0, 8),))
    w_qkv = noise(arg_keys[2], (3, D, D), D ** -0.5, 0.125, ((1, 8), (2, 4)), jnp.float32)
    w_out = noise(arg_keys[3], (D, D), (D // 32) ** -0.5, 0.75, ((0, 4), (1, 8)), jnp.float32)
    w_up = noise(arg_keys[4], (D, FF), D ** -0.5, 0.125, ((0, 8), (1, 4)), jnp.float32)
    w_down = noise(arg_keys[5], (FF, D), FF ** -0.5, 0.0625, ((0, 4), (1, 8)), jnp.float32)
    norm_gains = jnp.clip(1.0 + 0.15 * jax.random.normal(arg_keys[6], (2, D), jnp.float32), 0.25, 1.75)
    norm_biases = noise(arg_keys[7], (2, D), 0.5, 3.0, ((1, 8),), jnp.float32)
    m_qkv = noise(arg_keys[8], (3, D, D), (0.3 / (4 * D * D + 2 * D * FF + 4 * D) ** 0.5), 0.00024414062, ((1, 8), (2, 4)), jnp.float32)
    m_out = noise(arg_keys[9], (D, D), (0.3 / (4 * D * D + 2 * D * FF + 4 * D) ** 0.5), 0.00024414062, ((0, 4), (1, 8)), jnp.float32)
    m_up = noise(arg_keys[10], (D, FF), (0.3 / (4 * D * D + 2 * D * FF + 4 * D) ** 0.5), 0.00024414062, ((0, 8), (1, 4)), jnp.float32)
    m_down = noise(arg_keys[11], (FF, D), (0.3 / (4 * D * D + 2 * D * FF + 4 * D) ** 0.5), 0.00024414062, ((0, 4), (1, 8)), jnp.float32)
    m_gains = noise(arg_keys[12], (2, D), (0.3 / (4 * D * D + 2 * D * FF + 4 * D) ** 0.5), 0.00024414062, ((1, 8),), jnp.float32)
    m_biases = noise(arg_keys[13], (2, D), (0.3 / (4 * D * D + 2 * D * FF + 4 * D) ** 0.5), 0.00024414062, ((1, 8),), jnp.float32)
    v_qkv = jnp.clip(jnp.exp(math.log(3.972996509560289e-08) - 4.6051702 * jax.random.uniform(arg_keys[14], (3, D, D), jnp.float32) ** shard_levels(arg_keys[14], (3, D, D), ((1, 8), (2, 4)), -0.2, 0.2)), 3.9729963763335263e-10, 3.972996509560289e-08)
    v_out = jnp.clip(jnp.exp(math.log(3.972996509560289e-08) - 4.6051702 * jax.random.uniform(arg_keys[15], (D, D), jnp.float32) ** shard_levels(arg_keys[15], (D, D), ((0, 4), (1, 8)), -0.2, 0.2)), 3.9729963763335263e-10, 3.972996509560289e-08)
    v_up = jnp.clip(jnp.exp(math.log(3.972996509560289e-08) - 4.6051702 * jax.random.uniform(arg_keys[16], (D, FF), jnp.float32) ** shard_levels(arg_keys[16], (D, FF), ((0, 8), (1, 4)), -0.2, 0.2)), 3.9729963763335263e-10, 3.972996509560289e-08)
    v_down = jnp.clip(jnp.exp(math.log(3.972996509560289e-08) - 4.6051702 * jax.random.uniform(arg_keys[17], (FF, D), jnp.float32) ** shard_levels(arg_keys[17], (FF, D), ((0, 4), (1, 8)), -0.2, 0.2)), 3.9729963763335263e-10, 3.972996509560289e-08)
    v_gains = jnp.clip(jnp.exp(math.log(3.972996509560289e-08) - 4.6051702 * jax.random.uniform(arg_keys[18], (2, D), jnp.float32) ** shard_levels(arg_keys[18], (2, D), ((1, 8),), -0.2, 0.2)), 3.9729963763335263e-10, 3.972996509560289e-08)
    v_biases = jnp.clip(jnp.exp(math.log(3.972996509560289e-08) - 4.6051702 * jax.random.uniform(arg_keys[19], (2, D), jnp.float32) ** shard_levels(arg_keys[19], (2, D), ((1, 8),), -0.2, 0.2)), 3.9729963763335263e-10, 3.972996509560289e-08)
    seq_lengths = ragged_sizes(arg_keys[20], SEQS, TOKENS, SEQ_MAX, 2).astype(jnp.int32)
    decay_mask = set_ends((jax.random.randint(arg_keys[21], (6,), 0, 2) < 1).astype(jnp.int32), jax.random.fold_in(arg_keys[21], 1), 0, 1)
    return {"tokens": tokens, "cotangent": cotangent, "w_qkv": w_qkv, "w_out": w_out, "w_up": w_up, "w_down": w_down, "norm_gains": norm_gains, "norm_biases": norm_biases, "m_qkv": m_qkv, "m_out": m_out, "m_up": m_up, "m_down": m_down, "m_gains": m_gains, "m_biases": m_biases, "v_qkv": v_qkv, "v_out": v_out, "v_up": v_up, "v_down": v_down, "v_gains": v_gains, "v_biases": v_biases, "seq_lengths": seq_lengths, "decay_mask": decay_mask}


eps_norm = 1e-05
neg_big = -1e+30
beta_one = 0.9
beta_two = 0.95
adam_eps = 1e-08
learn_rate = 0.001
decay_rate = 0.1
step_count = 10.0

@jax.custom_vjp
def low(v):
    return lax.optimization_barrier(v.astype(jnp.bfloat16)).astype(jnp.float32)

@jax.custom_vjp
def low_back(v):
    return v

def low_keep(v):
    return (low(v), None)

def low_pass(kept, grad):
    return (grad,)

def back_keep(v):
    return (v, None)

def back_low(kept, grad):
    return (low(grad),)
low.defvjp(low_keep, low_pass)
low_back.defvjp(back_keep, back_low)

def token_labels(global_rows, seq_lengths, total_rows):
    lengths = seq_lengths.astype(jnp.int32)
    starts = (jnp.cumsum(lengths) - lengths).astype(jnp.int32)
    after = (global_rows[:, None] >= starts[None, :]).astype(jnp.int32)
    segment = (lax.optimization_barrier(jnp.sum(after, axis=1)) - 1).astype(jnp.int32)
    chosen = segment[:, None] == jnp.arange(lengths.shape[0], dtype=jnp.int32)[None, :]
    begin = lax.optimization_barrier(jnp.sum(jnp.where(chosen, starts[None, :], 0), axis=1)).astype(jnp.int32)
    block = ((global_rows - begin) // BLOCK).astype(jnp.int32)
    valid = (global_rows >= 0) & (global_rows < total_rows)
    return (segment, block, valid)

def layer_norm(rows, gain, bias):
    mean = lax.optimization_barrier(jnp.mean(rows, axis=1, keepdims=True))
    centred = rows - mean
    rstd = lax.rsqrt(lax.optimization_barrier(jnp.mean(centred * centred, axis=1, keepdims=True)) + eps_norm)
    return centred * rstd * gain + bias

def reference(tokens, cotangent, w_qkv, w_out, w_up, w_down, norm_gains, norm_biases, m_qkv, m_out, m_up, m_down, m_gains, m_biases, v_qkv, v_out, v_up, v_down, v_gains, v_biases, seq_lengths, decay_mask):
    highest = lax.Precision.HIGHEST
    total_rows = tokens.shape[0]
    head_size = D // HEADS
    scale = head_size ** (-0.5)
    block_rows = min(512, total_rows)
    blocks = total_rows // block_rows
    before = SEQ_MAX
    behind = block_rows + BLOCK
    window = before + block_rows + behind
    all_rows = jnp.arange(total_rows, dtype=jnp.int32)
    q_seg, q_blk, _ = token_labels(all_rows, seq_lengths, total_rows)
    pad_rows = jnp.arange(total_rows + before + behind, dtype=jnp.int32) - before
    k_seg, k_blk, k_valid = token_labels(pad_rows, seq_lengths, total_rows)

    def forward(wq, wo, wu, wd, gains, biases, x):
        cq, co, cu, cd = (low(wq), low(wo), low(wu), low(wd))
        cg, cb = (low(gains), low(biases))
        h1 = layer_norm(x, cg[0], cb[0])
        a1 = low(h1)
        qkv = jnp.einsum('td,cdh->cth', a1, cq, precision=highest)
        qkv = low(low_back(qkv))
        query = qkv[0].reshape(total_rows, HEADS, head_size)
        pad_spec = ((before, behind), (0, 0), (0, 0))
        keys = jnp.pad(qkv[1].reshape(total_rows, HEADS, head_size), pad_spec)
        values = jnp.pad(qkv[2].reshape(total_rows, HEADS, head_size), pad_spec)

        def one_block(start):
            qs = lax.dynamic_slice_in_dim(query, start, block_rows, 0)
            ks = lax.dynamic_slice_in_dim(keys, start, window, 0)
            vs = lax.dynamic_slice_in_dim(values, start, window, 0)
            qseg = lax.dynamic_slice_in_dim(q_seg, start, block_rows, 0)
            qblk = lax.dynamic_slice_in_dim(q_blk, start, block_rows, 0)
            kseg = lax.dynamic_slice_in_dim(k_seg, start, window, 0)
            kblk = lax.dynamic_slice_in_dim(k_blk, start, window, 0)
            kval = lax.dynamic_slice_in_dim(k_valid, start, window, 0)
            allowed = kval[None, :] & (kseg[None, :] == qseg[:, None]) & (kblk[None, :] <= qblk[:, None])
            raw = jnp.einsum('qhd,khd->hqk', qs, ks, precision=highest)
            scores = low_back(raw * scale)
            masked = jnp.where(allowed[None], scores, neg_big)
            top = lax.optimization_barrier(jnp.max(masked, axis=2, keepdims=True))
            lse = top + jnp.log(lax.optimization_barrier(jnp.sum(jnp.exp(masked - top), axis=2, keepdims=True)))
            prob = low(jnp.exp(masked - lse))
            return jnp.einsum('hqk,khd->qhd', prob, vs, precision=highest)
        block_starts = jnp.arange(blocks, dtype=jnp.int32) * block_rows
        vals = lax.map(jax.checkpoint(one_block), block_starts).reshape(total_rows, D)
        vals = low(low_back(vals))
        attn = low_back(jnp.dot(vals, co, precision=highest))
        y1 = x + attn
        a2 = low(layer_norm(y1, cg[1], cb[1]))
        up = low_back(jnp.dot(a2, cu, precision=highest))
        act = low(jax.nn.gelu(up, approximate=False))
        return y1 + jnp.dot(act, cd, precision=highest)
    masters = (w_qkv, w_out, w_up, w_down, norm_gains, norm_biases)
    firsts = (m_qkv, m_out, m_up, m_down, m_gains, m_biases)
    seconds = (v_qkv, v_out, v_up, v_down, v_gains, v_biases)
    x32 = tokens.astype(jnp.float32)
    out, pull = jax.vjp(forward, w_qkv, w_out, w_up, w_down, norm_gains, norm_biases, x32)
    grads = pull(cotangent.astype(jnp.float32))
    block_out = out.astype(jnp.bfloat16)
    grad_tokens = grads[6].astype(jnp.bfloat16)
    weight_grads = grads[:6]
    total_sq = jnp.float32(0.0)
    for grad in weight_grads:
        total_sq = total_sq + jnp.sum(grad * grad)
    grad_norm = jnp.sqrt(total_sq)
    factor = 1.0 / jnp.maximum(grad_norm, 1.0)
    fix_one = 1.0 - beta_one ** step_count
    fix_two = 1.0 - beta_two ** step_count
    steps, new_first, new_second = ([], [], [])
    for index in range(6):
        clipped = weight_grads[index] * factor
        first = beta_one * firsts[index] + (1.0 - beta_one) * clipped
        second = beta_two * seconds[index] + (1.0 - beta_two) * clipped * clipped
        decays = decay_mask[index].astype(jnp.float32)
        update = first / fix_one / (jnp.sqrt(second / fix_two) + adam_eps)
        amount = learn_rate * (update + decay_rate * decays * masters[index])
        steps.append(amount)
        new_first.append(first)
        new_second.append(second)
    return (block_out, grad_tokens, grad_norm, weight_grads[0], weight_grads[1], weight_grads[2], weight_grads[3], weight_grads[4], weight_grads[5], steps[0], steps[1], steps[2], steps[3], steps[4], steps[5], new_first[0], new_first[1], new_first[2], new_first[3], new_first[4], new_first[5], new_second[0], new_second[1], new_second[2], new_second[3], new_second[4], new_second[5])
```

```python
import functools
import math

import jax
import jax.numpy as jnp
from jax import lax
from jax.experimental import pallas as pl
from jax.experimental.pallas import tpu as pltpu
from jax.sharding import PartitionSpec as P

HEAD = 128
BLOCK = 256
Q_TILE = 256
K_TILE = 512

eps_norm = 1e-05
neg_big = -1e30
beta_one = 0.9
beta_two = 0.95
adam_eps = 1e-08
learn_rate = 0.001
decay_rate = 0.1
step_count = 10.0
inv_root_two = 1.0 / math.sqrt(2.0)
inv_root_two_pi = 1.0 / math.sqrt(2.0 * math.pi)
bf16 = jnp.bfloat16
f32 = jnp.float32


def ctx_xor(value, mask):
    count = lax.axis_size("ctx")
    return lax.ppermute(value, "ctx", [(place, place ^ mask) for place in range(count)])


def tp_shift(value, steps):
    count = lax.axis_size("tp")
    return lax.ppermute(value, "tp", [(place, (place + steps) % count) for place in range(count)])


def tp_gather(own):
    return [own] + [tp_shift(own, s) for s in range(1, lax.axis_size("tp"))]


def tp_scatter(partial):
    count = lax.axis_size("tp")
    rows = partial.shape[0] // count
    pieces = [partial[s * rows : (s + 1) * rows] for s in range(count)]
    got = [tp_shift(pieces[s], -s) for s in range(1, count)]
    total = pieces[0].astype(f32)
    for piece in got:
        total = total + piece.astype(f32)
    return total


def slots_to_rows(parts, tp_place):
    count = len(parts)
    rows = parts[0].shape[0]
    stacked = jnp.concatenate(parts, axis=0)
    order = [lax.rem(tp_place - j + count, count) * rows for j in range(count)]
    return jnp.concatenate([lax.dynamic_slice_in_dim(stacked, o, rows, 0) for o in order], axis=0)


def rows_to_slots(value, tp_place, count):
    rows = value.shape[0] // count
    order = [lax.rem(tp_place - s + count, count) * rows for s in range(count)]
    return jnp.concatenate([lax.dynamic_slice_in_dim(value, o, rows, 0) for o in order], axis=0)


def sum_over_all(value):
    ctx_bits = lax.axis_size("ctx").bit_length() - 1
    value = value + ctx_xor(value, 1)
    bit = 1
    while bit < ctx_bits:
        if bit + 1 < ctx_bits:
            low, high = 1 << bit, 1 << (bit + 1)
            one, two, three = (ctx_xor(value, low), ctx_xor(value, high), ctx_xor(value, low | high))
            value = (value + one) + (two + three)
            bit += 2
        else:
            value = value + ctx_xor(value, 1 << bit)
            bit += 1
    one, two, three = (tp_shift(value, 1), tp_shift(value, 2), tp_shift(value, 3))
    return (value + two) + (one + three)


def place_of(me, tp_place, mask, chunk, rows, chunks):
    part = rows // chunks
    inner = lax.rem(tp_place - chunk + chunks, chunks)
    return pl.multiple_of(jnp.bitwise_xor(me, mask) * rows + inner * part, part)


def scores_of(keys, query, lo, hi, base, scale):
    raw = lax.dot_general(keys, query, (((1,), (1,)), ((), ())), preferred_element_type=f32) * scale
    at = base + lax.broadcasted_iota(jnp.int32, raw.shape, 0)
    return jnp.where((at >= lo) & (at < hi), raw, neg_big)


def forward_kernel(rows, chunks, masks, scale, place, tiles, *refs):
    others = len(masks) - 1
    span, own = refs[0], refs[1]
    rest = refs[2 : 2 + others]
    out, out_t, lse_out, k_all, vt_all = refs[2 + others :]
    me, tp_place = place[0], place[1]
    part = rows // chunks
    for which, group in enumerate(masks):
        source = own if which == 0 else rest[which - 1]
        left = HEAD if which == 0 else 0
        for slot, mask in enumerate(group):
            for chunk in range(chunks):
                at = place_of(me, tp_place, mask, chunk, rows, chunks)
                top = slot * rows + chunk * part
                k_all[pl.ds(at, part), :] = source[top : top + part, left : left + HEAD]
                vt_all[:, pl.ds(at, part)] = source[top : top + part, left + HEAD : left + 2 * HEAD].T

    for tile in range(own.shape[0] // Q_TILE):
        cut = slice(tile * Q_TILE, (tile + 1) * Q_TILE)
        query = own[cut, :HEAD]
        lo, hi = span[0:1, cut], span[1:2, cut]

        def step(index, carry, query=query, lo=lo, hi=hi):
            top, total, acc = carry
            base = pl.multiple_of(index * K_TILE, K_TILE)
            scores = scores_of(k_all[pl.ds(base, K_TILE), :], query, lo, hi, base, scale)
            new_top = jnp.maximum(top, jnp.max(scores, axis=0, keepdims=True))
            fade = jnp.exp(top - new_top)
            prob = jnp.exp(scores - new_top)
            total = total * fade + jnp.sum(prob, axis=0, keepdims=True)
            acc = acc * fade + jnp.dot(
                vt_all[:, pl.ds(base, K_TILE)], prob.astype(bf16), preferred_element_type=f32
            )
            return (new_top, total, acc)

        start = (
            jnp.full((1, Q_TILE), neg_big, f32),
            jnp.zeros((1, Q_TILE), f32),
            jnp.zeros((HEAD, Q_TILE), f32),
        )
        top, total, acc = lax.fori_loop(tiles[0, tile], tiles[1, tile], step, start)
        result = acc / total
        out_t[:, cut] = result
        out[cut, :] = result.T.astype(bf16)
        lse_out[:, cut] = top + jnp.log(total)


def backward_kernel(rows, chunks, masks, scale, place, tiles, *refs):
    others = len(masks) - 1
    span, own, grad_out, out_t, lse_in = refs[:5]
    rest = refs[5 : 5 + others]
    dq_out, dkv_own = refs[5 + others : 7 + others]
    dkv_rest = refs[7 + others : 7 + 2 * others]
    k_all, kt_all, v_all, dk_all, dv_all = refs[7 + 2 * others :]
    me, tp_place = place[0], place[1]
    part = rows // chunks
    for which, group in enumerate(masks):
        source = own if which == 0 else rest[which - 1]
        left = HEAD if which == 0 else 0
        for slot, mask in enumerate(group):
            for chunk in range(chunks):
                at = place_of(me, tp_place, mask, chunk, rows, chunks)
                top = slot * rows + chunk * part
                keys = source[top : top + part, left : left + HEAD]
                k_all[pl.ds(at, part), :] = keys
                kt_all[:, pl.ds(at, part)] = keys.T
                v_all[pl.ds(at, part), :] = source[top : top + part, left + HEAD : left + 2 * HEAD]
    dk_all[...] = jnp.zeros_like(dk_all)
    dv_all[...] = jnp.zeros_like(dv_all)

    for tile in range(own.shape[0] // Q_TILE):
        cut = slice(tile * Q_TILE, (tile + 1) * Q_TILE)
        query, grad = own[cut, :HEAD], grad_out[cut, :]
        lo, hi, lse = span[0:1, cut], span[1:2, cut], lse_in[:, cut]
        inner = jnp.sum(grad.astype(f32).T * out_t[:, cut], axis=0, keepdims=True)

        def step(index, dq_t, query=query, grad=grad, lo=lo, hi=hi, lse=lse, inner=inner):
            base = pl.multiple_of(index * K_TILE, K_TILE)
            here = pl.ds(base, K_TILE)
            scores = scores_of(k_all[here, :], query, lo, hi, base, scale)
            prob = jnp.exp(scores - lse)
            grad_prob = lax.dot_general(
                v_all[here, :], grad, (((1,), (1,)), ((), ())), preferred_element_type=f32
            )
            grad_scores = (prob * (grad_prob - inner)).astype(bf16)
            dv_all[here, :] += jnp.dot(prob.astype(bf16), grad, preferred_element_type=f32)
            dk_all[here, :] += jnp.dot(grad_scores, query, preferred_element_type=f32)
            return dq_t + jnp.dot(kt_all[:, here], grad_scores, preferred_element_type=f32)

        dq_t = lax.fori_loop(
            tiles[0, tile], tiles[1, tile], step, jnp.zeros((HEAD, Q_TILE), f32)
        )
        dq_out[cut, :] = (dq_t * scale).T.astype(bf16)

    for which, group in enumerate(masks):
        target = dkv_own if which == 0 else dkv_rest[which - 1]
        for slot, mask in enumerate(group):
            for chunk in range(chunks):
                at = place_of(me, tp_place, mask, chunk, rows, chunks)
                top = slot * rows + chunk * part
                target[top : top + part, :HEAD] = (dk_all[pl.ds(at, part), :] * scale).astype(target.dtype)
                target[top : top + part, HEAD:] = dv_all[pl.ds(at, part), :].astype(target.dtype)


def in_vmem():
    return pl.BlockSpec(memory_space=pltpu.VMEM)


def in_smem():
    return pl.BlockSpec(memory_space=pltpu.SMEM)


def attention_forward(place, tiles, span, own, rest, rows, chunks, masks, total, scale):
    queries = own.shape[0]
    return pl.pallas_call(
        functools.partial(forward_kernel, rows, chunks, masks, scale),
        out_shape=(
            jax.ShapeDtypeStruct((queries, HEAD), bf16),
            jax.ShapeDtypeStruct((HEAD, queries), f32),
            jax.ShapeDtypeStruct((1, queries), f32),
        ),
        in_specs=[in_smem(), in_smem()] + [in_vmem()] * (2 + len(rest)),
        out_specs=(in_vmem(), in_vmem(), in_vmem()),
        scratch_shapes=[pltpu.VMEM((total, HEAD), bf16), pltpu.VMEM((HEAD, total), bf16)],
        compiler_params=pltpu.CompilerParams(vmem_limit_bytes=58 << 20),
        name="attention_forward",
    )(place, tiles, span, own, *rest)


def attention_backward(place, tiles, span, own, grad, out_t, lse, rest, rows, chunks, masks, total, scale):
    queries = own.shape[0]
    return pl.pallas_call(
        functools.partial(backward_kernel, rows, chunks, masks, scale),
        out_shape=(
            jax.ShapeDtypeStruct((queries, HEAD), bf16),
            jax.ShapeDtypeStruct((queries, 2 * HEAD), f32),
        )
        + tuple(jax.ShapeDtypeStruct(r.shape, bf16) for r in rest),
        in_specs=[in_smem(), in_smem()] + [in_vmem()] * (5 + len(rest)),
        out_specs=tuple(in_vmem() for _ in range(2 + len(rest))),
        scratch_shapes=[
            pltpu.VMEM((total, HEAD), bf16),
            pltpu.VMEM((HEAD, total), bf16),
            pltpu.VMEM((total, HEAD), bf16),
            pltpu.VMEM((total, HEAD), f32),
            pltpu.VMEM((total, HEAD), f32),
        ],
        compiler_params=pltpu.CompilerParams(vmem_limit_bytes=58 << 20),
        name="attention_backward",
    )(place, tiles, span, own, grad, out_t, lse, *rest)


def norm_parts(rows):
    mean = jnp.mean(rows, axis=1, keepdims=True)
    centred = rows - mean
    rstd = lax.rsqrt(jnp.mean(centred * centred, axis=1, keepdims=True) + eps_norm)
    return (centred * rstd, rstd)


def norm_back(grad_out, normed, rstd, gain):
    scaled = grad_out * gain
    inner = (
        scaled
        - jnp.mean(scaled, axis=1, keepdims=True)
        - normed * jnp.mean(scaled * normed, axis=1, keepdims=True)
    )
    return (inner * rstd, jnp.sum(grad_out * normed, axis=0), jnp.sum(grad_out, axis=0))


def adam_update(master, grad, first, second, factor, decays):
    clipped = grad * factor
    first_new = beta_one * first + (1.0 - beta_one) * clipped
    second_new = beta_two * second + (1.0 - beta_two) * clipped * clipped
    fix_one = 1.0 - beta_one**step_count
    fix_two = 1.0 - beta_two**step_count
    update = first_new / fix_one / (jnp.sqrt(second_new / fix_two) + adam_eps)
    amount = learn_rate * (update + decay_rate * decays * master)
    return (amount, first_new, second_new)


def key_span(positions, seq_lengths):
    ends = jnp.cumsum(seq_lengths)
    starts = ends - seq_lengths
    inside = (positions[:, None] >= starts[None, :]) & (positions[:, None] < ends[None, :])
    begin = jnp.sum(jnp.where(inside, starts[None, :], 0), axis=1)
    end = jnp.sum(jnp.where(inside, ends[None, :], 0), axis=1)
    block = (positions - begin) // BLOCK
    return (begin, jnp.minimum(begin + (block + 1) * BLOCK, end))


def per_device(
    tokens,
    cotangent,
    w_qkv,
    w_out,
    w_up,
    w_down,
    norm_gains,
    norm_biases,
    m_qkv,
    m_out,
    m_up,
    m_down,
    m_gains,
    m_biases,
    v_qkv,
    v_out,
    v_up,
    v_down,
    v_gains,
    v_biases,
    seq_lengths,
    decay_mask,
):
    rows, width = tokens.shape
    ctx_count, tp_count = lax.axis_size("ctx"), lax.axis_size("tp")
    ctx_place = lax.axis_index("ctx").astype(jnp.int32)
    tp_place = lax.axis_index("tp").astype(jnp.int32)
    total_rows = rows * ctx_count
    part_rows = rows // tp_count
    head_cols = w_out.shape[0]
    heads = head_cols // HEAD
    units = w_up.shape[1]
    ctx_cols = w_out.shape[1]
    scale = HEAD ** (-0.5)
    my_head = lax.rem(ctx_place // 2, heads)

    first_pack = jnp.concatenate((w_qkv[0], w_qkv[1], w_qkv[2], w_out.T), axis=1).astype(bf16)
    second_pack = jnp.concatenate((w_up, w_down.T), axis=1).astype(bf16)
    first_full = lax.all_gather(first_pack, "ctx", axis=0, tiled=True)
    second_pack, first_full = lax.optimization_barrier((second_pack, first_full))
    second_full = lax.all_gather(second_pack, "ctx", axis=0, tiled=True)
    qkv_full, out_full = first_full[:, : 3 * head_cols], first_full[:, 3 * head_cols :]
    up_full, down_full = second_full[:, :units], second_full[:, units:]

    small = jnp.concatenate((norm_gains, norm_biases), axis=0).astype(bf16)
    small = lax.all_gather(small, "ctx", axis=1, tiled=True).astype(f32)
    gain_one, gain_two, bias_one, bias_two = small[0], small[1], small[2], small[3]

    x_slots = rows_to_slots(tokens, tp_place, tp_count)
    c_slots = rows_to_slots(cotangent, tp_place, tp_count)
    normed, _ = norm_parts(x_slots.astype(f32))
    a1 = (normed * gain_one + bias_one).astype(bf16)

    group = [s << 1 for s in range(heads)]
    masks, rest_bits = ([group], [0] + list(range(heads.bit_length(), ctx_count.bit_length() - 1)))
    for bit in rest_bits:
        masks.append([m ^ (1 << bit) for g in masks for m in g])
    inner_rows = jnp.arange(part_rows, dtype=jnp.int32)
    positions = jnp.concatenate(
        [
            jnp.bitwise_xor(ctx_place, m) * rows + lax.rem(tp_place - s + tp_count, tp_count) * part_rows + inner_rows
            for m in group
            for s in range(tp_count)
        ]
    )
    lo, hi = key_span(positions, seq_lengths)
    span = jnp.stack((lo, hi))
    tiles = jnp.stack(
        (
            jnp.min(lo.reshape(-1, Q_TILE), axis=1) // K_TILE,
            (jnp.max(hi.reshape(-1, Q_TILE), axis=1) + K_TILE - 1) // K_TILE,
        )
    )
    place = jnp.stack((ctx_place, tp_place))

    qkv = jnp.dot(a1, qkv_full, preferred_element_type=f32).astype(bf16)
    own_parts = []
    for s in range(heads):
        at = jnp.bitwise_xor(my_head, s) * HEAD
        piece = jnp.concatenate(
            [lax.dynamic_slice_in_dim(qkv, j * head_cols + at, HEAD, 1) for j in range(3)], axis=1
        )
        own_parts.append(piece if s == 0 else ctx_xor(piece, s << 1))
    own = jnp.concatenate(own_parts, axis=0)
    rest, known = ([], own[:, HEAD:])
    for count, bit in enumerate(rest_bits):
        other = ctx_xor(known, 1 << bit)
        rest.append(other)
        if count + 1 < len(rest_bits):
            known = jnp.concatenate((known, other), axis=0)
    shape = (rows, tp_count, masks, total_rows, scale)
    mixed_low, mixed_t, lse = attention_forward(place, tiles, span, own, rest, *shape)

    back = [mixed_low[:rows]]
    for s in range(1, heads):
        back.append(ctx_xor(mixed_low[s * rows : (s + 1) * rows], s << 1))
    back = jnp.concatenate(back, axis=0)
    attn_vals = jnp.concatenate(
        [lax.dynamic_slice_in_dim(back, jnp.bitwise_xor(my_head, h) * rows, rows, 0) for h in range(heads)],
        axis=1,
    )
    attn = lax.dot_general(attn_vals, out_full, (((1,), (1,)), ((), ())), preferred_element_type=f32)
    x_own = x_slots[:part_rows].astype(f32)
    y1 = x_own + tp_scatter(attn.astype(bf16))
    normed2, rstd2 = norm_parts(y1)
    a2_own = (normed2 * gain_two + bias_two).astype(bf16)
    a2 = jnp.concatenate(tp_gather(a2_own), axis=0)

    grad_act = jnp.dot(c_slots, down_full, preferred_element_type=f32)
    up = jnp.dot(a2, up_full, preferred_element_type=f32)
    cdf = 0.5 * (1.0 + lax.erf(up * inv_root_two))
    act = (up * cdf).astype(bf16)
    slope = cdf + up * jnp.exp(-0.5 * up * up) * inv_root_two_pi
    grad_up_in = (grad_act * slope).astype(bf16)
    grad_h2 = lax.dot_general(grad_up_in, up_full, (((1,), (1,)), ((), ())), preferred_element_type=f32)
    grad_h2 = tp_scatter(grad_h2.astype(bf16))
    pair_left = jnp.stack((a2, c_slots))
    pair_right = jnp.stack((grad_up_in, act))
    pair_grad = jnp.einsum("btd,btf->bdf", pair_left, pair_right, preferred_element_type=f32).astype(bf16)
    pair_shard = lax.psum_scatter(pair_grad, "ctx", scatter_dimension=1, tiled=True)

    dx2, dg2, dc2 = norm_back(grad_h2, normed2, rstd2, gain_two)
    c_own = c_slots[:part_rows].astype(f32)
    grad_y1 = c_own + dx2
    grad_attn = jnp.concatenate(tp_gather(grad_y1.astype(bf16)), axis=0)
    mixed = lax.dot_general(act, down_full, (((1,), (1,)), ((), ())), preferred_element_type=f32).astype(bf16)
    mixed, grad_attn = lax.optimization_barrier((mixed, grad_attn))
    block_out = (y1 + tp_scatter(mixed)).astype(bf16)
    block_out = slots_to_rows(tp_gather(block_out), tp_place)

    grad_vals = jnp.dot(grad_attn, out_full, preferred_element_type=f32).astype(bf16)
    grad_outw = lax.dot_general(grad_attn, attn_vals, (((0,), (0,)), ((), ())), preferred_element_type=f32)
    out_shard = lax.psum_scatter(grad_outw.astype(bf16), "ctx", scatter_dimension=0, tiled=True)

    grads = []
    for s in range(heads):
        piece = lax.dynamic_slice_in_dim(grad_vals, jnp.bitwise_xor(my_head, s) * HEAD, HEAD, 1)
        grads.append(piece if s == 0 else ctx_xor(piece, s << 1))
    grads = jnp.concatenate(grads, axis=0)
    results = attention_backward(place, tiles, span, own, grads, mixed_t, lse, rest, *shape)
    grad_q, grad_kv, grad_rest = results[0], results[1], list(results[2:])
    for bit in reversed(rest_bits):
        got = ctx_xor(grad_rest.pop(), 1 << bit)
        cut = grad_kv.shape[0]
        grad_kv = grad_kv + got[:cut].astype(f32)
        grad_rest = split_add(grad_rest, got[cut:])
    grad_own = jnp.concatenate((grad_q, grad_kv.astype(bf16)), axis=1)
    back = [grad_own[:rows]]
    for s in range(1, heads):
        back.append(ctx_xor(grad_own[s * rows : (s + 1) * rows], s << 1))
    back = jnp.concatenate(back, axis=0)
    by_head = [
        lax.dynamic_slice_in_dim(back, jnp.bitwise_xor(my_head, h) * rows, rows, 0) for h in range(heads)
    ]
    grad_qkv_in = jnp.concatenate(
        [by_head[h][:, j * HEAD : (j + 1) * HEAD] for j in range(3) for h in range(heads)], axis=1
    )
    grad_qkvw = lax.dot_general(a1, grad_qkv_in, (((0,), (0,)), ((), ())), preferred_element_type=f32)
    qkv_shard = lax.psum_scatter(grad_qkvw.astype(bf16), "ctx", scatter_dimension=0, tiled=True)
    grad_h1 = lax.dot_general(grad_qkv_in, qkv_full, (((1,), (1,)), ((), ())), preferred_element_type=f32)
    grad_h1 = tp_scatter(grad_h1.astype(bf16))
    normed1, rstd1 = norm_parts(x_own)
    dx1, dg1, dc1 = norm_back(grad_h1, normed1, rstd1, gain_one)
    grad_tokens = (grad_y1 + dx1).astype(bf16)
    grad_tokens = slots_to_rows(tp_gather(grad_tokens), tp_place)

    qkv_grad = qkv_shard.astype(f32)
    out_grad = out_shard.astype(f32)
    up_grad = pair_shard[0].astype(f32)
    down_grad = pair_shard[1].astype(f32)
    square = jnp.sum(qkv_grad * qkv_grad) + jnp.sum(out_grad * out_grad)
    square = square + jnp.sum(up_grad * up_grad) + jnp.sum(down_grad * down_grad)
    lines = jnp.stack((dg1, dg2, dc1, dc2)).reshape(-1, HEAD)
    sent = jnp.concatenate((lines, jnp.full((8, HEAD), square, f32)), axis=0)
    total = sum_over_all(sent)
    small_grad = total[:-8].reshape(4, width)
    total_sq = total[-1, 0] + jnp.sum(small_grad * small_grad)
    grad_norm = jnp.sqrt(total_sq)
    factor = 1.0 / jnp.maximum(grad_norm, 1.0)
    small_own = lax.dynamic_slice_in_dim(small_grad, ctx_place * ctx_cols, ctx_cols, 1)

    shards = (
        jnp.stack([qkv_grad[:, j * head_cols : (j + 1) * head_cols] for j in range(3)]),
        out_grad.T,
        up_grad,
        down_grad.T,
        small_own[:2],
        small_own[2:],
    )
    masters = (w_qkv, w_out, w_up, w_down, norm_gains, norm_biases)
    firsts = (m_qkv, m_out, m_up, m_down, m_gains, m_biases)
    seconds = (v_qkv, v_out, v_up, v_down, v_gains, v_biases)
    amounts, new_first, new_second = ([], [], [])
    for index in range(6):
        decays = decay_mask[index].astype(f32)
        amount, first_new, second_new = adam_update(
            masters[index], shards[index], firsts[index], seconds[index], factor, decays
        )
        amounts.append(amount)
        new_first.append(first_new)
        new_second.append(second_new)
    return (block_out, grad_tokens, grad_norm, *shards, *amounts, *new_first, *new_second)


def split_add(arrays, extra):
    at, result = (0, [])
    for array in arrays:
        count = array.shape[0]
        result.append((array.astype(f32) + extra[at : at + count].astype(f32)).astype(array.dtype))
        at += count
    return result


def solution(mesh):
    small = P(None, "ctx")
    weights = (P(None, "ctx", "tp"), P("tp", "ctx"), P("ctx", "tp"), P("tp", "ctx"), small, small)
    rows = (P("ctx", None), P("ctx", None))
    return jax.shard_map(
        per_device,
        mesh=mesh,
        in_specs=(*rows, *weights, *weights, *weights, P(), P()),
        out_specs=(*rows, P(), *weights, *weights, *weights, *weights),
        check_vma=False,
    )
```

```python
import functools
import math

import jax
import jax.numpy as jnp
from jax import lax
from jax.experimental import pallas as pl
from jax.experimental.pallas import tpu as pltpu
from jax.sharding import PartitionSpec as P

HEAD = 128
BLOCK = 256
Q_TILE = 256
K_TILE = 512

eps_norm = 1e-05
neg_big = -1e30
beta_one = 0.9
beta_two = 0.95
adam_eps = 1e-08
learn_rate = 0.001
decay_rate = 0.1
step_count = 10.0
inv_root_two = 1.0 / math.sqrt(2.0)
inv_root_two_pi = 1.0 / math.sqrt(2.0 * math.pi)
bf16 = jnp.bfloat16
f32 = jnp.float32


def ctx_xor(value, mask):
    count = lax.axis_size("ctx")
    return lax.ppermute(value, "ctx", [(place, place ^ mask) for place in range(count)])


def ctx_gather(own, early):
    blocks = [None] * lax.axis_size("ctx")
    for mask in range(0, len(blocks), 2):
        blocks[mask] = own if mask == 0 else ctx_xor(own, mask)
    blocks[2], early = lax.optimization_barrier((blocks[2], early))
    for mask in range(0, len(blocks), 2):
        blocks[mask + 1] = ctx_xor(blocks[mask], 1)
    return (blocks, early)


def tp_xor(value, mask):
    count = lax.axis_size("tp")
    return lax.ppermute(value, "tp", [(place, place ^ mask) for place in range(count)])


def tp_gather(own):
    far_first = [tp_xor(own, s) for s in reversed(range(1, lax.axis_size("tp")))]
    return [own] + far_first[::-1]


def tp_send(partial):
    count = lax.axis_size("tp")
    rows = partial.shape[0] // count
    pieces = [partial[s * rows : (s + 1) * rows] for s in range(count)]
    far_first = [tp_xor(pieces[s], s) for s in reversed(range(1, count))]
    return [pieces[0]] + far_first[::-1]


def tp_total(parts):
    total = parts[0].astype(f32)
    for piece in parts[1:]:
        total = total + piece.astype(f32)
    return total


def tp_scatter(partial):
    return tp_total(tp_send(partial))


def slots_to_rows(parts, tp_place):
    return in_slots(jnp.concatenate(parts, axis=0), tp_place, len(parts))


def in_slots(value, tp_place, count):
    rows = value.shape[0] // count
    order = [jnp.bitwise_xor(tp_place, s) * rows for s in range(count)]
    return jnp.concatenate([lax.dynamic_slice_in_dim(value, o, rows, 0) for o in order], axis=0)


def sum_over_all(value):
    ctx_bits = lax.axis_size("ctx").bit_length() - 1
    one, two, three = (tp_xor(value, 1), tp_xor(value, 2), tp_xor(value, 3))
    value = (value + one) + (two + three)
    bit = 1
    while bit < ctx_bits:
        if bit + 1 < ctx_bits:
            low, high = 1 << bit, 1 << (bit + 1)
            one, two, three = (ctx_xor(value, low), ctx_xor(value, high), ctx_xor(value, low | high))
            value = (value + one) + (two + three)
            bit += 2
        else:
            value = value + ctx_xor(value, 1 << bit)
            bit += 1
    return value + ctx_xor(value, 1)


def place_of(me, tp_place, mask, chunk, rows, chunks):
    part = rows // chunks
    return pl.multiple_of(jnp.bitwise_xor(me, mask) * rows + jnp.bitwise_xor(tp_place, chunk) * part, part)


def scores_of(keys, query, lo, hi, base, scale):
    raw = lax.dot_general(keys, query, (((1,), (1,)), ((), ())), preferred_element_type=f32) * scale
    at = base + lax.broadcasted_iota(jnp.int32, raw.shape, 0)
    return jnp.where((at >= lo) & (at < hi), raw, neg_big)


def forward_kernel(rows, chunks, masks, scale, place, tiles, *refs):
    others = len(masks) - 1
    span, own = refs[0], refs[1]
    rest = refs[2 : 2 + others]
    out, out_t, lse_out, k_all, vt_all = refs[2 + others :]
    me, tp_place = place[0], place[1]
    part = rows // chunks
    for which, group in enumerate(masks):
        source = own if which == 0 else rest[which - 1]
        left = HEAD if which == 0 else 0
        for slot, mask in enumerate(group):
            for chunk in range(chunks):
                at = place_of(me, tp_place, mask, chunk, rows, chunks)
                top = slot * rows + chunk * part
                k_all[pl.ds(at, part), :] = source[top : top + part, left : left + HEAD]
                vt_all[:, pl.ds(at, part)] = source[top : top + part, left + HEAD : left + 2 * HEAD].T

    @pl.loop(0, own.shape[0] // Q_TILE)
    def _(tile):
        cut = pl.ds(pl.multiple_of(tile * Q_TILE, Q_TILE), Q_TILE)
        query = own[cut, :HEAD]
        lo, hi = span[0:1, cut], span[1:2, cut]

        def step(index, carry):
            top, total, acc = carry
            base = pl.multiple_of(index * K_TILE, K_TILE)
            scores = scores_of(k_all[pl.ds(base, K_TILE), :], query, lo, hi, base, scale)
            new_top = jnp.maximum(top, jnp.max(scores, axis=0, keepdims=True))
            fade = jnp.exp(top - new_top)
            prob = jnp.exp(scores - new_top)
            total = total * fade + jnp.sum(prob, axis=0, keepdims=True)
            acc = acc * fade + jnp.dot(
                vt_all[:, pl.ds(base, K_TILE)], prob.astype(bf16), preferred_element_type=f32
            )
            return (new_top, total, acc)

        start = (
            jnp.full((1, Q_TILE), neg_big, f32),
            jnp.zeros((1, Q_TILE), f32),
            jnp.zeros((HEAD, Q_TILE), f32),
        )
        top, total, acc = lax.fori_loop(tiles[0, tile], tiles[1, tile], step, start)
        result = acc / total
        out_t[:, cut] = result
        out[cut, :] = result.T.astype(bf16)
        lse_out[:, cut] = top + jnp.log(total)


def backward_kernel(rows, chunks, masks, scale, place, tiles, *refs):
    others = len(masks) - 1
    span, own, grad_out, out_t, lse_in = refs[:5]
    rest = refs[5 : 5 + others]
    dq_out, dkv_own = refs[5 + others : 7 + others]
    dkv_rest = refs[7 + others : 7 + 2 * others]
    k_all, kt_all, v_all, dk_all, dv_all = refs[7 + 2 * others :]
    me, tp_place = place[0], place[1]
    part = rows // chunks
    for which, group in enumerate(masks):
        source = own if which == 0 else rest[which - 1]
        left = HEAD if which == 0 else 0
        for slot, mask in enumerate(group):
            for chunk in range(chunks):
                at = place_of(me, tp_place, mask, chunk, rows, chunks)
                top = slot * rows + chunk * part
                keys = source[top : top + part, left : left + HEAD]
                k_all[pl.ds(at, part), :] = keys
                kt_all[:, pl.ds(at, part)] = keys.T
                v_all[pl.ds(at, part), :] = source[top : top + part, left + HEAD : left + 2 * HEAD]
    dk_all[...] = jnp.zeros_like(dk_all)
    dv_all[...] = jnp.zeros_like(dv_all)

    @pl.loop(0, own.shape[0] // Q_TILE)
    def _(tile):
        cut = pl.ds(pl.multiple_of(tile * Q_TILE, Q_TILE), Q_TILE)
        query, grad = own[cut, :HEAD], grad_out[cut, :]
        lo, hi, lse = span[0:1, cut], span[1:2, cut], lse_in[:, cut]
        inner = jnp.sum(grad.astype(f32).T * out_t[:, cut], axis=0, keepdims=True)

        def step(index, dq_t):
            base = pl.multiple_of(index * K_TILE, K_TILE)
            here = pl.ds(base, K_TILE)
            scores = scores_of(k_all[here, :], query, lo, hi, base, scale)
            prob = jnp.exp(scores - lse)
            grad_prob = lax.dot_general(
                v_all[here, :], grad, (((1,), (1,)), ((), ())), preferred_element_type=f32
            )
            grad_scores = (prob * (grad_prob - inner)).astype(bf16)
            dv_all[here, :] += jnp.dot(prob.astype(bf16), grad, preferred_element_type=f32)
            dk_all[here, :] += jnp.dot(grad_scores, query, preferred_element_type=f32)
            return dq_t + jnp.dot(kt_all[:, here], grad_scores, preferred_element_type=f32)

        dq_t = lax.fori_loop(
            tiles[0, tile], tiles[1, tile], step, jnp.zeros((HEAD, Q_TILE), f32)
        )
        dq_out[cut, :] = (dq_t * scale).T.astype(bf16)

    for which, group in enumerate(masks):
        target = dkv_own if which == 0 else dkv_rest[which - 1]
        for slot, mask in enumerate(group):
            for chunk in range(chunks):
                at = place_of(me, tp_place, mask, chunk, rows, chunks)
                top = slot * rows + chunk * part
                target[top : top + part, :HEAD] = (dk_all[pl.ds(at, part), :] * scale).astype(target.dtype)
                target[top : top + part, HEAD:] = dv_all[pl.ds(at, part), :].astype(target.dtype)


LARGE = pl.CostEstimate(flops=200_000_000_000, bytes_accessed=600_000_000, transcendentals=0)
LITTLE = pl.CostEstimate(flops=1, bytes_accessed=1, transcendentals=0)


def in_vmem():
    return pl.BlockSpec(memory_space=pltpu.VMEM)


def in_smem():
    return pl.BlockSpec(memory_space=pltpu.SMEM)


def attention_forward(place, tiles, span, own, rest, rows, chunks, masks, total, scale):
    queries = own.shape[0]
    return pl.pallas_call(
        functools.partial(forward_kernel, rows, chunks, masks, scale),
        out_shape=(
            jax.ShapeDtypeStruct((queries, HEAD), bf16),
            jax.ShapeDtypeStruct((HEAD, queries), f32),
            jax.ShapeDtypeStruct((1, queries), f32),
        ),
        in_specs=[in_smem(), in_smem()] + [in_vmem()] * (2 + len(rest)),
        out_specs=(in_vmem(), in_vmem(), in_vmem()),
        scratch_shapes=[pltpu.VMEM((total, HEAD), bf16), pltpu.VMEM((HEAD, total), bf16)],
        compiler_params=pltpu.CompilerParams(vmem_limit_bytes=58 << 20),
        cost_estimate=LITTLE,
        name="attention_forward",
    )(place, tiles, span, own, *rest)


def attention_backward(place, tiles, span, own, grad, out_t, lse, rest, rows, chunks, masks, total, scale):
    queries = own.shape[0]
    return pl.pallas_call(
        functools.partial(backward_kernel, rows, chunks, masks, scale),
        out_shape=(
            jax.ShapeDtypeStruct((queries, HEAD), bf16),
            jax.ShapeDtypeStruct((queries, 2 * HEAD), f32),
        )
        + tuple(jax.ShapeDtypeStruct(r.shape, bf16) for r in rest),
        in_specs=[in_smem(), in_smem()] + [in_vmem()] * (5 + len(rest)),
        out_specs=tuple(in_vmem() for _ in range(2 + len(rest))),
        scratch_shapes=[
            pltpu.VMEM((total, HEAD), bf16),
            pltpu.VMEM((HEAD, total), bf16),
            pltpu.VMEM((total, HEAD), bf16),
            pltpu.VMEM((total, HEAD), f32),
            pltpu.VMEM((total, HEAD), f32),
        ],
        compiler_params=pltpu.CompilerParams(vmem_limit_bytes=58 << 20),
        cost_estimate=LITTLE,
        name="attention_backward",
    )(place, tiles, span, own, grad, out_t, lse, *rest)


def merge_kernel(grad_q, grad_kv, *refs):
    got, outs = refs[0], refs[1:]
    rows = outs[0].shape[0]
    for slot, out in enumerate(outs):
        cut = slice(slot * rows, (slot + 1) * rows)
        out[:, :HEAD] = grad_q[cut, :]
        out[:, HEAD:] = (grad_kv[cut, :] + got[cut, :].astype(f32)).astype(bf16)


def merge(grad_q, grad_kv, got, count):
    rows = grad_q.shape[0] // count
    return pl.pallas_call(
        merge_kernel,
        out_shape=(jax.ShapeDtypeStruct((rows, 3 * HEAD), bf16),) * count,
        in_specs=[in_vmem()] * 3,
        out_specs=(in_vmem(),) * count,
        compiler_params=pltpu.CompilerParams(vmem_limit_bytes=58 << 20),
        cost_estimate=LARGE,
        name="merge",
    )(grad_q, grad_kv, got)


def lanes_of(me, mask, depth):
    at = jnp.bitwise_xor(me, mask) * depth
    return pl.ds(pl.multiple_of(at, depth), depth)


def project_kernel(rows, heads, depth, place, rows_in, *refs):
    blocks, (out, a1, small, weights, result) = refs[:-5], refs[-5:]
    me = place[0]
    my_head = lax.rem(me // 2, heads)
    if depth % HEAD:
        small[...] = blocks[-1][...]
        blocks = blocks[:-1]
    for mask, block in enumerate(blocks):
        at = lanes_of(me, mask, depth)
        weights[at, :] = block[:depth, :]
        if depth % HEAD == 0:
            small[:, at] = block[depth : depth + 8, :depth].astype(f32)
    part = rows // 4
    for quarter in range(4):
        cut = slice(quarter * part, (quarter + 1) * part)
        normed, _ = norm_parts(rows_in[cut, :].astype(f32))
        a1[cut, :] = (normed * small[0:1, :] + small[2:3, :]).astype(bf16)
    width = heads * HEAD
    for j in range(3):
        result[:, j * width : (j + 1) * width] = jnp.dot(
            a1[...], weights[:, j * width : (j + 1) * width], preferred_element_type=f32
        ).astype(bf16)
    for s in range(heads):
        at = jnp.bitwise_xor(my_head, s) * HEAD
        for j in range(3):
            here = pl.ds(pl.multiple_of(j * width + at, HEAD), HEAD)
            out[s * rows : (s + 1) * rows, j * HEAD : (j + 1) * HEAD] = result[:, here]


def project(place, rows_in, blocks, heads, depth):
    rows, width = rows_in.shape
    cols = 3 * heads * HEAD
    if depth % HEAD:
        known = jnp.stack([block[depth : depth + 8, :depth] for block in blocks])
        order = jnp.bitwise_xor(place[0], jnp.arange(len(blocks), dtype=jnp.int32))
        known = jnp.take(known, order, axis=0).transpose(1, 0, 2).reshape(8, width)
        blocks = [*blocks, known.astype(f32)]
    return pl.pallas_call(
        functools.partial(project_kernel, rows, heads, depth),
        out_shape=(
            jax.ShapeDtypeStruct((heads * rows, 3 * HEAD), bf16),
            jax.ShapeDtypeStruct((rows, width), bf16),
            jax.ShapeDtypeStruct((8, width), f32),
        ),
        in_specs=[in_smem()] + [in_vmem()] * (1 + len(blocks)),
        out_specs=(in_vmem(),) * 3,
        scratch_shapes=[pltpu.VMEM((width, cols), bf16), pltpu.VMEM((rows, cols), bf16)],
        compiler_params=pltpu.CompilerParams(vmem_limit_bytes=58 << 20),
        cost_estimate=LITTLE,
        name="project",
    )(place, rows_in, *blocks)


def weight_grad_kernel(masks, added, place, rows_in, grads, *refs):
    me, add, out = place[0], refs[0], refs[int(added)]
    depth = out.shape[0] // len(masks)
    whole = refs[-1] if depth % HEAD else None
    if whole is not None:
        whole[...] = lax.dot_general(rows_in[...], grads[...], (((0,), (0,)), ((), ())), preferred_element_type=f32)
    for slot, mask in enumerate(masks):
        at = lanes_of(me, mask, depth)
        here = slice(slot * depth, (slot + 1) * depth)
        if whole is not None:
            block = whole[at, :]
        else:
            block = lax.dot_general(
                rows_in[:, at], grads[...], (((0,), (0,)), ((), ())), preferred_element_type=f32
            )
        if added:
            block = block + add[here, :].astype(f32)
        out[here, :] = block.astype(bf16)


def weight_grad(place, rows_in, grads, masks, add, depth):
    extra = [] if add is None else [add]
    return pl.pallas_call(
        functools.partial(weight_grad_kernel, masks, add is not None),
        out_shape=jax.ShapeDtypeStruct((len(masks) * depth, grads.shape[1]), bf16),
        in_specs=[in_smem()] + [in_vmem()] * (2 + len(extra)),
        out_specs=in_vmem(),
        scratch_shapes=[pltpu.VMEM((rows_in.shape[1], grads.shape[1]), f32)] if depth % HEAD else [],
        compiler_params=pltpu.CompilerParams(vmem_limit_bytes=58 << 20),
        cost_estimate=LITTLE,
        name="weight_grad",
    )(place, rows_in, grads, *extra)


def input_grad_kernel(depth, place, grads, *refs):
    me = place[0]
    if depth % HEAD:
        blocks, out, weights = refs[:-2], refs[-2], refs[-1]
        for mask, block in enumerate(blocks):
            weights[lanes_of(me, mask, depth), :] = block[:depth, :]
        out[...] = lax.dot_general(
            grads[...], weights[...], (((1,), (1,)), ((), ())), preferred_element_type=f32
        ).astype(bf16)
        return
    blocks, out = refs[:-1], refs[-1]
    for mask, block in enumerate(blocks):
        out[:, lanes_of(me, mask, depth)] = lax.dot_general(
            grads[...], block[:depth, :], (((1,), (1,)), ((), ())), preferred_element_type=f32
        ).astype(bf16)


def input_grad(place, grads, blocks, depth):
    return pl.pallas_call(
        functools.partial(input_grad_kernel, depth),
        out_shape=jax.ShapeDtypeStruct((grads.shape[0], depth * len(blocks)), bf16),
        in_specs=[in_smem()] + [in_vmem()] * (1 + len(blocks)),
        out_specs=in_vmem(),
        scratch_shapes=[pltpu.VMEM((depth * len(blocks), grads.shape[1]), bf16)] if depth % HEAD else [],
        compiler_params=pltpu.CompilerParams(vmem_limit_bytes=58 << 20),
        cost_estimate=LITTLE,
        name="input_grad",
    )(place, grads, *blocks)


def pair_grad_kernel(half, left, right, other_left, other_right, out):
    def block(rows_in, grads):
        out[0] = lax.dot_general(
            rows_in[...], grads[...], (((0,), (0,)), ((), ())), preferred_element_type=f32
        ).astype(bf16)

    pl.when(pl.program_id(0) < half)(lambda: block(left, right))
    pl.when(pl.program_id(0) >= half)(lambda: block(other_left, other_right))


def pair_grad_of(left, right, other_left, other_right):
    rows, width = left.shape
    cols = right.shape[1]
    step, half = 256, width // 256
    first = pl.BlockSpec((rows, step), lambda i: (0, jnp.minimum(i, half - 1)))
    second = pl.BlockSpec((rows, step), lambda i: (0, jnp.maximum(i - half, 0)))
    return pl.pallas_call(
        functools.partial(pair_grad_kernel, half),
        grid=(2 * half,),
        out_shape=jax.ShapeDtypeStruct((2, width, cols), bf16),
        in_specs=[first, in_vmem(), second, in_vmem()],
        out_specs=pl.BlockSpec((1, step, cols), lambda i: (i // half, i % half, 0)),
        compiler_params=pltpu.CompilerParams(vmem_limit_bytes=58 << 20),
        cost_estimate=LITTLE,
        name="pair_grad",
    )(left, right, other_left, other_right)


def widen_kernel(pair, out_t, up, down, out, square):
    part = jnp.zeros((1, 1), f32)
    for source, target, turn in ((pair.at[0], up, False), (pair.at[1], down, True), (out_t, out, True)):
        value = source[...].astype(f32)
        part = part + jnp.sum(jnp.sum(value * value, axis=0, keepdims=True), axis=1, keepdims=True)
        target[...] = value.T if turn else value
    square[...] = jnp.broadcast_to(part, square.shape)


def widen(pair, out_t):
    _, cols, units = pair.shape
    shapes = ((cols, units), (units, cols), out_t.shape[::-1], (8, HEAD))
    return pl.pallas_call(
        widen_kernel,
        out_shape=tuple(jax.ShapeDtypeStruct(s, f32) for s in shapes),
        in_specs=[in_vmem(), in_vmem()],
        out_specs=(in_vmem(),) * 4,
        compiler_params=pltpu.CompilerParams(vmem_limit_bytes=58 << 20),
        cost_estimate=LITTLE,
        name="widen",
    )(pair, out_t)


ADAM_STEPS = 8


def adam_kernel(count, factor, decays, *refs):
    ins, outs = refs[: 4 * count], refs[4 * count :]
    for index in range(count):
        master, grad, first, second = (r[...] for r in ins[4 * index : 4 * index + 4])
        results = adam_update(master, grad, first, second, factor[0], decays[index])
        for target, value in zip(outs[3 * index : 3 * index + 3], results):
            target[...] = value


def adam(factor, decays, groups):
    specs, shapes, flat = ([], [], [])
    for group in groups:
        lines, cols = group[0].shape
        spec = pl.BlockSpec((lines // ADAM_STEPS, cols), lambda step: (step, 0))
        flat.extend(group)
        specs.extend([spec] * 3)
        shapes.extend([jax.ShapeDtypeStruct((lines, cols), f32)] * 3)
    in_specs = [s for spec in specs[::3] for s in [spec] * 4]
    results = pl.pallas_call(
        functools.partial(adam_kernel, len(groups)),
        grid=(ADAM_STEPS,),
        out_shape=tuple(shapes),
        in_specs=[in_smem(), in_smem()] + in_specs,
        out_specs=tuple(specs),
        compiler_params=pltpu.CompilerParams(vmem_limit_bytes=58 << 20),
        cost_estimate=LITTLE,
        name="adam",
    )(factor.reshape(1), decays, *flat)
    return [results[3 * i : 3 * i + 3] for i in range(len(groups))]


def norm_parts(rows):
    mean = jnp.mean(rows, axis=1, keepdims=True)
    centred = rows - mean
    rstd = lax.rsqrt(jnp.mean(centred * centred, axis=1, keepdims=True) + eps_norm)
    return (centred * rstd, rstd)


def norm_back(grad_out, normed, rstd, gain):
    scaled = grad_out * gain
    inner = (
        scaled
        - jnp.mean(scaled, axis=1, keepdims=True)
        - normed * jnp.mean(scaled * normed, axis=1, keepdims=True)
    )
    return (inner * rstd, jnp.sum(grad_out * normed, axis=0), jnp.sum(grad_out, axis=0))


def adam_update(master, grad, first, second, factor, decays):
    clipped = grad * factor
    first_new = beta_one * first + (1.0 - beta_one) * clipped
    second_new = beta_two * second + (1.0 - beta_two) * clipped * clipped
    fix_one = 1.0 - beta_one**step_count
    fix_two = 1.0 - beta_two**step_count
    update = first_new / fix_one / (jnp.sqrt(second_new / fix_two) + adam_eps)
    amount = learn_rate * (update + decay_rate * decays * master)
    return (amount, first_new, second_new)


def key_span(positions, seq_lengths):
    ends = jnp.cumsum(seq_lengths)
    starts = ends - seq_lengths
    inside = (positions[:, None] >= starts[None, :]) & (positions[:, None] < ends[None, :])
    begin = jnp.sum(jnp.where(inside, starts[None, :], 0), axis=1)
    end = jnp.sum(jnp.where(inside, ends[None, :], 0), axis=1)
    block = (positions - begin) // BLOCK
    return (begin, jnp.minimum(begin + (block + 1) * BLOCK, end))


def per_device(
    tokens,
    cotangent,
    w_qkv,
    w_out,
    w_up,
    w_down,
    norm_gains,
    norm_biases,
    m_qkv,
    m_out,
    m_up,
    m_down,
    m_gains,
    m_biases,
    v_qkv,
    v_out,
    v_up,
    v_down,
    v_gains,
    v_biases,
    seq_lengths,
    decay_mask,
):
    rows, width = tokens.shape
    ctx_count, tp_count = lax.axis_size("ctx"), lax.axis_size("tp")
    ctx_place = lax.axis_index("ctx").astype(jnp.int32)
    tp_place = lax.axis_index("tp").astype(jnp.int32)
    total_rows = rows * ctx_count
    part_rows = rows // tp_count
    head_cols = w_out.shape[0]
    heads = head_cols // HEAD
    units = w_up.shape[1]
    ctx_cols = w_out.shape[1]
    scale = HEAD ** (-0.5)
    my_head = lax.rem(ctx_place // 2, heads)

    place = jnp.stack((ctx_place, tp_place))

    small = jnp.concatenate((norm_gains, norm_biases), axis=0)
    small = jnp.pad(small, ((0, 12), (0, 3 * head_cols - ctx_cols)))
    qkv_pack = jnp.concatenate((w_qkv[0], w_qkv[1], w_qkv[2]), axis=1)
    qkv_pack = jnp.concatenate((qkv_pack, small), axis=0).astype(bf16)
    out_pack = w_out.T.astype(bf16)
    rest_pack = jnp.concatenate((w_up, w_down.T), axis=1).astype(bf16)

    x_slots = in_slots(tokens, tp_place, tp_count)
    c_slots = in_slots(cotangent, tp_place, tp_count)
    qkv_blocks, early = ctx_gather(qkv_pack, (out_pack, rest_pack, x_slots))
    out_pack, rest_pack, x_slots = early
    out_pack, rest_pack, qkv_blocks = lax.optimization_barrier((out_pack, rest_pack, qkv_blocks))
    out_full = lax.all_gather(out_pack, "ctx", axis=0, tiled=True)

    group = [s << 1 for s in range(heads)]
    masks, rest_bits = ([group], [0] + list(range(heads.bit_length(), ctx_count.bit_length() - 1)))
    for bit in rest_bits:
        masks.append([m ^ (1 << bit) for g in masks for m in g])
    inner_rows = jnp.arange(part_rows, dtype=jnp.int32)
    positions = jnp.concatenate(
        [
            jnp.bitwise_xor(ctx_place, m) * rows + jnp.bitwise_xor(tp_place, s) * part_rows + inner_rows
            for m in group
            for s in range(tp_count)
        ]
    )
    lo, hi = key_span(positions, seq_lengths)
    span = jnp.stack((lo, hi))
    tiles = jnp.stack(
        (
            jnp.min(lo.reshape(-1, Q_TILE), axis=1) // K_TILE,
            (jnp.max(hi.reshape(-1, Q_TILE), axis=1) + K_TILE - 1) // K_TILE,
        )
    )
    pieces, a1, small = project(place, x_slots, qkv_blocks, heads, ctx_cols)
    gain_one, gain_two, bias_two = small[0], small[1], small[3]
    own_parts = [pieces[:rows]]
    for s in range(1, heads):
        own_parts.append(ctx_xor(pieces[s * rows : (s + 1) * rows], s << 1))
    own_parts, rest_pack = lax.optimization_barrier((own_parts, rest_pack))
    rest_full = lax.all_gather(rest_pack, "ctx", axis=0, tiled=True)
    up_full, down_full = rest_full[:, :units], rest_full[:, units:]
    own = jnp.concatenate(own_parts, axis=0)
    rest, known = ([], own[:, HEAD:])
    for count, bit in enumerate(rest_bits):
        other = ctx_xor(known, 1 << bit)
        rest.append(other)
        if count + 1 < len(rest_bits):
            known = jnp.concatenate((known, other), axis=0)
    shape = (rows, tp_count, masks, total_rows, scale)
    mixed_low, mixed_t, lse = attention_forward(place, tiles, span, own, rest, *shape)

    back = [mixed_low[:rows]]
    for s in range(1, heads):
        back.append(ctx_xor(mixed_low[s * rows : (s + 1) * rows], s << 1))
    back = jnp.concatenate(back, axis=0)
    attn_vals = jnp.concatenate(
        [lax.dynamic_slice_in_dim(back, jnp.bitwise_xor(my_head, h) * rows, rows, 0) for h in range(heads)],
        axis=1,
    )
    attn = lax.dot_general(attn_vals, out_full, (((1,), (1,)), ((), ())), preferred_element_type=f32)
    x_own = x_slots[:part_rows].astype(f32)
    y1 = x_own + tp_scatter(attn.astype(bf16))
    normed2, rstd2 = norm_parts(y1)
    a2_own = (normed2 * gain_two + bias_two).astype(bf16)
    grad_act = jnp.dot(c_slots, down_full, preferred_element_type=f32)
    a2, grad_act = lax.optimization_barrier((tp_gather(a2_own), grad_act))
    a2 = jnp.concatenate(a2, axis=0)

    up = jnp.dot(a2, up_full, preferred_element_type=f32)
    cdf = 0.5 * (1.0 + lax.erf(up * inv_root_two))
    act = (up * cdf).astype(bf16)
    slope = cdf + up * jnp.exp(-0.5 * up * up) * inv_root_two_pi
    grad_up_in = (grad_act * slope).astype(bf16)
    grad_h2 = lax.dot_general(grad_up_in, up_full, (((1,), (1,)), ((), ())), preferred_element_type=f32).astype(bf16)
    grad_h2 = tp_send(grad_h2)
    grad_h2[1], act, grad_up_in = lax.optimization_barrier((grad_h2[1], act, grad_up_in))
    grad_h2 = tp_total(grad_h2)
    pair_grad = pair_grad_of(a2, grad_up_in, c_slots, act)
    pair_shard = lax.psum_scatter(pair_grad, "ctx", scatter_dimension=1, tiled=True)
    grad_h2, pair_grad = lax.optimization_barrier((grad_h2, pair_grad))

    dx2, dg2, dc2 = norm_back(grad_h2, normed2, rstd2, gain_two)
    c_own = c_slots[:part_rows].astype(f32)
    grad_y1 = c_own + dx2
    grad_attn = jnp.concatenate(tp_gather(grad_y1.astype(bf16)), axis=0)
    mixed = lax.dot_general(act, down_full, (((1,), (1,)), ((), ())), preferred_element_type=f32).astype(bf16)
    mixed, grad_attn = lax.optimization_barrier((mixed, grad_attn))
    block_out = (y1 + tp_scatter(mixed)).astype(bf16)

    grad_vals = jnp.dot(grad_attn, out_full, preferred_element_type=f32).astype(bf16)
    grad_outw = lax.dot_general(grad_attn, attn_vals, (((0,), (0,)), ((), ())), preferred_element_type=f32)
    grad_outw = grad_outw.astype(bf16)

    grads = []
    for s in range(heads):
        piece = lax.dynamic_slice_in_dim(grad_vals, jnp.bitwise_xor(my_head, s) * HEAD, HEAD, 1)
        grads.append(piece if s == 0 else ctx_xor(piece, s << 1))
    grads = jnp.concatenate(grads, axis=0)
    results = attention_backward(place, tiles, span, own, grads, mixed_t, lse, rest, *shape)
    results, block_out = lax.optimization_barrier((results, block_out))
    grad_q, grad_kv, grad_rest = results[0], results[1], list(results[2:])
    for bit in reversed(rest_bits):
        got = ctx_xor(grad_rest.pop(), 1 << bit)
        cut = grad_kv.shape[0]
        if grad_rest:
            grad_kv = grad_kv + got[:cut].astype(f32)
            grad_rest = split_add(grad_rest, got[cut:])
    grad_q, grad_outw = lax.optimization_barrier((grad_q, grad_outw))
    grad_own = merge(grad_q, grad_kv, got, heads)
    back = [grad_own[0]]
    for s in range(1, heads):
        back.append(ctx_xor(grad_own[s], s << 1))
    back = jnp.concatenate(back, axis=0)
    back, late, pair_shard = lax.optimization_barrier((back, grad_outw, pair_shard))
    out_shard = lax.psum_scatter(late, "ctx", scatter_dimension=0, tiled=True)
    by_head = [
        lax.dynamic_slice_in_dim(back, jnp.bitwise_xor(my_head, h) * rows, rows, 0) for h in range(heads)
    ]
    grad_qkv_in = jnp.concatenate(
        [by_head[h][:, j * HEAD : (j + 1) * HEAD] for j in range(3) for h in range(heads)], axis=1
    )
    grad_h1 = input_grad(place, grad_qkv_in, qkv_blocks, ctx_cols)
    grad_h1, grad_qkv_in = lax.optimization_barrier((grad_h1, grad_qkv_in))
    chips = list(range(0, ctx_count, 2))
    sent = weight_grad(place, a1, grad_qkv_in, [m ^ 1 for m in chips], None, ctx_cols)
    block_out, sent = lax.optimization_barrier((tp_gather(block_out), sent))
    got = ctx_xor(sent, 1)
    summed = weight_grad(place, a1, grad_qkv_in, chips, got, ctx_cols)
    grad_h1, summed = lax.optimization_barrier((grad_h1, summed))
    qkv_grad = summed[:ctx_cols].astype(f32)
    for slot, mask in enumerate(chips[1:], 1):
        qkv_grad = qkv_grad + ctx_xor(summed[slot * ctx_cols : (slot + 1) * ctx_cols], mask).astype(f32)
    grad_h1, qkv_grad = lax.optimization_barrier((tp_scatter(grad_h1), qkv_grad))
    block_out = slots_to_rows(block_out, tp_place)
    normed1, rstd1 = norm_parts(x_own)
    dx1, dg1, dc1 = norm_back(grad_h1, normed1, rstd1, gain_one)
    grad_tokens = (grad_y1 + dx1).astype(bf16)
    dx1, pair_shard, out_shard = lax.optimization_barrier((dx1, pair_shard, out_shard))
    up_grad, down_grad, out_grad, square = widen(pair_shard, out_shard)
    square = square[0, 0] + jnp.sum(qkv_grad * qkv_grad)
    lines = jnp.stack((dg1, dg2, dc1, dc2)).reshape(-1, HEAD)
    sent = jnp.concatenate((lines, jnp.full((8, HEAD), square, f32)), axis=0)
    total = sum_over_all(sent)
    grad_tokens = slots_to_rows(tp_gather(grad_tokens), tp_place)
    small_grad = total[:-8].reshape(4, width)
    total_sq = total[-1, 0] + jnp.sum(small_grad * small_grad)
    grad_norm = jnp.sqrt(total_sq)
    factor = 1.0 / jnp.maximum(grad_norm, 1.0)
    small_own = lax.dynamic_slice_in_dim(small_grad, ctx_place * ctx_cols, ctx_cols, 1)

    qkv_grad = jnp.stack([qkv_grad[:, j * head_cols : (j + 1) * head_cols] for j in range(3)])
    flags = decay_mask.astype(f32)
    flat = lambda value: value.reshape(-1, head_cols)
    matrices = adam(
        factor,
        flags,
        (
            (flat(w_qkv), flat(qkv_grad), flat(m_qkv), flat(v_qkv)),
            (w_out, out_grad, m_out, v_out),
            (w_up, up_grad, m_up, v_up),
            (w_down, down_grad, m_down, v_down),
        ),
    )
    matrices[0] = [value.reshape(w_qkv.shape) for value in matrices[0]]
    gains_new = adam_update(norm_gains, small_own[:2], m_gains, v_gains, factor, flags[4])
    biases_new = adam_update(norm_biases, small_own[2:], m_biases, v_biases, factor, flags[5])
    shards = (qkv_grad, out_grad, up_grad, down_grad, small_own[:2], small_own[2:])
    updates = list(zip(*matrices, gains_new, biases_new))
    return (block_out, grad_tokens, grad_norm, *shards, *updates[0], *updates[1], *updates[2])


def split_add(arrays, extra):
    at, result = (0, [])
    for array in arrays:
        count = array.shape[0]
        result.append((array.astype(f32) + extra[at : at + count].astype(f32)).astype(array.dtype))
        at += count
    return result


def solution(mesh):
    small = P(None, "ctx")
    weights = (P(None, "ctx", "tp"), P("tp", "ctx"), P("ctx", "tp"), P("tp", "ctx"), small, small)
    rows = (P("ctx", None), P("ctx", None))
    return jax.shard_map(
        per_device,
        mesh=mesh,
        in_specs=(*rows, *weights, *weights, *weights, P(), P()),
        out_specs=(*rows, P(), *weights, *weights, *weights, *weights),
        check_vma=False,
    )
```

```python
import functools
import math

import jax
import jax.numpy as jnp
from jax import lax
from jax.experimental import pallas as pl
from jax.experimental.pallas import tpu as pltpu
from jax.sharding import PartitionSpec as P

HEAD = 128
BLOCK = 256
Q_TILE = 512

eps_norm = 1e-05
neg_big = -1e30
beta_one = 0.9
beta_two = 0.95
adam_eps = 1e-08
learn_rate = 0.001
decay_rate = 0.1
step_count = 10.0
log2_e = math.log2(math.e)
inv_root_two = 1.0 / math.sqrt(2.0)
inv_root_two_pi = 1.0 / math.sqrt(2.0 * math.pi)
bf16 = jnp.bfloat16
f32 = jnp.float32


def ctx_xor(value, mask):
    count = lax.axis_size("ctx")
    return lax.ppermute(value, "ctx", [(place, place ^ mask) for place in range(count)])


def ctx_gather(own, early):
    blocks = [None] * lax.axis_size("ctx")
    for mask in range(0, len(blocks), 2):
        blocks[mask] = own if mask == 0 else ctx_xor(own, mask)
    blocks[2], early = lax.optimization_barrier((blocks[2], early))
    for mask in range(0, len(blocks), 2):
        blocks[mask + 1] = ctx_xor(blocks[mask], 1)
    return (blocks, early)


def tp_xor(value, mask):
    count = lax.axis_size("tp")
    return lax.ppermute(value, "tp", [(place, place ^ mask) for place in range(count)])


def tp_gather(own):
    return tp_gather_last(tp_gather_first(own))


def tp_gather_first(own):
    count = lax.axis_size("tp")
    return [own] + [tp_xor(own, s) for s in range(1, 3 if count == 4 else count)]


def tp_gather_last(parts):
    return parts + [tp_xor(parts[2], 1)] if lax.axis_size("tp") == 4 else parts


def tp_send(partial, behind=None):
    count = lax.axis_size("tp")
    rows = partial.shape[0] // count
    pieces = [partial[s * rows : (s + 1) * rows] for s in range(count)]
    if count != 4:
        return [pieces[0]] + [tp_xor(pieces[s], s) for s in range(1, count)]
    passed = tp_xor(pieces[3], 1)
    passed, near, _ = lax.optimization_barrier((passed, pieces[1], behind))
    joined = (pieces[2].astype(f32) + passed.astype(f32)).astype(bf16)
    return [pieces[0], tp_xor(near, 1), tp_xor(joined, 2)]


def tp_total(parts):
    total = parts[0].astype(f32)
    for piece in parts[1:]:
        total = total + piece.astype(f32)
    return total


def tp_scatter(partial):
    return tp_total(tp_send(partial))


def slots_to_rows(parts, tp_place):
    return in_slots(jnp.concatenate(parts, axis=0), tp_place, len(parts))


def in_slots(value, tp_place, count):
    rows = value.shape[0] // count
    order = [jnp.bitwise_xor(tp_place, s) * rows for s in range(count)]
    return jnp.concatenate([lax.dynamic_slice_in_dim(value, o, rows, 0) for o in order], axis=0)


def sum_over_all(value, later):
    if lax.axis_size("tp") == 4:
        one, two, three = (tp_xor(value, 1), tp_xor(value, 2), tp_xor(value, 3))
        value = (value + one) + (two + three)
    else:
        mask = 1
        while mask < lax.axis_size("tp"):
            value = value + tp_xor(value, mask)
            mask *= 2
    value, later = lax.optimization_barrier((value, later))
    mask = lax.axis_size("ctx") // 2
    while mask:
        value = value + ctx_xor(value, mask)
        mask //= 2
    return (value, later)


def scores_of(keys, query, where, lo, hi, scale):
    raw = lax.dot_general(keys, query, (((1,), (1,)), ((), ())), preferred_element_type=f32) * (scale * log2_e)
    return jnp.where((where >= lo) & (where < hi), raw, neg_big)


def key_halves(rows, place, chip):
    top = pl.multiple_of(jnp.bitwise_xor(chip, place[0] // 2) * rows, rows)
    core = lax.rem(place[0], 2)
    return (top, (2 * chip + core) * rows, (2 * chip + 1 - core) * rows)


def fill_positions(rows, chunks, place, where):
    where[...] = jnp.bitwise_xor(lax.broadcasted_iota(jnp.int32, where.shape, 0), place[1] * (rows // chunks))


def forward_kernel(rows, chunks, left, scale, place, tiles, span, own, *refs):
    even = own if left else refs[0]
    odd, out, out_t, lse_out, vt_even, vt_odd, where = refs[-7:]
    fill_positions(rows, chunks, place, where)
    for slot in range(odd.shape[0] // rows):
        cut = slice(slot * rows, (slot + 1) * rows)
        vt_even[:, cut] = even[cut, left + HEAD : left + 2 * HEAD].T
        vt_odd[:, cut] = odd[cut, HEAD:].T

    @pl.loop(0, own.shape[0] // Q_TILE)
    def _(tile):
        cut = pl.ds(pl.multiple_of(tile * Q_TILE, Q_TILE), Q_TILE)
        query = own[cut, :HEAD]
        lo, hi = span[0:1, cut], span[1:2, cut]

        def step(chip, carry):
            top, total, acc = carry
            at, first, second = key_halves(rows, place, chip)
            here = pl.ds(at, rows)
            one = scores_of(even[here, left : left + HEAD], query, where[...], lo - first, hi - first, scale)
            two = scores_of(odd[here, :HEAD], query, where[...], lo - second, hi - second, scale)
            new_top = jnp.maximum(
                top, jnp.maximum(jnp.max(one, axis=0, keepdims=True), jnp.max(two, axis=0, keepdims=True))
            )
            fade = jnp.exp2(top - new_top)
            one, two = jnp.exp2(one - new_top), jnp.exp2(two - new_top)
            total = total * fade + jnp.sum(one, axis=0, keepdims=True) + jnp.sum(two, axis=0, keepdims=True)
            acc = (
                acc * fade
                + jnp.dot(vt_even[:, here], one.astype(bf16), preferred_element_type=f32)
                + jnp.dot(vt_odd[:, here], two.astype(bf16), preferred_element_type=f32)
            )
            return (new_top, total, acc)

        start = (
            jnp.full((1, Q_TILE), neg_big, f32),
            jnp.zeros((1, Q_TILE), f32),
            jnp.zeros((HEAD, Q_TILE), f32),
        )
        top, total, acc = lax.fori_loop(tiles[0, tile], tiles[1, tile], step, start)
        result = acc / total
        out_t[:, cut] = result
        out[cut, :] = result.T.astype(bf16)
        lse_out[:, cut] = top + jnp.log2(total)


def backward_kernel(rows, chunks, left, scale, place, tiles, span, own, grad_out, out_t, lse_in, *refs):
    even = own if left else refs[0]
    odd, dq_out, dkv_even, dkv_odd, kt_even, kt_odd, d_odd, where = refs[-8:]
    fill_positions(rows, chunks, place, where)
    for slot in range(odd.shape[0] // rows):
        cut = slice(slot * rows, (slot + 1) * rows)
        kt_even[:, cut] = even[cut, left : left + HEAD].T
        kt_odd[:, cut] = odd[cut, :HEAD].T
    dkv_even[...] = jnp.zeros_like(dkv_even)
    d_odd[...] = jnp.zeros_like(d_odd)

    @pl.loop(0, own.shape[0] // Q_TILE)
    def _(tile):
        cut = pl.ds(pl.multiple_of(tile * Q_TILE, Q_TILE), Q_TILE)
        query, grad = own[cut, :HEAD], grad_out[cut, :]
        lo, hi, lse = span[0:1, cut], span[1:2, cut], lse_in[:, cut]
        inner = jnp.sum(grad.astype(f32).T * out_t[:, cut], axis=0, keepdims=True)

        def half(keys, values, keys_t, total, here, first, dq_t):
            scores = scores_of(keys, query, where[...], lo - first, hi - first, scale)
            prob = jnp.exp2(scores - lse)
            grad_prob = lax.dot_general(
                values, grad, (((1,), (1,)), ((), ())), preferred_element_type=f32
            )
            grad_scores = (prob * (grad_prob - inner)).astype(bf16)
            total[here, HEAD:] += jnp.dot(prob.astype(bf16), grad, preferred_element_type=f32)
            total[here, :HEAD] += jnp.dot(grad_scores, query, preferred_element_type=f32)
            return dq_t + jnp.dot(keys_t, grad_scores, preferred_element_type=f32)

        def step(chip, dq_t):
            at, first, second = key_halves(rows, place, chip)
            here = pl.ds(at, rows)
            keys, values = even[here, left : left + HEAD], even[here, left + HEAD : left + 2 * HEAD]
            dq_t = half(keys, values, kt_even[:, here], dkv_even, here, first, dq_t)
            return half(odd[here, :HEAD], odd[here, HEAD:], kt_odd[:, here], d_odd, here, second, dq_t)

        dq_t = lax.fori_loop(
            tiles[0, tile], tiles[1, tile], step, jnp.zeros((HEAD, Q_TILE), f32)
        )
        dq_out[cut, :] = (dq_t * scale).T.astype(bf16)

    dkv_even[:, :HEAD] = dkv_even[:, :HEAD] * scale
    dkv_odd[:, :HEAD] = (d_odd[:, :HEAD] * scale).astype(bf16)
    dkv_odd[:, HEAD:] = d_odd[:, HEAD:].astype(bf16)


LARGE = pl.CostEstimate(flops=145_000_000_000, bytes_accessed=145_000_000, transcendentals=0)
LITTLE = pl.CostEstimate(flops=1, bytes_accessed=1, transcendentals=0)


def in_vmem():
    return pl.BlockSpec(memory_space=pltpu.VMEM)


def in_smem():
    return pl.BlockSpec(memory_space=pltpu.SMEM)


def attention_forward(place, tiles, span, own, even, odd, rows, chunks, scale):
    queries, keys = own.shape[0], odd.shape[0]
    arrays = (own, odd) if even is None else (own, even, odd)
    return pl.pallas_call(
        functools.partial(forward_kernel, rows, chunks, HEAD if even is None else 0, scale),
        out_shape=(
            jax.ShapeDtypeStruct((queries, HEAD), bf16),
            jax.ShapeDtypeStruct((HEAD, queries), f32),
            jax.ShapeDtypeStruct((1, queries), f32),
        ),
        in_specs=[in_smem(), in_smem()] + [in_vmem()] * (1 + len(arrays)),
        out_specs=(in_vmem(), in_vmem(), in_vmem()),
        scratch_shapes=[
            pltpu.VMEM((HEAD, keys), bf16),
            pltpu.VMEM((HEAD, keys), bf16),
            pltpu.VMEM((rows, Q_TILE), jnp.int32),
        ],
        compiler_params=pltpu.CompilerParams(vmem_limit_bytes=58 << 20),
        cost_estimate=LITTLE,
        name="attention_forward",
    )(place, tiles, span, *arrays)


def attention_backward(place, tiles, span, own, grad, out_t, lse, even, odd, rows, chunks, scale):
    queries, keys = own.shape[0], odd.shape[0]
    arrays = (odd,) if even is None else (even, odd)
    return pl.pallas_call(
        functools.partial(backward_kernel, rows, chunks, HEAD if even is None else 0, scale),
        out_shape=(
            jax.ShapeDtypeStruct((queries, HEAD), bf16),
            jax.ShapeDtypeStruct((keys, 2 * HEAD), f32),
            jax.ShapeDtypeStruct((keys, 2 * HEAD), bf16),
        ),
        in_specs=[in_smem(), in_smem()] + [in_vmem()] * (5 + len(arrays)),
        out_specs=(in_vmem(),) * 3,
        scratch_shapes=[
            pltpu.VMEM((HEAD, keys), bf16),
            pltpu.VMEM((HEAD, keys), bf16),
            pltpu.VMEM((keys, 2 * HEAD), f32),
            pltpu.VMEM((rows, Q_TILE), jnp.int32),
        ],
        compiler_params=pltpu.CompilerParams(vmem_limit_bytes=58 << 20),
        cost_estimate=LITTLE,
        name="attention_backward",
    )(place, tiles, span, own, grad, out_t, lse, *arrays)


def merge_kernel(grad_q, grad_kv, *refs):
    got, outs = refs[0], refs[1:]
    rows = outs[0].shape[0]
    for slot, out in enumerate(outs):
        cut = slice(slot * rows, (slot + 1) * rows)
        out[:, :HEAD] = grad_q[cut, :]
        out[:, HEAD:] = (grad_kv[cut, :] + got[cut, :].astype(f32)).astype(bf16)


def merge(grad_q, grad_kv, got, count):
    rows = grad_q.shape[0] // count
    return pl.pallas_call(
        merge_kernel,
        out_shape=(jax.ShapeDtypeStruct((rows, 3 * HEAD), bf16),) * count,
        in_specs=[in_vmem()] * 3,
        out_specs=(in_vmem(),) * count,
        compiler_params=pltpu.CompilerParams(vmem_limit_bytes=58 << 20),
        cost_estimate=LARGE,
        name="merge",
    )(grad_q, grad_kv, got)


def lanes_of(me, mask, depth):
    at = jnp.bitwise_xor(me, mask) * depth
    return pl.ds(pl.multiple_of(at, depth), depth)


def project_kernel(rows, heads, depth, place, rows_in, *refs):
    blocks, outs, (a1, small, weights, result) = refs[: -4 - heads], refs[-4 - heads : -4], refs[-4:]
    me = place[0]
    my_head = lax.rem(me // 2, heads)
    if depth % HEAD:
        small[...] = blocks[-1][...]
        blocks = blocks[:-1]
    for mask, block in enumerate(blocks):
        at = lanes_of(me, mask, depth)
        weights[at, :] = block[:depth, :]
        if depth % HEAD == 0:
            small[:, at] = block[depth : depth + 8, :depth].astype(f32)
    part = rows // 4

    @pl.loop(0, 4)
    def _(quarter):
        cut = pl.ds(pl.multiple_of(quarter * part, part), part)
        normed, _ = norm_parts(rows_in[cut, :].astype(f32))
        a1[cut, :] = (normed * small[0:1, :] + small[2:3, :]).astype(bf16)

    width = heads * HEAD

    @pl.loop(0, 3)
    def _(j):
        cut = pl.ds(pl.multiple_of(j * width, width), width)
        result[:, cut] = jnp.dot(a1[...], weights[:, cut], preferred_element_type=f32).astype(bf16)

    for s in range(heads):
        at = jnp.bitwise_xor(my_head, s) * HEAD
        for j in range(3):
            here = pl.ds(pl.multiple_of(j * width + at, HEAD), HEAD)
            outs[s][:, j * HEAD : (j + 1) * HEAD] = result[:, here]


def project(place, rows_in, blocks, heads, depth):
    rows, width = rows_in.shape
    cols = 3 * heads * HEAD
    if depth % HEAD:
        known = jnp.stack([block[depth : depth + 8, :depth] for block in blocks])
        order = jnp.bitwise_xor(place[0], jnp.arange(len(blocks), dtype=jnp.int32))
        known = jnp.take(known, order, axis=0).transpose(1, 0, 2).reshape(8, width)
        blocks = [*blocks, known.astype(f32)]
    return pl.pallas_call(
        functools.partial(project_kernel, rows, heads, depth),
        out_shape=(
            *[jax.ShapeDtypeStruct((rows, 3 * HEAD), bf16)] * heads,
            jax.ShapeDtypeStruct((rows, width), bf16),
            jax.ShapeDtypeStruct((8, width), f32),
        ),
        in_specs=[in_smem()] + [in_vmem()] * (1 + len(blocks)),
        out_specs=(in_vmem(),) * (heads + 2),
        scratch_shapes=[pltpu.VMEM((width, cols), bf16), pltpu.VMEM((rows, cols), bf16)],
        compiler_params=pltpu.CompilerParams(vmem_limit_bytes=58 << 20),
        cost_estimate=LITTLE,
        name="project",
    )(place, rows_in, *blocks)


def weight_grad_kernel(flip, depth, place, *refs):
    me = place[0]
    pairs, refs = (refs[0:2], refs[2:4]), refs[4:]
    add, outs, whole = (refs[0], refs[1:-1], refs[-1]) if not flip else (None, refs[:-1], refs[-1])
    count = pairs[0][0].shape[1] // depth // 2
    if depth % HEAD:
        left = 0
        for rows_in, grads in pairs:
            cols = slice(left, left + grads.shape[1])
            whole[:, cols] = lax.dot_general(
                rows_in[...], grads[...], (((0,), (0,)), ((), ())), preferred_element_type=f32
            )
            left = cols.stop
    else:

        @pl.loop(0, count)
        def _(slot):
            at = lanes_of(me, 2 * slot + flip, depth)
            here = pl.ds(pl.multiple_of(slot * depth, depth), depth)
            left = 0
            for rows_in, grads in pairs:
                cols = slice(left, left + grads.shape[1])
                whole[here, cols] = lax.dot_general(
                    rows_in[:, at], grads[...], (((0,), (0,)), ((), ())), preferred_element_type=f32
                )
                left = cols.stop

    for slot in range(count):
        here = slice(slot * depth, (slot + 1) * depth)
        block = whole[lanes_of(me, 2 * slot + flip, depth), :] if depth % HEAD else whole[here, :]
        if flip:
            outs[0][here, :] = block.astype(bf16)
        else:
            outs[slot][...] = (block + add[here, :].astype(f32)).astype(bf16)


def weight_grad(place, pairs, depth, add=None):
    width, cols = pairs[0][0].shape[1], sum(grads.shape[1] for _, grads in pairs)
    count = width // depth // 2
    flip, extra = (1, []) if add is None else (0, [add])
    lines = [count * depth] if add is None else [depth] * count
    results = pl.pallas_call(
        functools.partial(weight_grad_kernel, flip, depth),
        out_shape=tuple(jax.ShapeDtypeStruct((n, cols), bf16) for n in lines),
        in_specs=[in_smem()] + [in_vmem()] * (4 + len(extra)),
        out_specs=(in_vmem(),) * len(lines),
        scratch_shapes=[pltpu.VMEM((width if depth % HEAD else count * depth, cols), f32)],
        compiler_params=pltpu.CompilerParams(vmem_limit_bytes=58 << 20),
        cost_estimate=LITTLE,
        name="weight_grad",
    )(place, *pairs[0], *pairs[1], *extra)
    return results if add is not None else results[0]


def input_grad_kernel(depth, place, grads, *refs):
    me = place[0]
    blocks, out, weights = refs[:-2], refs[-2], refs[-1]
    for mask, block in enumerate(blocks):
        weights[lanes_of(me, mask, depth), :] = block[:depth, :]
    step = 512

    @pl.loop(0, out.shape[1] // step)
    def _(part):
        here = pl.ds(pl.multiple_of(part * step, step), step)
        out[:, here] = lax.dot_general(
            grads[...], weights[here, :], (((1,), (1,)), ((), ())), preferred_element_type=f32
        ).astype(bf16)


def input_grad(place, grads, blocks, depth):
    return pl.pallas_call(
        functools.partial(input_grad_kernel, depth),
        out_shape=jax.ShapeDtypeStruct((grads.shape[0], depth * len(blocks)), bf16),
        in_specs=[in_smem()] + [in_vmem()] * (1 + len(blocks)),
        out_specs=in_vmem(),
        scratch_shapes=[pltpu.VMEM((depth * len(blocks), grads.shape[1]), bf16)],
        compiler_params=pltpu.CompilerParams(vmem_limit_bytes=58 << 20),
        cost_estimate=LITTLE,
        name="input_grad",
    )(place, grads, *blocks)


def pair_grad_kernel(half, left, right, other_left, other_right, out):
    def block(rows_in, grads):
        out[0] = lax.dot_general(
            rows_in[...], grads[...], (((0,), (0,)), ((), ())), preferred_element_type=f32
        ).astype(bf16)

    pl.when(pl.program_id(0) < half)(lambda: block(left, right))
    pl.when(pl.program_id(0) >= half)(lambda: block(other_left, other_right))


def pair_grad_of(left, right, other_left, other_right):
    rows, width = left.shape
    cols = right.shape[1]
    step, half = 256, width // 256
    first = pl.BlockSpec((rows, step), lambda i: (0, jnp.minimum(i, half - 1)))
    second = pl.BlockSpec((rows, step), lambda i: (0, jnp.maximum(i - half, 0)))
    return pl.pallas_call(
        functools.partial(pair_grad_kernel, half),
        grid=(2 * half,),
        out_shape=jax.ShapeDtypeStruct((2, width, cols), bf16),
        in_specs=[first, in_vmem(), second, in_vmem()],
        out_specs=pl.BlockSpec((1, step, cols), lambda i: (i // half, i % half, 0)),
        compiler_params=pltpu.CompilerParams(vmem_limit_bytes=58 << 20),
        cost_estimate=LITTLE,
        name="pair_grad",
    )(left, right, other_left, other_right)


def widen_kernel(pair, up, down, square):
    part = jnp.zeros((1, 1), f32)
    for source, target, turn in ((pair.at[0], up, False), (pair.at[1], down, True)):
        value = source[...].astype(f32)
        part = part + jnp.sum(jnp.sum(value * value, axis=0, keepdims=True), axis=1, keepdims=True)
        target[...] = value.T if turn else value
    square[...] = jnp.broadcast_to(part, square.shape)


def widen(pair):
    _, cols, units = pair.shape
    shapes = ((cols, units), (units, cols), (8, HEAD))
    return pl.pallas_call(
        widen_kernel,
        out_shape=tuple(jax.ShapeDtypeStruct(s, f32) for s in shapes),
        in_specs=[in_vmem()],
        out_specs=(in_vmem(),) * 3,
        compiler_params=pltpu.CompilerParams(vmem_limit_bytes=58 << 20),
        cost_estimate=LITTLE,
        name="widen",
    )(pair)


def total_kernel(head_cols, *refs):
    pieces, (qkv, out, square) = refs[:-3], refs[-3:]
    part = jnp.zeros((1, 1), f32)
    for j in range(4):
        cut = slice(j * head_cols, (j + 1) * head_cols)
        value = pieces[0][:, cut].astype(f32)
        for piece in pieces[1:]:
            value = value + piece[:, cut].astype(f32)
        part = part + jnp.sum(jnp.sum(value * value, axis=0, keepdims=True), axis=1, keepdims=True)
        if j < 3:
            qkv[j] = value
        else:
            out[...] = value.T
    square[...] = jnp.broadcast_to(part, square.shape)


def total_of(pieces, head_cols):
    depth = pieces[0].shape[0]
    shapes = ((3, depth, head_cols), (head_cols, depth), (8, HEAD))
    return pl.pallas_call(
        functools.partial(total_kernel, head_cols),
        out_shape=tuple(jax.ShapeDtypeStruct(s, f32) for s in shapes),
        in_specs=[in_vmem()] * len(pieces),
        out_specs=(in_vmem(),) * 3,
        compiler_params=pltpu.CompilerParams(vmem_limit_bytes=58 << 20),
        cost_estimate=LITTLE,
        name="total",
    )(*pieces)


ADAM_STEPS = 8


def adam_kernel(count, factor, decays, *refs):
    ins, outs = refs[: 4 * count], refs[4 * count :]
    for index in range(count):
        master, grad, first, second = (r[...] for r in ins[4 * index : 4 * index + 4])
        results = adam_update(master, grad, first, second, factor[0], decays[index])
        for target, value in zip(outs[3 * index : 3 * index + 3], results):
            target[...] = value


def adam(factor, decays, groups):
    specs, shapes, flat = ([], [], [])
    for group in groups:
        lines, cols = group[0].shape
        spec = pl.BlockSpec((lines // ADAM_STEPS, cols), lambda step: (step, 0))
        flat.extend(group)
        specs.extend([spec] * 3)
        shapes.extend([jax.ShapeDtypeStruct((lines, cols), f32)] * 3)
    in_specs = [s for spec in specs[::3] for s in [spec] * 4]
    results = pl.pallas_call(
        functools.partial(adam_kernel, len(groups)),
        grid=(ADAM_STEPS,),
        out_shape=tuple(shapes),
        in_specs=[in_smem(), in_smem()] + in_specs,
        out_specs=tuple(specs),
        compiler_params=pltpu.CompilerParams(vmem_limit_bytes=58 << 20),
        cost_estimate=LITTLE,
        name="adam",
    )(factor.reshape(1), decays, *flat)
    return [results[3 * i : 3 * i + 3] for i in range(len(groups))]


def norm_parts(rows):
    mean = jnp.mean(rows, axis=1, keepdims=True)
    centred = rows - mean
    rstd = lax.rsqrt(jnp.mean(centred * centred, axis=1, keepdims=True) + eps_norm)
    return (centred * rstd, rstd)


def norm_back(grad_out, normed, rstd, gain):
    scaled = grad_out * gain
    inner = (
        scaled
        - jnp.mean(scaled, axis=1, keepdims=True)
        - normed * jnp.mean(scaled * normed, axis=1, keepdims=True)
    )
    return (inner * rstd, jnp.sum(grad_out * normed, axis=0), jnp.sum(grad_out, axis=0))


def adam_update(master, grad, first, second, factor, decays):
    clipped = grad * factor
    first_new = beta_one * first + (1.0 - beta_one) * clipped
    second_new = beta_two * second + (1.0 - beta_two) * clipped * clipped
    fix_one = 1.0 - beta_one**step_count
    fix_two = 1.0 - beta_two**step_count
    update = first_new / fix_one / (jnp.sqrt(second_new / fix_two) + adam_eps)
    amount = learn_rate * (update + decay_rate * decays * master)
    return (amount, first_new, second_new)


def key_span(positions, seq_lengths):
    ends = jnp.cumsum(seq_lengths)
    starts = ends - seq_lengths
    inside = (positions[:, None] >= starts[None, :]) & (positions[:, None] < ends[None, :])
    begin = jnp.sum(jnp.where(inside, starts[None, :], 0), axis=1)
    end = jnp.sum(jnp.where(inside, ends[None, :], 0), axis=1)
    block = (positions - begin) // BLOCK
    return (begin, jnp.minimum(begin + (block + 1) * BLOCK, end))


def per_device(
    tokens,
    cotangent,
    w_qkv,
    w_out,
    w_up,
    w_down,
    norm_gains,
    norm_biases,
    m_qkv,
    m_out,
    m_up,
    m_down,
    m_gains,
    m_biases,
    v_qkv,
    v_out,
    v_up,
    v_down,
    v_gains,
    v_biases,
    seq_lengths,
    decay_mask,
):
    rows, width = tokens.shape
    ctx_count, tp_count = lax.axis_size("ctx"), lax.axis_size("tp")
    ctx_place = lax.axis_index("ctx").astype(jnp.int32)
    tp_place = lax.axis_index("tp").astype(jnp.int32)
    total_rows = rows * ctx_count
    part_rows = rows // tp_count
    head_cols = w_out.shape[0]
    heads = head_cols // HEAD
    units = w_up.shape[1]
    ctx_cols = w_out.shape[1]
    scale = HEAD ** (-0.5)
    my_head = lax.rem(ctx_place // 2, heads)

    place = jnp.stack((ctx_place, tp_place))

    small = jnp.concatenate((norm_gains, norm_biases), axis=0)
    small = jnp.pad(small, ((0, 12), (0, 3 * head_cols - ctx_cols)))
    qkv_pack = jnp.concatenate((w_qkv[0], w_qkv[1], w_qkv[2]), axis=1)
    qkv_pack = jnp.concatenate((qkv_pack, small), axis=0).astype(bf16)
    out_pack = w_out.T.astype(bf16)
    rest_pack = jnp.concatenate((w_up, w_down.T), axis=1).astype(bf16)

    x_slots = in_slots(tokens, tp_place, tp_count)
    c_slots = in_slots(cotangent, tp_place, tp_count)
    qkv_blocks, early = ctx_gather(qkv_pack, (out_pack, rest_pack, x_slots))
    out_pack, rest_pack, x_slots = early
    out_pack, rest_pack, qkv_blocks = lax.optimization_barrier((out_pack, rest_pack, qkv_blocks))
    out_full = lax.all_gather(out_pack, "ctx", axis=0, tiled=True)

    group = [s << 1 for s in range(heads)]
    far_bits = list(range(heads.bit_length(), ctx_count.bit_length() - 1))
    inner_rows = jnp.arange(part_rows, dtype=jnp.int32)
    positions = jnp.concatenate(
        [
            jnp.bitwise_xor(ctx_place, m) * rows + jnp.bitwise_xor(tp_place, s) * part_rows + inner_rows
            for m in group
            for s in range(tp_count)
        ]
    )
    lo, hi = key_span(positions, seq_lengths)
    span = jnp.stack((lo, hi))
    tiles = jnp.stack(
        (
            jnp.min(lo.reshape(-1, Q_TILE), axis=1) // (2 * rows),
            (jnp.max(hi.reshape(-1, Q_TILE), axis=1) + 2 * rows - 1) // (2 * rows),
        )
    )
    *pieces, a1, small = project(place, x_slots, qkv_blocks, heads, ctx_cols)
    gain_one, gain_two, bias_two = small[0], small[1], small[3]
    own_parts = [pieces[0]] + [ctx_xor(pieces[s], s << 1) for s in range(1, heads)]
    own_parts, rest_pack = lax.optimization_barrier((own_parts, rest_pack))
    rest_full = lax.all_gather(rest_pack, "ctx", axis=0, tiled=True)
    up_full, down_full = rest_full[:, :units], rest_full[:, units:]
    own = jnp.concatenate(own_parts, axis=0)
    even = own[:, HEAD:]
    for bit in far_bits:
        even = jnp.concatenate((even, ctx_xor(even, 1 << bit)), axis=0)
    odd = ctx_xor(even, 1)
    even = even if far_bits else None
    shape = (rows, tp_count, scale)
    mixed_low, mixed_t, lse = attention_forward(place, tiles, span, own, even, odd, *shape)

    back = [mixed_low[:rows]]
    for s in range(1, heads):
        back.append(ctx_xor(mixed_low[s * rows : (s + 1) * rows], s << 1))
    back = jnp.concatenate(back, axis=0)
    attn_vals = jnp.concatenate(
        [lax.dynamic_slice_in_dim(back, jnp.bitwise_xor(my_head, h) * rows, rows, 0) for h in range(heads)],
        axis=1,
    )
    attn = lax.dot_general(attn_vals, out_full, (((1,), (1,)), ((), ())), preferred_element_type=f32)
    x_own = x_slots[:part_rows].astype(f32)
    y1 = x_own + tp_scatter(attn.astype(bf16))
    normed2, rstd2 = norm_parts(y1)
    a2_own = (normed2 * gain_two + bias_two).astype(bf16)
    grad_act = jnp.dot(c_slots, down_full, preferred_element_type=f32)
    a2, grad_act = lax.optimization_barrier((tp_gather(a2_own), grad_act))
    a2 = jnp.concatenate(a2, axis=0)

    up = jnp.dot(a2, up_full, preferred_element_type=f32)
    cdf = 0.5 * (1.0 + lax.erf(up * inv_root_two))
    act = (up * cdf).astype(bf16)
    slope = cdf + up * jnp.exp(-0.5 * up * up) * inv_root_two_pi
    grad_up_in = (grad_act * slope).astype(bf16)
    grad_h2 = lax.dot_general(grad_up_in, up_full, (((1,), (1,)), ((), ())), preferred_element_type=f32).astype(bf16)
    grad_h2, act, grad_up_in = lax.optimization_barrier((grad_h2, act, grad_up_in))
    grad_h2 = tp_send(grad_h2)
    grad_h2 = tp_total(grad_h2)
    pair_grad = pair_grad_of(a2, grad_up_in, c_slots, act)
    pair_shard = lax.psum_scatter(pair_grad, "ctx", scatter_dimension=1, tiled=True)
    grad_h2, pair_grad = lax.optimization_barrier((grad_h2, pair_grad))

    dx2, dg2, dc2 = norm_back(grad_h2, normed2, rstd2, gain_two)
    c_own = c_slots[:part_rows].astype(f32)
    grad_y1 = c_own + dx2
    grad_attn = jnp.concatenate(tp_gather(grad_y1.astype(bf16)), axis=0)
    mixed = lax.dot_general(act, down_full, (((1,), (1,)), ((), ())), preferred_element_type=f32).astype(bf16)
    mixed, grad_attn = lax.optimization_barrier((mixed, grad_attn))
    block_out = (y1 + tp_scatter(mixed)).astype(bf16)

    grad_vals = jnp.dot(grad_attn, out_full, preferred_element_type=f32).astype(bf16)

    grads = []
    for s in range(heads):
        piece = lax.dynamic_slice_in_dim(grad_vals, jnp.bitwise_xor(my_head, s) * HEAD, HEAD, 1)
        grads.append(piece if s == 0 else ctx_xor(piece, s << 1))
    grads = jnp.concatenate(grads, axis=0)
    results = attention_backward(place, tiles, span, own, grads, mixed_t, lse, even, odd, *shape)
    grad_q, grad_kv, grad_odd = results
    got = ctx_xor(grad_odd, 1)
    for bit in reversed(far_bits):
        grad_kv = grad_kv + got.astype(f32)
        half = grad_kv.shape[0] // 2
        got = ctx_xor(grad_kv[half:].astype(bf16), 1 << bit)
        grad_kv = grad_kv[:half]
    got, block_out = lax.optimization_barrier((got, block_out))
    grad_own = merge(grad_q, grad_kv, got, heads)
    back = [grad_own[0]]
    for s in range(1, heads):
        back.append(ctx_xor(grad_own[s], s << 1))
    back = jnp.concatenate(back, axis=0)
    by_head = [
        lax.dynamic_slice_in_dim(back, jnp.bitwise_xor(my_head, h) * rows, rows, 0) for h in range(heads)
    ]
    grad_qkv_in = jnp.concatenate(
        [by_head[h][:, j * HEAD : (j + 1) * HEAD] for j in range(3) for h in range(heads)], axis=1
    )
    chips = list(range(0, ctx_count, 2))
    pairs = ((a1, grad_qkv_in), (grad_attn, attn_vals))
    sent = weight_grad(place, pairs, ctx_cols)
    sent, later, block_out = lax.optimization_barrier((sent, grad_qkv_in, tp_gather_first(block_out)))
    got = ctx_xor(sent, 1)
    grad_h1 = input_grad(place, later, qkv_blocks, ctx_cols)
    block_out, grad_h1 = lax.optimization_barrier((tp_gather_last(block_out), grad_h1))
    got, pair_shard = lax.optimization_barrier((got, pair_shard))
    summed = weight_grad(place, pairs, ctx_cols, got)
    grad_h1 = tp_send(grad_h1, summed)
    up_grad, down_grad, square = widen(pair_shard)
    arrived = [ctx_xor(summed[slot], mask) for slot, mask in enumerate(chips) if slot]
    grad_h1, _, up_grad = lax.optimization_barrier((grad_h1, summed, up_grad))
    grad_h1 = tp_total(grad_h1)
    block_out = slots_to_rows(block_out, tp_place)
    normed1, rstd1 = norm_parts(x_own)
    dx1, dg1, dc1 = norm_back(grad_h1, normed1, rstd1, gain_one)
    grad_tokens = (grad_y1 + dx1).astype(bf16)
    qkv_grad, out_grad, more = total_of([summed[0], *arrived], head_cols)
    square = square[0, 0] + more[0, 0]
    lines = jnp.stack((dg1, dg2, dc1, dc2)).reshape(-1, HEAD)
    sent = jnp.concatenate((lines, jnp.full((8, HEAD), square, f32)), axis=0)
    sent, grad_tokens = lax.optimization_barrier((sent, tp_gather_first(grad_tokens)))
    total, grad_tokens = sum_over_all(sent, grad_tokens)
    grad_tokens = tp_gather_last(grad_tokens)
    small_grad = total[:-8].reshape(4, width)
    total_sq = total[-1, 0] + jnp.sum(small_grad * small_grad)
    grad_norm = jnp.sqrt(total_sq)
    factor = 1.0 / jnp.maximum(grad_norm, 1.0)
    small_own = lax.dynamic_slice_in_dim(small_grad, ctx_place * ctx_cols, ctx_cols, 1)

    flags = decay_mask.astype(f32)
    flat = lambda value: value.reshape(-1, head_cols)
    matrices = adam(
        factor,
        flags,
        (
            (flat(w_qkv), flat(qkv_grad), flat(m_qkv), flat(v_qkv)),
            (w_out, out_grad, m_out, v_out),
            (w_up, up_grad, m_up, v_up),
            (w_down, down_grad, m_down, v_down),
        ),
    )
    matrices[0] = [value.reshape(w_qkv.shape) for value in matrices[0]]
    gains_new = adam_update(norm_gains, small_own[:2], m_gains, v_gains, factor, flags[4])
    biases_new = adam_update(norm_biases, small_own[2:], m_biases, v_biases, factor, flags[5])
    grad_tokens = slots_to_rows(grad_tokens, tp_place)
    shards = (qkv_grad, out_grad, up_grad, down_grad, small_own[:2], small_own[2:])
    updates = list(zip(*matrices, gains_new, biases_new))
    return (block_out, grad_tokens, grad_norm, *shards, *updates[0], *updates[1], *updates[2])


def solution(mesh):
    small = P(None, "ctx")
    weights = (P(None, "ctx", "tp"), P("tp", "ctx"), P("ctx", "tp"), P("tp", "ctx"), small, small)
    rows = (P("ctx", None), P("ctx", None))
    return jax.shard_map(
        per_device,
        mesh=mesh,
        in_specs=(*rows, *weights, *weights, *weights, P(), P()),
        out_specs=(*rows, P(), *weights, *weights, *weights, *weights),
        check_vma=False,
    )
```

```python
import functools
import math

import jax
import jax.numpy as jnp
from jax import lax
from jax.experimental import pallas as pl
from jax.experimental.pallas import tpu as pltpu
from jax.sharding import PartitionSpec as P

HEAD = 128
BLOCK = 256
Q_TILE = 512

eps_norm = 1e-05
neg_big = -1e30
beta_one = 0.9
beta_two = 0.95
adam_eps = 1e-08
learn_rate = 0.001
decay_rate = 0.1
step_count = 10.0
log2_e = math.log2(math.e)
inv_root_two = 1.0 / math.sqrt(2.0)
inv_root_two_pi = 1.0 / math.sqrt(2.0 * math.pi)
bf16 = jnp.bfloat16
f32 = jnp.float32


def ctx_xor(value, mask):
    count = lax.axis_size("ctx")
    return lax.ppermute(value, "ctx", [(place, place ^ mask) for place in range(count)])


def ctx_gather(own, early):
    blocks = [None] * lax.axis_size("ctx")
    for mask in range(0, len(blocks), 2):
        blocks[mask] = own if mask == 0 else ctx_xor(own, mask)
    blocks[2], early = lax.optimization_barrier((blocks[2], early))
    for mask in range(0, len(blocks), 2):
        blocks[mask + 1] = ctx_xor(blocks[mask], 1)
    return (blocks, early)


def tp_xor(value, mask):
    count = lax.axis_size("tp")
    return lax.ppermute(value, "tp", [(place, place ^ mask) for place in range(count)])


def tp_gather(own):
    return tp_gather_last(tp_gather_first(own))


def tp_gather_first(own):
    count = lax.axis_size("tp")
    return [own] + [tp_xor(own, s) for s in range(1, 3 if count == 4 else count)]


def tp_gather_last(parts):
    return parts + [tp_xor(parts[2], 1)] if lax.axis_size("tp") == 4 else parts


def tp_send(partial, behind=None):
    count = lax.axis_size("tp")
    rows = partial.shape[0] // count
    pieces = [partial[s * rows : (s + 1) * rows] for s in range(count)]
    if count != 4:
        return [pieces[0]] + [tp_xor(pieces[s], s) for s in range(1, count)]
    passed = tp_xor(pieces[3], 1)
    passed, near, _ = lax.optimization_barrier((passed, pieces[1], behind))
    joined = (pieces[2].astype(f32) + passed.astype(f32)).astype(bf16)
    return [pieces[0], tp_xor(near, 1), tp_xor(joined, 2)]


def tp_total(parts):
    total = parts[0].astype(f32)
    for piece in parts[1:]:
        total = total + piece.astype(f32)
    return total


def tp_scatter(partial):
    return tp_total(tp_send(partial))


def slots_to_rows(parts, tp_place):
    return in_slots(jnp.concatenate(parts, axis=0), tp_place, len(parts))


def in_slots(value, tp_place, count):
    rows = value.shape[0] // count
    order = [jnp.bitwise_xor(tp_place, s) * rows for s in range(count)]
    return jnp.concatenate([lax.dynamic_slice_in_dim(value, o, rows, 0) for o in order], axis=0)


def sum_over_all(value, later):
    if lax.axis_size("tp") == 4:
        one, two, three = (tp_xor(value, 1), tp_xor(value, 2), tp_xor(value, 3))
        value = (value + one) + (two + three)
    else:
        mask = 1
        while mask < lax.axis_size("tp"):
            value = value + tp_xor(value, mask)
            mask *= 2
    value, later = lax.optimization_barrier((value, later))
    mask = lax.axis_size("ctx") // 2
    while mask:
        value = value + ctx_xor(value, mask)
        mask //= 2
    return (value, later)


def scores_of(keys, query, where, lo, hi, scale):
    raw = lax.dot_general(keys, query, (((1,), (1,)), ((), ())), preferred_element_type=f32) * (scale * log2_e)
    return jnp.where((where >= lo) & (where < hi), raw, neg_big)


def key_halves(rows, place, chip):
    top = pl.multiple_of(jnp.bitwise_xor(chip, place[0] // 2) * rows, rows)
    core = lax.rem(place[0], 2)
    return (top, (2 * chip + core) * rows, (2 * chip + 1 - core) * rows)


def fill_positions(rows, chunks, place, where):
    where[...] = jnp.bitwise_xor(lax.broadcasted_iota(jnp.int32, where.shape, 0), place[1] * (rows // chunks))


def forward_kernel(rows, chunks, left, scale, place, tiles, span, own, *refs):
    even = own if left else refs[0]
    odd, out, out_t, lse_out, vt_even, vt_odd, where = refs[-7:]
    fill_positions(rows, chunks, place, where)
    for slot in range(odd.shape[0] // rows):
        cut = slice(slot * rows, (slot + 1) * rows)
        vt_even[:, cut] = even[cut, left + HEAD : left + 2 * HEAD].T
        vt_odd[:, cut] = odd[cut, HEAD:].T

    @pl.loop(0, own.shape[0] // Q_TILE)
    def _(tile):
        cut = pl.ds(pl.multiple_of(tile * Q_TILE, Q_TILE), Q_TILE)
        query = own[cut, :HEAD]
        lo, hi = span[0:1, cut], span[1:2, cut]

        def step(chip, carry):
            top, total, acc = carry
            at, first, second = key_halves(rows, place, chip)
            here = pl.ds(at, rows)
            one = scores_of(even[here, left : left + HEAD], query, where[...], lo - first, hi - first, scale)
            two = scores_of(odd[here, :HEAD], query, where[...], lo - second, hi - second, scale)
            new_top = jnp.maximum(
                top, jnp.maximum(jnp.max(one, axis=0, keepdims=True), jnp.max(two, axis=0, keepdims=True))
            )
            fade = jnp.exp2(top - new_top)
            one, two = jnp.exp2(one - new_top), jnp.exp2(two - new_top)
            total = total * fade + jnp.sum(one, axis=0, keepdims=True) + jnp.sum(two, axis=0, keepdims=True)
            acc = (
                acc * fade
                + jnp.dot(vt_even[:, here], one.astype(bf16), preferred_element_type=f32)
                + jnp.dot(vt_odd[:, here], two.astype(bf16), preferred_element_type=f32)
            )
            return (new_top, total, acc)

        start = (
            jnp.full((1, Q_TILE), neg_big, f32),
            jnp.zeros((1, Q_TILE), f32),
            jnp.zeros((HEAD, Q_TILE), f32),
        )
        top, total, acc = lax.fori_loop(tiles[0, tile], tiles[1, tile], step, start)
        result = acc / total
        out_t[:, cut] = result
        out[cut, :] = result.T.astype(bf16)
        lse_out[:, cut] = top + jnp.log2(total)


def backward_kernel(rows, chunks, left, scale, place, tiles, span, own, grad_out, out_t, lse_in, *refs):
    even = own if left else refs[0]
    odd, dq_out, dkv_even, dkv_odd, kt_even, kt_odd, d_odd, where = refs[-8:]
    fill_positions(rows, chunks, place, where)
    for slot in range(odd.shape[0] // rows):
        cut = slice(slot * rows, (slot + 1) * rows)
        kt_even[:, cut] = even[cut, left : left + HEAD].T
        kt_odd[:, cut] = odd[cut, :HEAD].T
    dkv_even[...] = jnp.zeros_like(dkv_even)
    d_odd[...] = jnp.zeros_like(d_odd)

    @pl.loop(0, own.shape[0] // Q_TILE)
    def _(tile):
        cut = pl.ds(pl.multiple_of(tile * Q_TILE, Q_TILE), Q_TILE)
        query, grad = own[cut, :HEAD], grad_out[cut, :]
        lo, hi, lse = span[0:1, cut], span[1:2, cut], lse_in[:, cut]
        inner = jnp.sum(grad.astype(f32).T * out_t[:, cut], axis=0, keepdims=True)

        def half(keys, values, keys_t, total, here, first, dq_t):
            scores = scores_of(keys, query, where[...], lo - first, hi - first, scale)
            prob = jnp.exp2(scores - lse)
            grad_prob = lax.dot_general(
                values, grad, (((1,), (1,)), ((), ())), preferred_element_type=f32
            )
            grad_scores = (prob * (grad_prob - inner)).astype(bf16)
            total[here, HEAD:] += jnp.dot(prob.astype(bf16), grad, preferred_element_type=f32)
            total[here, :HEAD] += jnp.dot(grad_scores, query, preferred_element_type=f32)
            return dq_t + jnp.dot(keys_t, grad_scores, preferred_element_type=f32)

        def step(chip, dq_t):
            at, first, second = key_halves(rows, place, chip)
            here = pl.ds(at, rows)
            keys, values = even[here, left : left + HEAD], even[here, left + HEAD : left + 2 * HEAD]
            dq_t = half(keys, values, kt_even[:, here], dkv_even, here, first, dq_t)
            return half(odd[here, :HEAD], odd[here, HEAD:], kt_odd[:, here], d_odd, here, second, dq_t)

        dq_t = lax.fori_loop(
            tiles[0, tile], tiles[1, tile], step, jnp.zeros((HEAD, Q_TILE), f32)
        )
        dq_out[cut, :] = (dq_t * scale).T.astype(bf16)

    dkv_even[:, :HEAD] = dkv_even[:, :HEAD] * scale
    dkv_odd[:, :HEAD] = (d_odd[:, :HEAD] * scale).astype(bf16)
    dkv_odd[:, HEAD:] = d_odd[:, HEAD:].astype(bf16)


LARGE = pl.CostEstimate(flops=180_000_000_000, bytes_accessed=180_000_000, transcendentals=0)
LITTLE = pl.CostEstimate(flops=1, bytes_accessed=1, transcendentals=0)


def in_vmem():
    return pl.BlockSpec(memory_space=pltpu.VMEM)


def in_smem():
    return pl.BlockSpec(memory_space=pltpu.SMEM)


def attention_forward(place, tiles, span, own, even, odd, rows, chunks, scale):
    queries, keys = own.shape[0], odd.shape[0]
    arrays = (own, odd) if even is None else (own, even, odd)
    return pl.pallas_call(
        functools.partial(forward_kernel, rows, chunks, HEAD if even is None else 0, scale),
        out_shape=(
            jax.ShapeDtypeStruct((queries, HEAD), bf16),
            jax.ShapeDtypeStruct((HEAD, queries), f32),
            jax.ShapeDtypeStruct((1, queries), f32),
        ),
        in_specs=[in_smem(), in_smem()] + [in_vmem()] * (1 + len(arrays)),
        out_specs=(in_vmem(), in_vmem(), in_vmem()),
        scratch_shapes=[
            pltpu.VMEM((HEAD, keys), bf16),
            pltpu.VMEM((HEAD, keys), bf16),
            pltpu.VMEM((rows, Q_TILE), jnp.int32),
        ],
        compiler_params=pltpu.CompilerParams(vmem_limit_bytes=58 << 20),
        cost_estimate=LITTLE,
        name="attention_forward",
    )(place, tiles, span, *arrays)


def attention_backward(place, tiles, span, own, grad, out_t, lse, even, odd, rows, chunks, scale):
    queries, keys = own.shape[0], odd.shape[0]
    arrays = (odd,) if even is None else (even, odd)
    return pl.pallas_call(
        functools.partial(backward_kernel, rows, chunks, HEAD if even is None else 0, scale),
        out_shape=(
            jax.ShapeDtypeStruct((queries, HEAD), bf16),
            jax.ShapeDtypeStruct((keys, 2 * HEAD), f32),
            jax.ShapeDtypeStruct((keys, 2 * HEAD), bf16),
        ),
        in_specs=[in_smem(), in_smem()] + [in_vmem()] * (5 + len(arrays)),
        out_specs=(in_vmem(),) * 3,
        scratch_shapes=[
            pltpu.VMEM((HEAD, keys), bf16),
            pltpu.VMEM((HEAD, keys), bf16),
            pltpu.VMEM((keys, 2 * HEAD), f32),
            pltpu.VMEM((rows, Q_TILE), jnp.int32),
        ],
        compiler_params=pltpu.CompilerParams(vmem_limit_bytes=58 << 20),
        cost_estimate=LITTLE,
        name="attention_backward",
    )(place, tiles, span, own, grad, out_t, lse, *arrays)


def merge_kernel(grad_q, grad_kv, *refs):
    got, outs = refs[0], refs[1:]
    rows = outs[0].shape[0]
    for slot, out in enumerate(outs):
        cut = slice(slot * rows, (slot + 1) * rows)
        out[:, :HEAD] = grad_q[cut, :]
        out[:, HEAD:] = (grad_kv[cut, :] + got[cut, :].astype(f32)).astype(bf16)


def merge(grad_q, grad_kv, got, count):
    rows = grad_q.shape[0] // count
    return pl.pallas_call(
        merge_kernel,
        out_shape=(jax.ShapeDtypeStruct((rows, 3 * HEAD), bf16),) * count,
        in_specs=[in_vmem()] * 3,
        out_specs=(in_vmem(),) * count,
        compiler_params=pltpu.CompilerParams(vmem_limit_bytes=58 << 20),
        cost_estimate=LARGE,
        name="merge",
    )(grad_q, grad_kv, got)


def lanes_of(me, mask, depth):
    at = jnp.bitwise_xor(me, mask) * depth
    return pl.ds(pl.multiple_of(at, depth), depth)


def project_kernel(rows, heads, depth, place, rows_in, *refs):
    blocks, outs, (a1, small, weights, result) = refs[: -4 - heads], refs[-4 - heads : -4], refs[-4:]
    me = place[0]
    my_head = lax.rem(me // 2, heads)
    if depth % HEAD:
        small[...] = blocks[-1][...]
        blocks = blocks[:-1]
    for mask, block in enumerate(blocks):
        at = lanes_of(me, mask, depth)
        weights[at, :] = block[:depth, :]
        if depth % HEAD == 0:
            small[:, at] = block[depth : depth + 8, :depth].astype(f32)
    part = rows // 4

    for quarter in range(4):
        cut = slice(quarter * part, (quarter + 1) * part)
        normed, _ = norm_parts(rows_in[cut, :].astype(f32))
        a1[cut, :] = (normed * small[0:1, :] + small[2:3, :]).astype(bf16)

    width = heads * HEAD

    for j in range(3):
        cut = slice(j * width, (j + 1) * width)
        result[:, cut] = jnp.dot(a1[...], weights[:, cut], preferred_element_type=f32).astype(bf16)

    for s in range(heads):
        at = jnp.bitwise_xor(my_head, s) * HEAD
        for j in range(3):
            here = pl.ds(pl.multiple_of(j * width + at, HEAD), HEAD)
            outs[s][:, j * HEAD : (j + 1) * HEAD] = result[:, here]


def project(place, rows_in, blocks, heads, depth):
    rows, width = rows_in.shape
    cols = 3 * heads * HEAD
    if depth % HEAD:
        known = jnp.stack([block[depth : depth + 8, :depth] for block in blocks])
        order = jnp.bitwise_xor(place[0], jnp.arange(len(blocks), dtype=jnp.int32))
        known = jnp.take(known, order, axis=0).transpose(1, 0, 2).reshape(8, width)
        blocks = [*blocks, known.astype(f32)]
    return pl.pallas_call(
        functools.partial(project_kernel, rows, heads, depth),
        out_shape=(
            *[jax.ShapeDtypeStruct((rows, 3 * HEAD), bf16)] * heads,
            jax.ShapeDtypeStruct((rows, width), bf16),
            jax.ShapeDtypeStruct((8, width), f32),
        ),
        in_specs=[in_smem()] + [in_vmem()] * (1 + len(blocks)),
        out_specs=(in_vmem(),) * (heads + 2),
        scratch_shapes=[pltpu.VMEM((width, cols), bf16), pltpu.VMEM((rows, cols), bf16)],
        compiler_params=pltpu.CompilerParams(vmem_limit_bytes=58 << 20),
        cost_estimate=LITTLE,
        name="project",
    )(place, rows_in, *blocks)


def weight_grad_kernel(flip, depth, place, rows_in, grads, *refs):
    me = place[0]
    count = rows_in.shape[1] // depth // 2
    outs = refs[:1] if flip else refs[1 : 1 + count]
    if depth % HEAD:
        whole = refs[-1]
        whole[...] = lax.dot_general(rows_in[...], grads[...], (((0,), (0,)), ((), ())), preferred_element_type=f32)
    for slot in range(count):
        at, here = lanes_of(me, 2 * slot + flip, depth), slice(slot * depth, (slot + 1) * depth)
        if depth % HEAD:
            block = whole[at, :]
        else:
            block = lax.dot_general(
                rows_in[:, at], grads[...], (((0,), (0,)), ((), ())), preferred_element_type=f32
            )
        if flip:
            outs[0][here, :] = block.astype(bf16)
        else:
            outs[slot][...] = (block + refs[0][here, :].astype(f32)).astype(bf16)


def weight_grad(place, rows_in, grads, depth, add=None):
    width, cols = rows_in.shape[1], grads.shape[1]
    count = width // depth // 2
    flip, extra = (1, []) if add is None else (0, [add])
    lines = [count * depth] if add is None else [depth] * count
    results = pl.pallas_call(
        functools.partial(weight_grad_kernel, flip, depth),
        out_shape=tuple(jax.ShapeDtypeStruct((n, cols), bf16) for n in lines),
        in_specs=[in_smem()] + [in_vmem()] * (2 + len(extra)),
        out_specs=(in_vmem(),) * len(lines),
        scratch_shapes=[pltpu.VMEM((width, cols), f32)] if depth % HEAD else [],
        compiler_params=pltpu.CompilerParams(vmem_limit_bytes=58 << 20),
        cost_estimate=LITTLE,
        name="weight_grad",
    )(place, rows_in, grads, *extra)
    return results if add is not None else results[0]


def input_grad_kernel(depth, place, grads, *refs):
    me = place[0]
    blocks, out, weights = refs[:-2], refs[-2], refs[-1]
    for mask, block in enumerate(blocks):
        weights[lanes_of(me, mask, depth), :] = block[:depth, :]
    step = 512

    @pl.loop(0, out.shape[1] // step)
    def _(part):
        here = pl.ds(pl.multiple_of(part * step, step), step)
        out[:, here] = lax.dot_general(
            grads[...], weights[here, :], (((1,), (1,)), ((), ())), preferred_element_type=f32
        ).astype(bf16)


def input_grad(place, grads, blocks, depth):
    return pl.pallas_call(
        functools.partial(input_grad_kernel, depth),
        out_shape=jax.ShapeDtypeStruct((grads.shape[0], depth * len(blocks)), bf16),
        in_specs=[in_smem()] + [in_vmem()] * (1 + len(blocks)),
        out_specs=in_vmem(),
        scratch_shapes=[pltpu.VMEM((depth * len(blocks), grads.shape[1]), bf16)],
        compiler_params=pltpu.CompilerParams(vmem_limit_bytes=58 << 20),
        cost_estimate=LARGE,
        name="input_grad",
    )(place, grads, *blocks)


def pair_grad_kernel(half, left, right, other_left, other_right, out):
    def block(rows_in, grads):
        out[0] = lax.dot_general(
            rows_in[...], grads[...], (((0,), (0,)), ((), ())), preferred_element_type=f32
        ).astype(bf16)

    pl.when(pl.program_id(0) < half)(lambda: block(left, right))
    pl.when(pl.program_id(0) >= half)(lambda: block(other_left, other_right))


def pair_grad_of(left, right, other_left, other_right):
    rows, width = left.shape
    cols = right.shape[1]
    step, half = 512, width // 512
    first = pl.BlockSpec((rows, step), lambda i: (0, jnp.minimum(i, half - 1)))
    second = pl.BlockSpec((rows, step), lambda i: (0, jnp.maximum(i - half, 0)))
    return pl.pallas_call(
        functools.partial(pair_grad_kernel, half),
        grid=(2 * half,),
        out_shape=jax.ShapeDtypeStruct((2, width, cols), bf16),
        in_specs=[first, in_vmem(), second, in_vmem()],
        out_specs=pl.BlockSpec((1, step, cols), lambda i: (i // half, i % half, 0)),
        compiler_params=pltpu.CompilerParams(vmem_limit_bytes=58 << 20),
        cost_estimate=LITTLE,
        name="pair_grad",
    )(left, right, other_left, other_right)


def widen_kernel(pair, up, down, square):
    part = jnp.zeros((1, 1), f32)
    for source, target, turn in ((pair.at[0], up, False), (pair.at[1], down, True)):
        value = source[...].astype(f32)
        part = part + jnp.sum(jnp.sum(value * value, axis=0, keepdims=True), axis=1, keepdims=True)
        target[...] = value.T if turn else value
    square[...] = jnp.broadcast_to(part, square.shape)


def widen(pair):
    _, cols, units = pair.shape
    shapes = ((cols, units), (units, cols), (8, HEAD))
    return pl.pallas_call(
        widen_kernel,
        out_shape=tuple(jax.ShapeDtypeStruct(s, f32) for s in shapes),
        in_specs=[in_vmem()],
        out_specs=(in_vmem(),) * 3,
        compiler_params=pltpu.CompilerParams(vmem_limit_bytes=58 << 20),
        cost_estimate=LITTLE,
        name="widen",
    )(pair)


def total_kernel(head_cols, out_t, *refs):
    pieces, (qkv, out, square) = refs[:-3], refs[-3:]
    value = out_t[...].astype(f32)
    out[...] = value.T
    part = jnp.sum(jnp.sum(value * value, axis=0, keepdims=True), axis=1, keepdims=True)
    for j in range(3):
        cut = slice(j * head_cols, (j + 1) * head_cols)
        value = pieces[0][:, cut].astype(f32)
        for piece in pieces[1:]:
            value = value + piece[:, cut].astype(f32)
        part = part + jnp.sum(jnp.sum(value * value, axis=0, keepdims=True), axis=1, keepdims=True)
        qkv[j] = value
    square[...] = jnp.broadcast_to(part, square.shape)


def total_of(pieces, out_t, head_cols):
    depth = pieces[0].shape[0]
    shapes = ((3, depth, head_cols), (head_cols, depth), (8, HEAD))
    return pl.pallas_call(
        functools.partial(total_kernel, head_cols),
        out_shape=tuple(jax.ShapeDtypeStruct(s, f32) for s in shapes),
        in_specs=[in_vmem()] * (1 + len(pieces)),
        out_specs=(in_vmem(),) * 3,
        compiler_params=pltpu.CompilerParams(vmem_limit_bytes=58 << 20),
        cost_estimate=LITTLE,
        name="total",
    )(out_t, *pieces)


ADAM_STEPS = 4


def adam_kernel(count, factor, decays, *refs):
    ins, outs = refs[: 4 * count], refs[4 * count :]
    for index in range(count):
        master, grad, first, second = (r[...] for r in ins[4 * index : 4 * index + 4])
        results = adam_update(master, grad, first, second, factor[0], decays[index])
        for target, value in zip(outs[3 * index : 3 * index + 3], results):
            target[...] = value


def adam(factor, decays, groups):
    specs, shapes, flat = ([], [], [])
    for group in groups:
        lines, cols = group[0].shape
        spec = pl.BlockSpec((lines // ADAM_STEPS, cols), lambda step: (step, 0))
        flat.extend(group)
        specs.extend([spec] * 3)
        shapes.extend([jax.ShapeDtypeStruct((lines, cols), f32)] * 3)
    in_specs = [s for spec in specs[::3] for s in [spec] * 4]
    results = pl.pallas_call(
        functools.partial(adam_kernel, len(groups)),
        grid=(ADAM_STEPS,),
        out_shape=tuple(shapes),
        in_specs=[in_smem(), in_smem()] + in_specs,
        out_specs=tuple(specs),
        compiler_params=pltpu.CompilerParams(vmem_limit_bytes=58 << 20),
        cost_estimate=LITTLE,
        name="adam",
    )(factor.reshape(1), decays, *flat)
    return [results[3 * i : 3 * i + 3] for i in range(len(groups))]


def norm_parts(rows):
    mean = jnp.mean(rows, axis=1, keepdims=True)
    centred = rows - mean
    rstd = lax.rsqrt(jnp.mean(centred * centred, axis=1, keepdims=True) + eps_norm)
    return (centred * rstd, rstd)


def norm_back(grad_out, normed, rstd, gain):
    scaled = grad_out * gain
    inner = (
        scaled
        - jnp.mean(scaled, axis=1, keepdims=True)
        - normed * jnp.mean(scaled * normed, axis=1, keepdims=True)
    )
    return (inner * rstd, jnp.sum(grad_out * normed, axis=0), jnp.sum(grad_out, axis=0))


def adam_update(master, grad, first, second, factor, decays):
    clipped = grad * factor
    first_new = beta_one * first + (1.0 - beta_one) * clipped
    second_new = beta_two * second + (1.0 - beta_two) * clipped * clipped
    fix_one = 1.0 - beta_one**step_count
    fix_two = 1.0 - beta_two**step_count
    update = first_new / fix_one / (jnp.sqrt(second_new / fix_two) + adam_eps)
    amount = learn_rate * (update + decay_rate * decays * master)
    return (amount, first_new, second_new)


def key_span(positions, seq_lengths):
    ends = jnp.cumsum(seq_lengths)
    starts = ends - seq_lengths
    inside = (positions[:, None] >= starts[None, :]) & (positions[:, None] < ends[None, :])
    begin = jnp.sum(jnp.where(inside, starts[None, :], 0), axis=1)
    end = jnp.sum(jnp.where(inside, ends[None, :], 0), axis=1)
    block = (positions - begin) // BLOCK
    return (begin, jnp.minimum(begin + (block + 1) * BLOCK, end))


def per_device(
    tokens,
    cotangent,
    w_qkv,
    w_out,
    w_up,
    w_down,
    norm_gains,
    norm_biases,
    m_qkv,
    m_out,
    m_up,
    m_down,
    m_gains,
    m_biases,
    v_qkv,
    v_out,
    v_up,
    v_down,
    v_gains,
    v_biases,
    seq_lengths,
    decay_mask,
):
    rows, width = tokens.shape
    ctx_count, tp_count = lax.axis_size("ctx"), lax.axis_size("tp")
    ctx_place = lax.axis_index("ctx").astype(jnp.int32)
    tp_place = lax.axis_index("tp").astype(jnp.int32)
    total_rows = rows * ctx_count
    part_rows = rows // tp_count
    head_cols = w_out.shape[0]
    heads = head_cols // HEAD
    units = w_up.shape[1]
    ctx_cols = w_out.shape[1]
    scale = HEAD ** (-0.5)
    my_head = lax.rem(ctx_place // 2, heads)

    place = jnp.stack((ctx_place, tp_place))

    small = jnp.concatenate((norm_gains, norm_biases), axis=0)
    small = jnp.pad(small, ((0, 12), (0, 3 * head_cols - ctx_cols)))
    qkv_pack = jnp.concatenate((w_qkv[0], w_qkv[1], w_qkv[2]), axis=1)
    qkv_pack = jnp.concatenate((qkv_pack, small), axis=0).astype(bf16)
    out_pack = w_out.T.astype(bf16)
    rest_pack = jnp.concatenate((w_up, w_down.T), axis=1).astype(bf16)

    x_slots = in_slots(tokens, tp_place, tp_count)
    c_slots = in_slots(cotangent, tp_place, tp_count)
    qkv_blocks, early = ctx_gather(qkv_pack, (out_pack, rest_pack, x_slots))
    out_pack, rest_pack, x_slots = early
    out_pack, rest_pack, qkv_blocks = lax.optimization_barrier((out_pack, rest_pack, qkv_blocks))
    out_full = lax.all_gather(out_pack, "ctx", axis=0, tiled=True)

    group = [s << 1 for s in range(heads)]
    far_bits = list(range(heads.bit_length(), ctx_count.bit_length() - 1))
    inner_rows = jnp.arange(part_rows, dtype=jnp.int32)
    positions = jnp.concatenate(
        [
            jnp.bitwise_xor(ctx_place, m) * rows + jnp.bitwise_xor(tp_place, s) * part_rows + inner_rows
            for m in group
            for s in range(tp_count)
        ]
    )
    lo, hi = key_span(positions, seq_lengths)
    span = jnp.stack((lo, hi))
    tiles = jnp.stack(
        (
            jnp.min(lo.reshape(-1, Q_TILE), axis=1) // (2 * rows),
            (jnp.max(hi.reshape(-1, Q_TILE), axis=1) + 2 * rows - 1) // (2 * rows),
        )
    )
    *pieces, a1, small = project(place, x_slots, qkv_blocks, heads, ctx_cols)
    gain_one, gain_two, bias_two = small[0], small[1], small[3]
    own_parts = [pieces[0]] + [ctx_xor(pieces[s], s << 1) for s in range(1, heads)]
    own_parts, rest_pack = lax.optimization_barrier((own_parts, rest_pack))
    rest_full = lax.all_gather(rest_pack, "ctx", axis=0, tiled=True)
    up_full, down_full = rest_full[:, :units], rest_full[:, units:]
    own = jnp.concatenate(own_parts, axis=0)
    even = own[:, HEAD:]
    for bit in far_bits:
        even = jnp.concatenate((even, ctx_xor(even, 1 << bit)), axis=0)
    odd = ctx_xor(even, 1)
    even = even if far_bits else None
    shape = (rows, tp_count, scale)
    mixed_low, mixed_t, lse = attention_forward(place, tiles, span, own, even, odd, *shape)

    back = [mixed_low[:rows]]
    for s in range(1, heads):
        back.append(ctx_xor(mixed_low[s * rows : (s + 1) * rows], s << 1))
    back = jnp.concatenate(back, axis=0)
    attn_vals = jnp.concatenate(
        [lax.dynamic_slice_in_dim(back, jnp.bitwise_xor(my_head, h) * rows, rows, 0) for h in range(heads)],
        axis=1,
    )
    attn = lax.dot_general(attn_vals, out_full, (((1,), (1,)), ((), ())), preferred_element_type=f32)
    x_own = x_slots[:part_rows].astype(f32)
    y1 = x_own + tp_scatter(attn.astype(bf16))
    normed2, rstd2 = norm_parts(y1)
    a2_own = (normed2 * gain_two + bias_two).astype(bf16)
    grad_act = jnp.dot(c_slots, down_full, preferred_element_type=f32)
    a2, grad_act = lax.optimization_barrier((tp_gather(a2_own), grad_act))
    a2 = jnp.concatenate(a2, axis=0)

    up = jnp.dot(a2, up_full, preferred_element_type=f32)
    cdf = 0.5 * (1.0 + lax.erf(up * inv_root_two))
    act = (up * cdf).astype(bf16)
    slope = cdf + up * jnp.exp(-0.5 * up * up) * inv_root_two_pi
    grad_up_in = (grad_act * slope).astype(bf16)
    grad_h2 = lax.dot_general(grad_up_in, up_full, (((1,), (1,)), ((), ())), preferred_element_type=f32).astype(bf16)
    grad_h2, act, grad_up_in = lax.optimization_barrier((grad_h2, act, grad_up_in))
    grad_h2 = tp_send(grad_h2)
    grad_h2 = tp_total(grad_h2)
    pair_grad = pair_grad_of(a2, grad_up_in, c_slots, act)
    pair_shard = lax.psum_scatter(pair_grad, "ctx", scatter_dimension=1, tiled=True)
    grad_h2, pair_grad = lax.optimization_barrier((grad_h2, pair_grad))

    dx2, dg2, dc2 = norm_back(grad_h2, normed2, rstd2, gain_two)
    c_own = c_slots[:part_rows].astype(f32)
    grad_y1 = c_own + dx2
    grad_attn = jnp.concatenate(tp_gather(grad_y1.astype(bf16)), axis=0)
    mixed = lax.dot_general(act, down_full, (((1,), (1,)), ((), ())), preferred_element_type=f32).astype(bf16)
    mixed, grad_attn = lax.optimization_barrier((mixed, grad_attn))
    block_out = (y1 + tp_scatter(mixed)).astype(bf16)

    grad_outw = lax.dot_general(grad_attn, attn_vals, (((0,), (0,)), ((), ())), preferred_element_type=f32)
    grad_outw = grad_outw.astype(bf16)
    grad_vals = jnp.dot(grad_attn, out_full, preferred_element_type=f32).astype(bf16)

    grads = []
    for s in range(heads):
        piece = lax.dynamic_slice_in_dim(grad_vals, jnp.bitwise_xor(my_head, s) * HEAD, HEAD, 1)
        grads.append(piece if s == 0 else ctx_xor(piece, s << 1))
    grads = jnp.concatenate(grads, axis=0)
    results = attention_backward(place, tiles, span, own, grads, mixed_t, lse, even, odd, *shape)
    grad_q, grad_kv, grad_odd = results
    got = ctx_xor(grad_odd, 1)
    for bit in reversed(far_bits):
        grad_kv = grad_kv + got.astype(f32)
        half = grad_kv.shape[0] // 2
        got = ctx_xor(grad_kv[half:].astype(bf16), 1 << bit)
        grad_kv = grad_kv[:half]
    got, block_out = lax.optimization_barrier((got, block_out))
    grad_own = merge(grad_q, grad_kv, got, heads)
    back = [grad_own[0]]
    for s in range(1, heads):
        back.append(ctx_xor(grad_own[s], s << 1))
    back = jnp.concatenate(back, axis=0)
    back, grad_outw = lax.optimization_barrier((back, grad_outw))
    by_head = [
        lax.dynamic_slice_in_dim(back, jnp.bitwise_xor(my_head, h) * rows, rows, 0) for h in range(heads)
    ]
    grad_qkv_in = jnp.concatenate(
        [by_head[h][:, j * HEAD : (j + 1) * HEAD] for j in range(3) for h in range(heads)], axis=1
    )
    chips = list(range(0, ctx_count, 2))
    sent = weight_grad(place, a1, grad_qkv_in, ctx_cols)
    sent, later, block_out = lax.optimization_barrier((sent, grad_qkv_in, tp_gather_first(block_out)))
    got = ctx_xor(sent, 1)
    grad_outw, pair_shard = lax.optimization_barrier((grad_outw, pair_shard))
    out_shard = lax.psum_scatter(grad_outw, "ctx", scatter_dimension=0, tiled=True)
    grad_h1 = input_grad(place, later, qkv_blocks, ctx_cols)
    block_out, grad_h1 = lax.optimization_barrier((tp_gather_last(block_out), grad_h1))
    summed = weight_grad(place, a1, grad_qkv_in, ctx_cols, got)
    grad_h1 = tp_send(grad_h1, summed)
    up_grad, down_grad, square = widen(pair_shard)
    arrived = [ctx_xor(summed[slot], mask) for slot, mask in enumerate(chips) if slot]
    grad_h1, _, up_grad, out_shard = lax.optimization_barrier((grad_h1, summed, up_grad, out_shard))
    grad_h1 = tp_total(grad_h1)
    block_out = slots_to_rows(block_out, tp_place)
    normed1, rstd1 = norm_parts(x_own)
    dx1, dg1, dc1 = norm_back(grad_h1, normed1, rstd1, gain_one)
    grad_tokens = (grad_y1 + dx1).astype(bf16)
    qkv_grad, out_grad, more = total_of([summed[0], *arrived], out_shard, head_cols)
    square = square[0, 0] + more[0, 0]
    lines = jnp.stack((dg1, dg2, dc1, dc2)).reshape(-1, HEAD)
    sent = jnp.concatenate((lines, jnp.full((8, HEAD), square, f32)), axis=0)
    sent, grad_tokens = lax.optimization_barrier((sent, tp_gather_first(grad_tokens)))
    total, grad_tokens = sum_over_all(sent, grad_tokens)
    grad_tokens = tp_gather_last(grad_tokens)
    small_grad = total[:-8].reshape(4, width)
    total_sq = total[-1, 0] + jnp.sum(small_grad * small_grad)
    grad_norm = jnp.sqrt(total_sq)
    factor = 1.0 / jnp.maximum(grad_norm, 1.0)
    small_own = lax.dynamic_slice_in_dim(small_grad, ctx_place * ctx_cols, ctx_cols, 1)

    flags = decay_mask.astype(f32)
    flat = lambda value: value.reshape(-1, head_cols)
    matrices = adam(
        factor,
        flags,
        (
            (flat(w_qkv), flat(qkv_grad), flat(m_qkv), flat(v_qkv)),
            (w_out, out_grad, m_out, v_out),
            (w_up, up_grad, m_up, v_up),
            (w_down, down_grad, m_down, v_down),
        ),
    )
    matrices[0] = [value.reshape(w_qkv.shape) for value in matrices[0]]
    gains_new = adam_update(norm_gains, small_own[:2], m_gains, v_gains, factor, flags[4])
    biases_new = adam_update(norm_biases, small_own[2:], m_biases, v_biases, factor, flags[5])
    grad_tokens = slots_to_rows(grad_tokens, tp_place)
    shards = (qkv_grad, out_grad, up_grad, down_grad, small_own[:2], small_own[2:])
    updates = list(zip(*matrices, gains_new, biases_new))
    return (block_out, grad_tokens, grad_norm, *shards, *updates[0], *updates[1], *updates[2])


def solution(mesh):
    small = P(None, "ctx")
    weights = (P(None, "ctx", "tp"), P("tp", "ctx"), P("ctx", "tp"), P("tp", "ctx"), small, small)
    rows = (P("ctx", None), P("ctx", None))
    return jax.shard_map(
        per_device,
        mesh=mesh,
        in_specs=(*rows, *weights, *weights, *weights, P(), P()),
        out_specs=(*rows, P(), *weights, *weights, *weights, *weights),
        check_vma=False,
    )
```

```python
import functools
import math

import jax
import jax.numpy as jnp
from jax import lax
from jax.experimental import pallas as pl
from jax.experimental.pallas import tpu as pltpu
from jax.sharding import PartitionSpec as P

HEAD = 128
BLOCK = 256
Q_TILE = 512

eps_norm = 1e-05
neg_big = -1e30
beta_one = 0.9
beta_two = 0.95
adam_eps = 1e-08
learn_rate = 0.001
decay_rate = 0.1
step_count = 10.0
log2_e = math.log2(math.e)
inv_root_two = 1.0 / math.sqrt(2.0)
inv_root_two_pi = 1.0 / math.sqrt(2.0 * math.pi)
bf16 = jnp.bfloat16
f32 = jnp.float32


def ctx_xor(value, mask):
    count = lax.axis_size("ctx")
    return lax.ppermute(value, "ctx", [(place, place ^ mask) for place in range(count)])


def ctx_gather(own, early):
    blocks = [None] * lax.axis_size("ctx")
    for mask in range(0, len(blocks), 2):
        blocks[mask] = own if mask == 0 else ctx_xor(own, mask)
    blocks[2], early = lax.optimization_barrier((blocks[2], early))
    for mask in range(0, len(blocks), 2):
        blocks[mask + 1] = ctx_xor(blocks[mask], 1)
    return (blocks, early)


def tp_xor(value, mask):
    count = lax.axis_size("tp")
    return lax.ppermute(value, "tp", [(place, place ^ mask) for place in range(count)])


def tp_gather(own):
    return tp_gather_last(tp_gather_first(own))


def tp_gather_first(own):
    count = lax.axis_size("tp")
    return [own] + [tp_xor(own, s) for s in range(1, 3 if count == 4 else count)]


def tp_gather_last(parts):
    return parts + [tp_xor(parts[2], 1)] if lax.axis_size("tp") == 4 else parts


def tp_send(partial, behind=None):
    count = lax.axis_size("tp")
    rows = partial.shape[0] // count
    pieces = [partial[s * rows : (s + 1) * rows] for s in range(count)]
    if count != 4:
        return [pieces[0]] + [tp_xor(pieces[s], s) for s in range(1, count)]
    passed = tp_xor(pieces[3], 1)
    passed, near, _ = lax.optimization_barrier((passed, pieces[1], behind))
    joined = (pieces[2].astype(f32) + passed.astype(f32)).astype(bf16)
    return [pieces[0], tp_xor(near, 1), tp_xor(joined, 2)]


def tp_total(parts):
    total = parts[0].astype(f32)
    for piece in parts[1:]:
        total = total + piece.astype(f32)
    return total


def tp_scatter(partial):
    return tp_total(tp_send(partial))


def slots_to_rows(parts, tp_place):
    return in_slots(jnp.concatenate(parts, axis=0), tp_place, len(parts))


def in_slots(value, tp_place, count):
    rows = value.shape[0] // count
    order = [jnp.bitwise_xor(tp_place, s) * rows for s in range(count)]
    return jnp.concatenate([lax.dynamic_slice_in_dim(value, o, rows, 0) for o in order], axis=0)


def sum_over_all(value, later):
    if lax.axis_size("tp") == 4:
        one, two, three = (tp_xor(value, 1), tp_xor(value, 2), tp_xor(value, 3))
        value = (value + one) + (two + three)
    else:
        mask = 1
        while mask < lax.axis_size("tp"):
            value = value + tp_xor(value, mask)
            mask *= 2
    value, later = lax.optimization_barrier((value, later))
    mask = lax.axis_size("ctx") // 2
    while mask:
        value = value + ctx_xor(value, mask)
        mask //= 2
    return (value, later)


def scores_of(keys, query, where, lo, hi, scale):
    raw = lax.dot_general(keys, query, (((1,), (1,)), ((), ())), preferred_element_type=f32) * (scale * log2_e)
    return jnp.where((where >= lo) & (where < hi), raw, neg_big)


def key_halves(rows, place, chip):
    top = pl.multiple_of(jnp.bitwise_xor(chip, place[0] // 2) * rows, rows)
    core = lax.rem(place[0], 2)
    return (top, (2 * chip + core) * rows, (2 * chip + 1 - core) * rows)


def fill_positions(rows, chunks, place, where):
    where[...] = jnp.bitwise_xor(lax.broadcasted_iota(jnp.int32, where.shape, 0), place[1] * (rows // chunks))


def forward_kernel(rows, chunks, left, scale, place, tiles, span, own, *refs):
    even = own if left else refs[0]
    odd, out, out_t, lse_out, vt_even, vt_odd, where = refs[-7:]
    fill_positions(rows, chunks, place, where)
    for slot in range(odd.shape[0] // rows):
        cut = slice(slot * rows, (slot + 1) * rows)
        vt_even[:, cut] = even[cut, left + HEAD : left + 2 * HEAD].T
        vt_odd[:, cut] = odd[cut, HEAD:].T

    @pl.loop(0, own.shape[0] // Q_TILE)
    def _(tile):
        cut = pl.ds(pl.multiple_of(tile * Q_TILE, Q_TILE), Q_TILE)
        query = own[cut, :HEAD]
        lo, hi = span[0:1, cut], span[1:2, cut]

        def step(chip, carry):
            top, total, acc = carry
            at, first, second = key_halves(rows, place, chip)
            here = pl.ds(at, rows)
            one = scores_of(even[here, left : left + HEAD], query, where[...], lo - first, hi - first, scale)
            two = scores_of(odd[here, :HEAD], query, where[...], lo - second, hi - second, scale)
            new_top = jnp.maximum(
                top, jnp.maximum(jnp.max(one, axis=0, keepdims=True), jnp.max(two, axis=0, keepdims=True))
            )
            fade = jnp.exp2(top - new_top)
            one, two = jnp.exp2(one - new_top), jnp.exp2(two - new_top)
            total = total * fade + jnp.sum(one, axis=0, keepdims=True) + jnp.sum(two, axis=0, keepdims=True)
            acc = (
                acc * fade
                + jnp.dot(vt_even[:, here], one.astype(bf16), preferred_element_type=f32)
                + jnp.dot(vt_odd[:, here], two.astype(bf16), preferred_element_type=f32)
            )
            return (new_top, total, acc)

        start = (
            jnp.full((1, Q_TILE), neg_big, f32),
            jnp.zeros((1, Q_TILE), f32),
            jnp.zeros((HEAD, Q_TILE), f32),
        )
        top, total, acc = lax.fori_loop(tiles[0, tile], tiles[1, tile], step, start)
        result = acc / total
        out_t[:, cut] = result
        out[cut, :] = result.T.astype(bf16)
        lse_out[:, cut] = top + jnp.log2(total)


def backward_kernel(rows, chunks, left, scale, place, tiles, span, own, grad_out, out_t, lse_in, *refs):
    even = own if left else refs[0]
    odd, dq_out, dkv_even, dkv_odd, kt_even, kt_odd, d_odd, where = refs[-8:]
    fill_positions(rows, chunks, place, where)
    for slot in range(odd.shape[0] // rows):
        cut = slice(slot * rows, (slot + 1) * rows)
        kt_even[:, cut] = even[cut, left : left + HEAD].T
        kt_odd[:, cut] = odd[cut, :HEAD].T
    dkv_even[...] = jnp.zeros_like(dkv_even)
    d_odd[...] = jnp.zeros_like(d_odd)

    @pl.loop(0, own.shape[0] // Q_TILE)
    def _(tile):
        cut = pl.ds(pl.multiple_of(tile * Q_TILE, Q_TILE), Q_TILE)
        query, grad = own[cut, :HEAD], grad_out[cut, :]
        lo, hi, lse = span[0:1, cut], span[1:2, cut], lse_in[:, cut]
        inner = jnp.sum(grad.astype(f32).T * out_t[:, cut], axis=0, keepdims=True)

        def half(keys, values, keys_t, total, here, first, dq_t):
            scores = scores_of(keys, query, where[...], lo - first, hi - first, scale)
            prob = jnp.exp2(scores - lse)
            grad_prob = lax.dot_general(
                values, grad, (((1,), (1,)), ((), ())), preferred_element_type=f32
            )
            grad_scores = (prob * (grad_prob - inner)).astype(bf16)
            total[here, HEAD:] += jnp.dot(prob.astype(bf16), grad, preferred_element_type=f32)
            total[here, :HEAD] += jnp.dot(grad_scores, query, preferred_element_type=f32)
            return dq_t + jnp.dot(keys_t, grad_scores, preferred_element_type=f32)

        def step(chip, dq_t):
            at, first, second = key_halves(rows, place, chip)
            here = pl.ds(at, rows)
            keys, values = even[here, left : left + HEAD], even[here, left + HEAD : left + 2 * HEAD]
            dq_t = half(keys, values, kt_even[:, here], dkv_even, here, first, dq_t)
            return half(odd[here, :HEAD], odd[here, HEAD:], kt_odd[:, here], d_odd, here, second, dq_t)

        dq_t = lax.fori_loop(
            tiles[0, tile], tiles[1, tile], step, jnp.zeros((HEAD, Q_TILE), f32)
        )
        dq_out[cut, :] = (dq_t * scale).T.astype(bf16)

    dkv_even[:, :HEAD] = dkv_even[:, :HEAD] * scale
    dkv_odd[:, :HEAD] = (d_odd[:, :HEAD] * scale).astype(bf16)
    dkv_odd[:, HEAD:] = d_odd[:, HEAD:].astype(bf16)


LARGE = pl.CostEstimate(flops=180_000_000_000, bytes_accessed=180_000_000, transcendentals=0)
LITTLE = pl.CostEstimate(flops=1, bytes_accessed=1, transcendentals=0)


def in_vmem():
    return pl.BlockSpec(memory_space=pltpu.VMEM)


def in_smem():
    return pl.BlockSpec(memory_space=pltpu.SMEM)


def attention_forward(place, tiles, span, own, even, odd, rows, chunks, scale):
    queries, keys = own.shape[0], odd.shape[0]
    arrays = (own, odd) if even is None else (own, even, odd)
    return pl.pallas_call(
        functools.partial(forward_kernel, rows, chunks, HEAD if even is None else 0, scale),
        out_shape=(
            jax.ShapeDtypeStruct((queries, HEAD), bf16),
            jax.ShapeDtypeStruct((HEAD, queries), f32),
            jax.ShapeDtypeStruct((1, queries), f32),
        ),
        in_specs=[in_smem(), in_smem()] + [in_vmem()] * (1 + len(arrays)),
        out_specs=(in_vmem(), in_vmem(), in_vmem()),
        scratch_shapes=[
            pltpu.VMEM((HEAD, keys), bf16),
            pltpu.VMEM((HEAD, keys), bf16),
            pltpu.VMEM((rows, Q_TILE), jnp.int32),
        ],
        compiler_params=pltpu.CompilerParams(vmem_limit_bytes=58 << 20),
        cost_estimate=LITTLE,
        name="attention_forward",
    )(place, tiles, span, *arrays)


def attention_backward(place, tiles, span, own, grad, out_t, lse, even, odd, rows, chunks, scale):
    queries, keys = own.shape[0], odd.shape[0]
    arrays = (odd,) if even is None else (even, odd)
    return pl.pallas_call(
        functools.partial(backward_kernel, rows, chunks, HEAD if even is None else 0, scale),
        out_shape=(
            jax.ShapeDtypeStruct((queries, HEAD), bf16),
            jax.ShapeDtypeStruct((keys, 2 * HEAD), f32),
            jax.ShapeDtypeStruct((keys, 2 * HEAD), bf16),
        ),
        in_specs=[in_smem(), in_smem()] + [in_vmem()] * (5 + len(arrays)),
        out_specs=(in_vmem(),) * 3,
        scratch_shapes=[
            pltpu.VMEM((HEAD, keys), bf16),
            pltpu.VMEM((HEAD, keys), bf16),
            pltpu.VMEM((keys, 2 * HEAD), f32),
            pltpu.VMEM((rows, Q_TILE), jnp.int32),
        ],
        compiler_params=pltpu.CompilerParams(vmem_limit_bytes=58 << 20),
        cost_estimate=LITTLE,
        name="attention_backward",
    )(place, tiles, span, own, grad, out_t, lse, *arrays)


def merge_kernel(grad_q, grad_kv, *refs):
    got, outs = refs[0], refs[1:]
    rows = outs[0].shape[0]
    for slot, out in enumerate(outs):
        cut = slice(slot * rows, (slot + 1) * rows)
        out[:, :HEAD] = grad_q[cut, :]
        out[:, HEAD:] = (grad_kv[cut, :] + got[cut, :].astype(f32)).astype(bf16)


def merge(grad_q, grad_kv, got, count):
    rows = grad_q.shape[0] // count
    return pl.pallas_call(
        merge_kernel,
        out_shape=(jax.ShapeDtypeStruct((rows, 3 * HEAD), bf16),) * count,
        in_specs=[in_vmem()] * 3,
        out_specs=(in_vmem(),) * count,
        compiler_params=pltpu.CompilerParams(vmem_limit_bytes=58 << 20),
        cost_estimate=LARGE,
        name="merge",
    )(grad_q, grad_kv, got)


def lanes_of(me, mask, depth):
    at = jnp.bitwise_xor(me, mask) * depth
    return pl.ds(pl.multiple_of(at, depth), depth)


def project_kernel(rows, heads, depth, place, rows_in, *refs):
    blocks, outs, (a1, small, weights, result) = refs[: -4 - heads], refs[-4 - heads : -4], refs[-4:]
    me = place[0]
    my_head = lax.rem(me // 2, heads)
    if depth % HEAD:
        small[...] = blocks[-1][...]
        blocks = blocks[:-1]
    for mask, block in enumerate(blocks):
        at = lanes_of(me, mask, depth)
        weights[at, :] = block[:depth, :]
        if depth % HEAD == 0:
            small[:, at] = block[depth : depth + 8, :depth].astype(f32)
    part = rows // 4

    for quarter in range(4):
        cut = slice(quarter * part, (quarter + 1) * part)
        normed, _ = norm_parts(rows_in[cut, :].astype(f32))
        a1[cut, :] = (normed * small[0:1, :] + small[2:3, :]).astype(bf16)

    width = heads * HEAD

    for j in range(3):
        cut = slice(j * width, (j + 1) * width)
        result[:, cut] = jnp.dot(a1[...], weights[:, cut], preferred_element_type=f32).astype(bf16)

    for s in range(heads):
        at = jnp.bitwise_xor(my_head, s) * HEAD
        for j in range(3):
            here = pl.ds(pl.multiple_of(j * width + at, HEAD), HEAD)
            outs[s][:, j * HEAD : (j + 1) * HEAD] = result[:, here]


def project(place, rows_in, blocks, heads, depth):
    rows, width = rows_in.shape
    cols = 3 * heads * HEAD
    if depth % HEAD:
        known = jnp.stack([block[depth : depth + 8, :depth] for block in blocks])
        order = jnp.bitwise_xor(place[0], jnp.arange(len(blocks), dtype=jnp.int32))
        known = jnp.take(known, order, axis=0).transpose(1, 0, 2).reshape(8, width)
        blocks = [*blocks, known.astype(f32)]
    return pl.pallas_call(
        functools.partial(project_kernel, rows, heads, depth),
        out_shape=(
            *[jax.ShapeDtypeStruct((rows, 3 * HEAD), bf16)] * heads,
            jax.ShapeDtypeStruct((rows, width), bf16),
            jax.ShapeDtypeStruct((8, width), f32),
        ),
        in_specs=[in_smem()] + [in_vmem()] * (1 + len(blocks)),
        out_specs=(in_vmem(),) * (heads + 2),
        scratch_shapes=[pltpu.VMEM((width, cols), bf16), pltpu.VMEM((rows, cols), bf16)],
        compiler_params=pltpu.CompilerParams(vmem_limit_bytes=58 << 20),
        cost_estimate=LITTLE,
        name="project",
    )(place, rows_in, *blocks)


def weight_grad_kernel(flip, depth, place, rows_in, grads, *refs):
    me = place[0]
    count = rows_in.shape[1] // depth // 2
    outs = refs[:1] if flip else refs[1 : 1 + count]
    if depth % HEAD:
        whole = refs[-1]
        whole[...] = lax.dot_general(rows_in[...], grads[...], (((0,), (0,)), ((), ())), preferred_element_type=f32)
    for slot in range(count):
        at, here = lanes_of(me, 2 * slot + flip, depth), slice(slot * depth, (slot + 1) * depth)
        if depth % HEAD:
            block = whole[at, :]
        else:
            block = lax.dot_general(
                rows_in[:, at], grads[...], (((0,), (0,)), ((), ())), preferred_element_type=f32
            )
        if flip:
            outs[0][here, :] = block.astype(bf16)
        else:
            outs[slot][...] = (block + refs[0][here, :].astype(f32)).astype(bf16)


def weight_grad(place, rows_in, grads, depth, add=None):
    width, cols = rows_in.shape[1], grads.shape[1]
    count = width // depth // 2
    flip, extra = (1, []) if add is None else (0, [add])
    lines = [count * depth] if add is None else [depth] * count
    results = pl.pallas_call(
        functools.partial(weight_grad_kernel, flip, depth),
        out_shape=tuple(jax.ShapeDtypeStruct((n, cols), bf16) for n in lines),
        in_specs=[in_smem()] + [in_vmem()] * (2 + len(extra)),
        out_specs=(in_vmem(),) * len(lines),
        scratch_shapes=[pltpu.VMEM((width, cols), f32)] if depth % HEAD else [],
        compiler_params=pltpu.CompilerParams(vmem_limit_bytes=58 << 20),
        cost_estimate=LITTLE,
        name="weight_grad",
    )(place, rows_in, grads, *extra)
    return results if add is not None else results[0]


def input_grad_kernel(depth, place, grads, *refs):
    me = place[0]
    blocks, out, weights = refs[:-2], refs[-2], refs[-1]
    for mask, block in enumerate(blocks):
        weights[lanes_of(me, mask, depth), :] = block[:depth, :]
    step = 512

    @pl.loop(0, out.shape[1] // step)
    def _(part):
        here = pl.ds(pl.multiple_of(part * step, step), step)
        out[:, here] = lax.dot_general(
            grads[...], weights[here, :], (((1,), (1,)), ((), ())), preferred_element_type=f32
        ).astype(bf16)


def input_grad(place, grads, blocks, depth):
    return pl.pallas_call(
        functools.partial(input_grad_kernel, depth),
        out_shape=jax.ShapeDtypeStruct((grads.shape[0], depth * len(blocks)), bf16),
        in_specs=[in_smem()] + [in_vmem()] * (1 + len(blocks)),
        out_specs=in_vmem(),
        scratch_shapes=[pltpu.VMEM((depth * len(blocks), grads.shape[1]), bf16)],
        compiler_params=pltpu.CompilerParams(vmem_limit_bytes=58 << 20),
        cost_estimate=LARGE,
        name="input_grad",
    )(place, grads, *blocks)


def pair_grad_kernel(half, left, right, other_left, other_right, out):
    def block(rows_in, grads):
        out[0] = lax.dot_general(
            rows_in[...], grads[...], (((0,), (0,)), ((), ())), preferred_element_type=f32
        ).astype(bf16)

    pl.when(pl.program_id(0) < half)(lambda: block(left, right))
    pl.when(pl.program_id(0) >= half)(lambda: block(other_left, other_right))


def pair_grad_of(left, right, other_left, other_right):
    rows, width = left.shape
    cols = right.shape[1]
    step, half = 512, width // 512
    first = pl.BlockSpec((rows, step), lambda i: (0, jnp.minimum(i, half - 1)))
    second = pl.BlockSpec((rows, step), lambda i: (0, jnp.maximum(i - half, 0)))
    return pl.pallas_call(
        functools.partial(pair_grad_kernel, half),
        grid=(2 * half,),
        out_shape=jax.ShapeDtypeStruct((2, width, cols), bf16),
        in_specs=[first, in_vmem(), second, in_vmem()],
        out_specs=pl.BlockSpec((1, step, cols), lambda i: (i // half, i % half, 0)),
        compiler_params=pltpu.CompilerParams(vmem_limit_bytes=58 << 20),
        cost_estimate=LITTLE,
        name="pair_grad",
    )(left, right, other_left, other_right)


def widen_kernel(pair, up, down, square):
    part = jnp.zeros((1, 1), f32)
    for source, target, turn in ((pair.at[0], up, False), (pair.at[1], down, True)):
        value = source[...].astype(f32)
        part = part + jnp.sum(jnp.sum(value * value, axis=0, keepdims=True), axis=1, keepdims=True)
        target[...] = value.T if turn else value
    square[...] = jnp.broadcast_to(part, square.shape)


def widen(pair):
    _, cols, units = pair.shape
    shapes = ((cols, units), (units, cols), (8, HEAD))
    return pl.pallas_call(
        widen_kernel,
        out_shape=tuple(jax.ShapeDtypeStruct(s, f32) for s in shapes),
        in_specs=[in_vmem()],
        out_specs=(in_vmem(),) * 3,
        compiler_params=pltpu.CompilerParams(vmem_limit_bytes=58 << 20),
        cost_estimate=LITTLE,
        name="widen",
    )(pair)


def total_kernel(head_cols, out_t, *refs):
    pieces, (qkv, out, square) = refs[:-3], refs[-3:]
    value = out_t[...].astype(f32)
    out[...] = value.T
    part = jnp.sum(jnp.sum(value * value, axis=0, keepdims=True), axis=1, keepdims=True)
    for j in range(3):
        cut = slice(j * head_cols, (j + 1) * head_cols)
        value = pieces[0][:, cut].astype(f32)
        for piece in pieces[1:]:
            value = value + piece[:, cut].astype(f32)
        part = part + jnp.sum(jnp.sum(value * value, axis=0, keepdims=True), axis=1, keepdims=True)
        qkv[j] = value
    square[...] = jnp.broadcast_to(part, square.shape)


def total_of(pieces, out_t, head_cols):
    depth = pieces[0].shape[0]
    shapes = ((3, depth, head_cols), (head_cols, depth), (8, HEAD))
    return pl.pallas_call(
        functools.partial(total_kernel, head_cols),
        out_shape=tuple(jax.ShapeDtypeStruct(s, f32) for s in shapes),
        in_specs=[in_vmem()] * (1 + len(pieces)),
        out_specs=(in_vmem(),) * 3,
        compiler_params=pltpu.CompilerParams(vmem_limit_bytes=58 << 20),
        cost_estimate=LITTLE,
        name="total",
    )(out_t, *pieces)


ADAM_STEPS = 4


def adam_kernel(count, factor, decays, *refs):
    ins, outs = refs[: 4 * count], refs[4 * count :]
    for index in range(count):
        master, grad, first, second = (r[...] for r in ins[4 * index : 4 * index + 4])
        results = adam_update(master, grad, first, second, factor[0], decays[index])
        for target, value in zip(outs[3 * index : 3 * index + 3], results):
            target[...] = value


def adam(factor, decays, groups):
    specs, shapes, flat = ([], [], [])
    for group in groups:
        lines, cols = group[0].shape
        spec = pl.BlockSpec((lines // ADAM_STEPS, cols), lambda step: (step, 0))
        flat.extend(group)
        specs.extend([spec] * 3)
        shapes.extend([jax.ShapeDtypeStruct((lines, cols), f32)] * 3)
    in_specs = [s for spec in specs[::3] for s in [spec] * 4]
    results = pl.pallas_call(
        functools.partial(adam_kernel, len(groups)),
        grid=(ADAM_STEPS,),
        out_shape=tuple(shapes),
        in_specs=[in_smem(), in_smem()] + in_specs,
        out_specs=tuple(specs),
        compiler_params=pltpu.CompilerParams(vmem_limit_bytes=58 << 20),
        cost_estimate=LITTLE,
        name="adam",
    )(factor.reshape(1), decays, *flat)
    return [results[3 * i : 3 * i + 3] for i in range(len(groups))]


def norm_parts(rows):
    mean = jnp.mean(rows, axis=1, keepdims=True)
    centred = rows - mean
    rstd = lax.rsqrt(jnp.mean(centred * centred, axis=1, keepdims=True) + eps_norm)
    return (centred * rstd, rstd)


def norm_back(grad_out, normed, rstd, gain):
    scaled = grad_out * gain
    inner = (
        scaled
        - jnp.mean(scaled, axis=1, keepdims=True)
        - normed * jnp.mean(scaled * normed, axis=1, keepdims=True)
    )
    return (inner * rstd, jnp.sum(grad_out * normed, axis=0), jnp.sum(grad_out, axis=0))


def adam_update(master, grad, first, second, factor, decays):
    clipped = grad * factor
    first_new = beta_one * first + (1.0 - beta_one) * clipped
    second_new = beta_two * second + (1.0 - beta_two) * clipped * clipped
    fix_one = 1.0 - beta_one**step_count
    fix_two = 1.0 - beta_two**step_count
    update = first_new / fix_one / (jnp.sqrt(second_new / fix_two) + adam_eps)
    amount = learn_rate * (update + decay_rate * decays * master)
    return (amount, first_new, second_new)


def key_span(positions, seq_lengths):
    ends = jnp.cumsum(seq_lengths)
    starts = ends - seq_lengths
    inside = (positions[:, None] >= starts[None, :]) & (positions[:, None] < ends[None, :])
    begin = jnp.sum(jnp.where(inside, starts[None, :], 0), axis=1)
    end = jnp.sum(jnp.where(inside, ends[None, :], 0), axis=1)
    block = (positions - begin) // BLOCK
    return (begin, jnp.minimum(begin + (block + 1) * BLOCK, end))


def per_device(
    tokens,
    cotangent,
    w_qkv,
    w_out,
    w_up,
    w_down,
    norm_gains,
    norm_biases,
    m_qkv,
    m_out,
    m_up,
    m_down,
    m_gains,
    m_biases,
    v_qkv,
    v_out,
    v_up,
    v_down,
    v_gains,
    v_biases,
    seq_lengths,
    decay_mask,
):
    rows, width = tokens.shape
    ctx_count, tp_count = lax.axis_size("ctx"), lax.axis_size("tp")
    ctx_place = lax.axis_index("ctx").astype(jnp.int32)
    tp_place = lax.axis_index("tp").astype(jnp.int32)
    total_rows = rows * ctx_count
    part_rows = rows // tp_count
    head_cols = w_out.shape[0]
    heads = head_cols // HEAD
    units = w_up.shape[1]
    ctx_cols = w_out.shape[1]
    scale = HEAD ** (-0.5)
    my_head = lax.rem(ctx_place // 2, heads)

    place = jnp.stack((ctx_place, tp_place))

    small = jnp.concatenate((norm_gains, norm_biases), axis=0)
    small = jnp.pad(small, ((0, 12), (0, 3 * head_cols - ctx_cols)))
    qkv_pack = jnp.concatenate((w_qkv[0], w_qkv[1], w_qkv[2]), axis=1)
    qkv_pack = jnp.concatenate((qkv_pack, small), axis=0).astype(bf16)
    out_pack = w_out.T.astype(bf16)
    rest_pack = jnp.concatenate((w_up, w_down.T), axis=1).astype(bf16)

    x_slots = in_slots(tokens, tp_place, tp_count)
    c_slots = in_slots(cotangent, tp_place, tp_count)
    qkv_blocks, early = ctx_gather(qkv_pack, (out_pack, rest_pack, x_slots))
    out_pack, rest_pack, x_slots = early
    out_pack, rest_pack, qkv_blocks = lax.optimization_barrier((out_pack, rest_pack, qkv_blocks))
    out_full = lax.all_gather(out_pack, "ctx", axis=0, tiled=True)

    group = [s << 1 for s in range(heads)]
    far_bits = list(range(heads.bit_length(), ctx_count.bit_length() - 1))
    inner_rows = jnp.arange(part_rows, dtype=jnp.int32)
    positions = jnp.concatenate(
        [
            jnp.bitwise_xor(ctx_place, m) * rows + jnp.bitwise_xor(tp_place, s) * part_rows + inner_rows
            for m in group
            for s in range(tp_count)
        ]
    )
    lo, hi = key_span(positions, seq_lengths)
    span = jnp.stack((lo, hi))
    tiles = jnp.stack(
        (
            jnp.min(lo.reshape(-1, Q_TILE), axis=1) // (2 * rows),
            (jnp.max(hi.reshape(-1, Q_TILE), axis=1) + 2 * rows - 1) // (2 * rows),
        )
    )
    *pieces, a1, small = project(place, x_slots, qkv_blocks, heads, ctx_cols)
    gain_one, gain_two, bias_two = small[0], small[1], small[3]
    own_parts = [pieces[0]] + [ctx_xor(pieces[s], s << 1) for s in range(1, heads)]
    own_parts, rest_pack = lax.optimization_barrier((own_parts, rest_pack))
    rest_full = lax.all_gather(rest_pack, "ctx", axis=0, tiled=True)
    up_full, down_full = rest_full[:, :units], rest_full[:, units:]
    own = jnp.concatenate(own_parts, axis=0)
    even = own[:, HEAD:]
    for bit in far_bits:
        even = jnp.concatenate((even, ctx_xor(even, 1 << bit)), axis=0)
    odd = ctx_xor(even, 1)
    even = even if far_bits else None
    shape = (rows, tp_count, scale)
    mixed_low, mixed_t, lse = attention_forward(place, tiles, span, own, even, odd, *shape)

    back = [mixed_low[:rows]]
    for s in range(1, heads):
        back.append(ctx_xor(mixed_low[s * rows : (s + 1) * rows], s << 1))
    back = jnp.concatenate(back, axis=0)
    attn_vals = jnp.concatenate(
        [lax.dynamic_slice_in_dim(back, jnp.bitwise_xor(my_head, h) * rows, rows, 0) for h in range(heads)],
        axis=1,
    )
    attn = lax.dot_general(attn_vals, out_full, (((1,), (1,)), ((), ())), preferred_element_type=f32)
    x_own = x_slots[:part_rows].astype(f32)
    y1 = x_own + tp_scatter(attn.astype(bf16))
    normed2, rstd2 = norm_parts(y1)
    a2_own = (normed2 * gain_two + bias_two).astype(bf16)
    grad_act = jnp.dot(c_slots, down_full, preferred_element_type=f32)
    a2, grad_act = lax.optimization_barrier((tp_gather(a2_own), grad_act))
    a2 = jnp.concatenate(a2, axis=0)

    up = jnp.dot(a2, up_full, preferred_element_type=f32)
    cdf = 0.5 * (1.0 + lax.erf(up * inv_root_two))
    act = (up * cdf).astype(bf16)
    slope = cdf + up * jnp.exp(-0.5 * up * up) * inv_root_two_pi
    grad_up_in = (grad_act * slope).astype(bf16)
    grad_h2 = lax.dot_general(grad_up_in, up_full, (((1,), (1,)), ((), ())), preferred_element_type=f32).astype(bf16)
    grad_h2, act, grad_up_in = lax.optimization_barrier((grad_h2, act, grad_up_in))
    pair_grad = pair_grad_of(a2, grad_up_in, c_slots, act)
    pair_shard = lax.psum_scatter(pair_grad, "ctx", scatter_dimension=1, tiled=True)
    grad_h2 = tp_total(tp_send(grad_h2, pair_grad))

    dx2, dg2, dc2 = norm_back(grad_h2, normed2, rstd2, gain_two)
    c_own = c_slots[:part_rows].astype(f32)
    grad_y1 = c_own + dx2
    grad_attn = jnp.concatenate(tp_gather(grad_y1.astype(bf16)), axis=0)
    mixed = lax.dot_general(act, down_full, (((1,), (1,)), ((), ())), preferred_element_type=f32).astype(bf16)
    mixed, grad_attn = lax.optimization_barrier((mixed, grad_attn))
    block_out = (y1 + tp_scatter(mixed)).astype(bf16)

    grad_outw = lax.dot_general(grad_attn, attn_vals, (((0,), (0,)), ((), ())), preferred_element_type=f32)
    grad_outw = grad_outw.astype(bf16)
    grad_vals = jnp.dot(grad_attn, out_full, preferred_element_type=f32).astype(bf16)

    grads = []
    for s in range(heads):
        piece = lax.dynamic_slice_in_dim(grad_vals, jnp.bitwise_xor(my_head, s) * HEAD, HEAD, 1)
        grads.append(piece if s == 0 else ctx_xor(piece, s << 1))
    grads = jnp.concatenate(grads, axis=0)
    results = attention_backward(place, tiles, span, own, grads, mixed_t, lse, even, odd, *shape)
    grad_q, grad_kv, grad_odd = results
    got = ctx_xor(grad_odd, 1)
    for bit in reversed(far_bits):
        grad_kv = grad_kv + got.astype(f32)
        half = grad_kv.shape[0] // 2
        got = ctx_xor(grad_kv[half:].astype(bf16), 1 << bit)
        grad_kv = grad_kv[:half]
    got, block_out = lax.optimization_barrier((got, block_out))
    grad_own = merge(grad_q, grad_kv, got, heads)
    back = [grad_own[0]]
    for s in range(1, heads):
        back.append(ctx_xor(grad_own[s], s << 1))
    back = jnp.concatenate(back, axis=0)
    back, grad_outw = lax.optimization_barrier((back, grad_outw))
    by_head = [
        lax.dynamic_slice_in_dim(back, jnp.bitwise_xor(my_head, h) * rows, rows, 0) for h in range(heads)
    ]
    grad_qkv_in = jnp.concatenate(
        [by_head[h][:, j * HEAD : (j + 1) * HEAD] for j in range(3) for h in range(heads)], axis=1
    )
    chips = list(range(0, ctx_count, 2))
    sent = weight_grad(place, a1, grad_qkv_in, ctx_cols)
    sent, later, block_out = lax.optimization_barrier((sent, grad_qkv_in, tp_gather_first(block_out)))
    got = ctx_xor(sent, 1)
    grad_outw, pair_shard = lax.optimization_barrier((grad_outw, pair_shard))
    out_shard = lax.psum_scatter(grad_outw, "ctx", scatter_dimension=0, tiled=True)
    grad_h1 = input_grad(place, later, qkv_blocks, ctx_cols)
    block_out, grad_h1 = lax.optimization_barrier((tp_gather_last(block_out), grad_h1))
    summed = weight_grad(place, a1, grad_qkv_in, ctx_cols, got)
    grad_h1 = tp_send(grad_h1, summed)
    up_grad, down_grad, square = widen(pair_shard)
    arrived = [ctx_xor(summed[slot], mask) for slot, mask in enumerate(chips) if slot]
    grad_h1, _, up_grad, out_shard = lax.optimization_barrier((grad_h1, summed, up_grad, out_shard))
    grad_h1 = tp_total(grad_h1)
    block_out = slots_to_rows(block_out, tp_place)
    normed1, rstd1 = norm_parts(x_own)
    dx1, dg1, dc1 = norm_back(grad_h1, normed1, rstd1, gain_one)
    grad_tokens = (grad_y1 + dx1).astype(bf16)
    qkv_grad, out_grad, more = total_of([summed[0], *arrived], out_shard, head_cols)
    square = square[0, 0] + more[0, 0]
    lines = jnp.stack((dg1, dg2, dc1, dc2)).reshape(-1, HEAD)
    sent = jnp.concatenate((lines, jnp.full((8, HEAD), square, f32)), axis=0)
    sent, grad_tokens = lax.optimization_barrier((sent, tp_gather_first(grad_tokens)))
    total, grad_tokens = sum_over_all(sent, grad_tokens)
    grad_tokens = tp_gather_last(grad_tokens)
    small_grad = total[:-8].reshape(4, width)
    total_sq = total[-1, 0] + jnp.sum(small_grad * small_grad)
    grad_norm = jnp.sqrt(total_sq)
    factor = 1.0 / jnp.maximum(grad_norm, 1.0)
    small_own = lax.dynamic_slice_in_dim(small_grad, ctx_place * ctx_cols, ctx_cols, 1)

    flags = decay_mask.astype(f32)
    flat = lambda value: value.reshape(-1, head_cols)
    matrices = adam(
        factor,
        flags,
        (
            (flat(w_qkv), flat(qkv_grad), flat(m_qkv), flat(v_qkv)),
            (w_out, out_grad, m_out, v_out),
            (w_up, up_grad, m_up, v_up),
            (w_down, down_grad, m_down, v_down),
        ),
    )
    matrices[0] = [value.reshape(w_qkv.shape) for value in matrices[0]]
    gains_new = adam_update(norm_gains, small_own[:2], m_gains, v_gains, factor, flags[4])
    biases_new = adam_update(norm_biases, small_own[2:], m_biases, v_biases, factor, flags[5])
    grad_tokens = slots_to_rows(grad_tokens, tp_place)
    shards = (qkv_grad, out_grad, up_grad, down_grad, small_own[:2], small_own[2:])
    updates = list(zip(*matrices, gains_new, biases_new))
    return (block_out, grad_tokens, grad_norm, *shards, *updates[0], *updates[1], *updates[2])


def solution(mesh):
    small = P(None, "ctx")
    weights = (P(None, "ctx", "tp"), P("tp", "ctx"), P("ctx", "tp"), P("tp", "ctx"), small, small)
    rows = (P("ctx", None), P("ctx", None))
    return jax.shard_map(
        per_device,
        mesh=mesh,
        in_specs=(*rows, *weights, *weights, *weights, P(), P()),
        out_specs=(*rows, P(), *weights, *weights, *weights, *weights),
        check_vma=False,
    )
```

```python
import functools
import math

import jax
import jax.numpy as jnp
from jax import lax
from jax.experimental import pallas as pl
from jax.experimental.pallas import tpu as pltpu
from jax.sharding import PartitionSpec as P

HEAD = 128
BLOCK = 256
Q_TILE = 512

eps_norm = 1e-05
neg_big = -1e30
beta_one = 0.9
beta_two = 0.95
adam_eps = 1e-08
learn_rate = 0.001
decay_rate = 0.1
step_count = 10.0
log2_e = math.log2(math.e)
inv_root_two = 1.0 / math.sqrt(2.0)
inv_root_two_pi = 1.0 / math.sqrt(2.0 * math.pi)
bf16 = jnp.bfloat16
f32 = jnp.float32


def ctx_xor(value, mask):
    count = lax.axis_size("ctx")
    return lax.ppermute(value, "ctx", [(place, place ^ mask) for place in range(count)])


def ctx_gather(own, early):
    blocks = [None] * lax.axis_size("ctx")
    for mask in range(0, len(blocks), 2):
        blocks[mask] = own if mask == 0 else ctx_xor(own, mask)
    blocks[2], early = lax.optimization_barrier((blocks[2], early))
    for mask in range(0, len(blocks), 2):
        blocks[mask + 1] = ctx_xor(blocks[mask], 1)
    return (blocks, early)


def tp_xor(value, mask):
    count = lax.axis_size("tp")
    return lax.ppermute(value, "tp", [(place, place ^ mask) for place in range(count)])


def tp_gather(own):
    return tp_gather_last(tp_gather_first(own))


def tp_gather_first(own):
    count = lax.axis_size("tp")
    return [own] + [tp_xor(own, s) for s in range(1, 3 if count == 4 else count)]


def tp_gather_last(parts):
    return parts + [tp_xor(parts[2], 1)] if lax.axis_size("tp") == 4 else parts


def tp_send(partial, behind=None):
    count = lax.axis_size("tp")
    rows = partial.shape[0] // count
    pieces = [partial[s * rows : (s + 1) * rows] for s in range(count)]
    if count != 4:
        return [pieces[0]] + [tp_xor(pieces[s], s) for s in range(1, count)]
    passed = tp_xor(pieces[3], 1)
    passed, near, _ = lax.optimization_barrier((passed, pieces[1], behind))
    joined = (pieces[2].astype(f32) + passed.astype(f32)).astype(bf16)
    return [pieces[0], tp_xor(near, 1), tp_xor(joined, 2)]


def tp_total(parts):
    total = parts[0].astype(f32)
    for piece in parts[1:]:
        total = total + piece.astype(f32)
    return total


def tp_scatter(partial):
    return tp_total(tp_send(partial))


def slots_to_rows(parts, tp_place):
    return in_slots(jnp.concatenate(parts, axis=0), tp_place, len(parts))


def in_slots(value, tp_place, count):
    rows = value.shape[0] // count
    order = [jnp.bitwise_xor(tp_place, s) * rows for s in range(count)]
    return jnp.concatenate([lax.dynamic_slice_in_dim(value, o, rows, 0) for o in order], axis=0)


def sum_over_all(value, later):
    if lax.axis_size("tp") == 4:
        one, two, three = (tp_xor(value, 1), tp_xor(value, 2), tp_xor(value, 3))
        value = (value + one) + (two + three)
    else:
        mask = 1
        while mask < lax.axis_size("tp"):
            value = value + tp_xor(value, mask)
            mask *= 2
    value, later = lax.optimization_barrier((value, later))
    mask = lax.axis_size("ctx") // 2
    while mask:
        value = value + ctx_xor(value, mask)
        mask //= 2
    return (value, later)


def scores_of(keys, query, where, lo, hi, scale):
    raw = lax.dot_general(keys, query, (((1,), (1,)), ((), ())), preferred_element_type=f32) * (scale * log2_e)
    return jnp.where((where >= lo) & (where < hi), raw, neg_big)


def key_halves(rows, place, chip):
    top = pl.multiple_of(jnp.bitwise_xor(chip, place[0] // 2) * rows, rows)
    core = lax.rem(place[0], 2)
    return (top, (2 * chip + core) * rows, (2 * chip + 1 - core) * rows)


def fill_positions(rows, chunks, place, where):
    where[...] = jnp.bitwise_xor(lax.broadcasted_iota(jnp.int32, where.shape, 0), place[1] * (rows // chunks))


def forward_kernel(rows, chunks, left, scale, place, tiles, span, own, *refs):
    even = own if left else refs[0]
    odd, out, out_t, lse_out, vt_even, vt_odd, where = refs[-7:]
    fill_positions(rows, chunks, place, where)
    for slot in range(odd.shape[0] // rows):
        cut = slice(slot * rows, (slot + 1) * rows)
        vt_even[:, cut] = even[cut, left + HEAD : left + 2 * HEAD].T
        vt_odd[:, cut] = odd[cut, HEAD:].T

    @pl.loop(0, own.shape[0] // Q_TILE)
    def _(tile):
        cut = pl.ds(pl.multiple_of(tile * Q_TILE, Q_TILE), Q_TILE)
        query = own[cut, :HEAD]
        lo, hi = span[0:1, cut], span[1:2, cut]

        def step(chip, carry):
            top, total, acc = carry
            at, first, second = key_halves(rows, place, chip)
            here = pl.ds(at, rows)
            one = scores_of(even[here, left : left + HEAD], query, where[...], lo - first, hi - first, scale)
            two = scores_of(odd[here, :HEAD], query, where[...], lo - second, hi - second, scale)
            new_top = jnp.maximum(
                top, jnp.maximum(jnp.max(one, axis=0, keepdims=True), jnp.max(two, axis=0, keepdims=True))
            )
            fade = jnp.exp2(top - new_top)
            one, two = jnp.exp2(one - new_top), jnp.exp2(two - new_top)
            total = total * fade + jnp.sum(one, axis=0, keepdims=True) + jnp.sum(two, axis=0, keepdims=True)
            acc = (
                acc * fade
                + jnp.dot(vt_even[:, here], one.astype(bf16), preferred_element_type=f32)
                + jnp.dot(vt_odd[:, here], two.astype(bf16), preferred_element_type=f32)
            )
            return (new_top, total, acc)

        start = (
            jnp.full((1, Q_TILE), neg_big, f32),
            jnp.zeros((1, Q_TILE), f32),
            jnp.zeros((HEAD, Q_TILE), f32),
        )
        top, total, acc = lax.fori_loop(tiles[0, tile], tiles[1, tile], step, start)
        result = acc / total
        out_t[:, cut] = result
        out[cut, :] = result.T.astype(bf16)
        lse_out[:, cut] = top + jnp.log2(total)


def backward_kernel(rows, chunks, left, scale, place, tiles, span, own, grad_out, out_t, lse_in, *refs):
    even = own if left else refs[0]
    odd, dq_out, dkv_even, dkv_odd, kt_even, kt_odd, d_odd, where = refs[-8:]
    fill_positions(rows, chunks, place, where)
    for slot in range(odd.shape[0] // rows):
        cut = slice(slot * rows, (slot + 1) * rows)
        kt_even[:, cut] = even[cut, left : left + HEAD].T
        kt_odd[:, cut] = odd[cut, :HEAD].T
    dkv_even[...] = jnp.zeros_like(dkv_even)
    d_odd[...] = jnp.zeros_like(d_odd)

    @pl.loop(0, own.shape[0] // Q_TILE)
    def _(tile):
        cut = pl.ds(pl.multiple_of(tile * Q_TILE, Q_TILE), Q_TILE)
        query, grad = own[cut, :HEAD], grad_out[cut, :]
        lo, hi, lse = span[0:1, cut], span[1:2, cut], lse_in[:, cut]
        inner = jnp.sum(grad.astype(f32).T * out_t[:, cut], axis=0, keepdims=True)

        def half(keys, values, keys_t, total, here, first, dq_t):
            scores = scores_of(keys, query, where[...], lo - first, hi - first, scale)
            prob = jnp.exp2(scores - lse)
            grad_prob = lax.dot_general(
                values, grad, (((1,), (1,)), ((), ())), preferred_element_type=f32
            )
            grad_scores = (prob * (grad_prob - inner)).astype(bf16)
            total[here, HEAD:] += jnp.dot(prob.astype(bf16), grad, preferred_element_type=f32)
            total[here, :HEAD] += jnp.dot(grad_scores, query, preferred_element_type=f32)
            return dq_t + jnp.dot(keys_t, grad_scores, preferred_element_type=f32)

        def step(chip, dq_t):
            at, first, second = key_halves(rows, place, chip)
            here = pl.ds(at, rows)
            keys, values = even[here, left : left + HEAD], even[here, left + HEAD : left + 2 * HEAD]
            dq_t = half(keys, values, kt_even[:, here], dkv_even, here, first, dq_t)
            return half(odd[here, :HEAD], odd[here, HEAD:], kt_odd[:, here], d_odd, here, second, dq_t)

        dq_t = lax.fori_loop(
            tiles[0, tile], tiles[1, tile], step, jnp.zeros((HEAD, Q_TILE), f32)
        )
        dq_out[cut, :] = (dq_t * scale).T.astype(bf16)

    dkv_even[:, :HEAD] = dkv_even[:, :HEAD] * scale
    dkv_odd[:, :HEAD] = (d_odd[:, :HEAD] * scale).astype(bf16)
    dkv_odd[:, HEAD:] = d_odd[:, HEAD:].astype(bf16)


LARGE = pl.CostEstimate(flops=180_000_000_000, bytes_accessed=180_000_000, transcendentals=0)
LITTLE = pl.CostEstimate(flops=1, bytes_accessed=1, transcendentals=0)


def in_vmem():
    return pl.BlockSpec(memory_space=pltpu.VMEM)


def in_smem():
    return pl.BlockSpec(memory_space=pltpu.SMEM)


def attention_forward(place, tiles, span, own, even, odd, rows, chunks, scale):
    queries, keys = own.shape[0], odd.shape[0]
    arrays = (own, odd) if even is None else (own, even, odd)
    return pl.pallas_call(
        functools.partial(forward_kernel, rows, chunks, HEAD if even is None else 0, scale),
        out_shape=(
            jax.ShapeDtypeStruct((queries, HEAD), bf16),
            jax.ShapeDtypeStruct((HEAD, queries), f32),
            jax.ShapeDtypeStruct((1, queries), f32),
        ),
        in_specs=[in_smem(), in_smem()] + [in_vmem()] * (1 + len(arrays)),
        out_specs=(in_vmem(), in_vmem(), in_vmem()),
        scratch_shapes=[
            pltpu.VMEM((HEAD, keys), bf16),
            pltpu.VMEM((HEAD, keys), bf16),
            pltpu.VMEM((rows, Q_TILE), jnp.int32),
        ],
        compiler_params=pltpu.CompilerParams(vmem_limit_bytes=58 << 20),
        cost_estimate=LITTLE,
        name="attention_forward",
    )(place, tiles, span, *arrays)


def attention_backward(place, tiles, span, own, grad, out_t, lse, even, odd, rows, chunks, scale):
    queries, keys = own.shape[0], odd.shape[0]
    arrays = (odd,) if even is None else (even, odd)
    return pl.pallas_call(
        functools.partial(backward_kernel, rows, chunks, HEAD if even is None else 0, scale),
        out_shape=(
            jax.ShapeDtypeStruct((queries, HEAD), bf16),
            jax.ShapeDtypeStruct((keys, 2 * HEAD), f32),
            jax.ShapeDtypeStruct((keys, 2 * HEAD), bf16),
        ),
        in_specs=[in_smem(), in_smem()] + [in_vmem()] * (5 + len(arrays)),
        out_specs=(in_vmem(),) * 3,
        scratch_shapes=[
            pltpu.VMEM((HEAD, keys), bf16),
            pltpu.VMEM((HEAD, keys), bf16),
            pltpu.VMEM((keys, 2 * HEAD), f32),
            pltpu.VMEM((rows, Q_TILE), jnp.int32),
        ],
        compiler_params=pltpu.CompilerParams(vmem_limit_bytes=58 << 20),
        cost_estimate=LITTLE,
        name="attention_backward",
    )(place, tiles, span, own, grad, out_t, lse, *arrays)


def merge_kernel(grad_q, grad_kv, *refs):
    got, outs = refs[0], refs[1:]
    rows = outs[0].shape[0]
    for slot, out in enumerate(outs):
        cut = slice(slot * rows, (slot + 1) * rows)
        out[:, :HEAD] = grad_q[cut, :]
        out[:, HEAD:] = (grad_kv[cut, :] + got[cut, :].astype(f32)).astype(bf16)


def merge(grad_q, grad_kv, got, count):
    rows = grad_q.shape[0] // count
    return pl.pallas_call(
        merge_kernel,
        out_shape=(jax.ShapeDtypeStruct((rows, 3 * HEAD), bf16),) * count,
        in_specs=[in_vmem()] * 3,
        out_specs=(in_vmem(),) * count,
        compiler_params=pltpu.CompilerParams(vmem_limit_bytes=58 << 20),
        cost_estimate=LARGE,
        name="merge",
    )(grad_q, grad_kv, got)


def lanes_of(me, mask, depth):
    at = jnp.bitwise_xor(me, mask) * depth
    return pl.ds(pl.multiple_of(at, depth), depth)


def project_kernel(rows, heads, depth, place, rows_in, *refs):
    blocks, outs, (a1, small, weights, result) = refs[: -4 - heads], refs[-4 - heads : -4], refs[-4:]
    me = place[0]
    my_head = lax.rem(me // 2, heads)
    if depth % HEAD:
        small[...] = blocks[-1][...]
        blocks = blocks[:-1]
    for mask, block in enumerate(blocks):
        at = lanes_of(me, mask, depth)
        weights[at, :] = block[:depth, :]
        if depth % HEAD == 0:
            small[:, at] = block[depth : depth + 8, :depth].astype(f32)
    part = rows // 4

    for quarter in range(4):
        cut = slice(quarter * part, (quarter + 1) * part)
        normed, _ = norm_parts(rows_in[cut, :].astype(f32))
        a1[cut, :] = (normed * small[0:1, :] + small[2:3, :]).astype(bf16)

    width = heads * HEAD

    for j in range(3):
        cut = slice(j * width, (j + 1) * width)
        result[:, cut] = jnp.dot(a1[...], weights[:, cut], preferred_element_type=f32).astype(bf16)

    for s in range(heads):
        at = jnp.bitwise_xor(my_head, s) * HEAD
        for j in range(3):
            here = pl.ds(pl.multiple_of(j * width + at, HEAD), HEAD)
            outs[s][:, j * HEAD : (j + 1) * HEAD] = result[:, here]


def project(place, rows_in, blocks, heads, depth):
    rows, width = rows_in.shape
    cols = 3 * heads * HEAD
    if depth % HEAD:
        known = jnp.stack([block[depth : depth + 8, :depth] for block in blocks])
        order = jnp.bitwise_xor(place[0], jnp.arange(len(blocks), dtype=jnp.int32))
        known = jnp.take(known, order, axis=0).transpose(1, 0, 2).reshape(8, width)
        blocks = [*blocks, known.astype(f32)]
    return pl.pallas_call(
        functools.partial(project_kernel, rows, heads, depth),
        out_shape=(
            *[jax.ShapeDtypeStruct((rows, 3 * HEAD), bf16)] * heads,
            jax.ShapeDtypeStruct((rows, width), bf16),
            jax.ShapeDtypeStruct((8, width), f32),
        ),
        in_specs=[in_smem()] + [in_vmem()] * (1 + len(blocks)),
        out_specs=(in_vmem(),) * (heads + 2),
        scratch_shapes=[pltpu.VMEM((width, cols), bf16), pltpu.VMEM((rows, cols), bf16)],
        compiler_params=pltpu.CompilerParams(vmem_limit_bytes=58 << 20),
        cost_estimate=LITTLE,
        name="project",
    )(place, rows_in, *blocks)


def weight_grad_kernel(flip, depth, place, rows_in, grads, *refs):
    me = place[0]
    count = rows_in.shape[1] // depth // 2
    outs = refs[:1] if flip else refs[1 : 1 + count]
    if depth % HEAD:
        whole = refs[-1]
        whole[...] = lax.dot_general(rows_in[...], grads[...], (((0,), (0,)), ((), ())), preferred_element_type=f32)
    for slot in range(count):
        at, here = lanes_of(me, 2 * slot + flip, depth), slice(slot * depth, (slot + 1) * depth)
        if depth % HEAD:
            block = whole[at, :]
        else:
            block = lax.dot_general(
                rows_in[:, at], grads[...], (((0,), (0,)), ((), ())), preferred_element_type=f32
            )
        if flip:
            outs[0][here, :] = block.astype(bf16)
        else:
            outs[slot][...] = (block + refs[0][here, :].astype(f32)).astype(bf16)


def weight_grad(place, rows_in, grads, depth, add=None):
    width, cols = rows_in.shape[1], grads.shape[1]
    count = width // depth // 2
    flip, extra = (1, []) if add is None else (0, [add])
    lines = [count * depth] if add is None else [depth] * count
    results = pl.pallas_call(
        functools.partial(weight_grad_kernel, flip, depth),
        out_shape=tuple(jax.ShapeDtypeStruct((n, cols), bf16) for n in lines),
        in_specs=[in_smem()] + [in_vmem()] * (2 + len(extra)),
        out_specs=(in_vmem(),) * len(lines),
        scratch_shapes=[pltpu.VMEM((width, cols), f32)] if depth % HEAD else [],
        compiler_params=pltpu.CompilerParams(vmem_limit_bytes=58 << 20),
        cost_estimate=LITTLE,
        name="weight_grad",
    )(place, rows_in, grads, *extra)
    return results if add is not None else results[0]


def input_grad_kernel(depth, place, grads, *refs):
    me = place[0]
    blocks, out, weights = refs[:-2], refs[-2], refs[-1]
    for mask, block in enumerate(blocks):
        weights[lanes_of(me, mask, depth), :] = block[:depth, :]
    step = 512

    @pl.loop(0, out.shape[1] // step)
    def _(part):
        here = pl.ds(pl.multiple_of(part * step, step), step)
        out[:, here] = lax.dot_general(
            grads[...], weights[here, :], (((1,), (1,)), ((), ())), preferred_element_type=f32
        ).astype(bf16)


def input_grad(place, grads, blocks, depth):
    return pl.pallas_call(
        functools.partial(input_grad_kernel, depth),
        out_shape=jax.ShapeDtypeStruct((grads.shape[0], depth * len(blocks)), bf16),
        in_specs=[in_smem()] + [in_vmem()] * (1 + len(blocks)),
        out_specs=in_vmem(),
        scratch_shapes=[pltpu.VMEM((depth * len(blocks), grads.shape[1]), bf16)],
        compiler_params=pltpu.CompilerParams(vmem_limit_bytes=58 << 20),
        cost_estimate=LARGE,
        name="input_grad",
    )(place, grads, *blocks)


def pair_grad_kernel(half, left, right, other_left, other_right, out):
    def block(rows_in, grads):
        out[0] = lax.dot_general(
            rows_in[...], grads[...], (((0,), (0,)), ((), ())), preferred_element_type=f32
        ).astype(bf16)

    pl.when(pl.program_id(0) < half)(lambda: block(left, right))
    pl.when(pl.program_id(0) >= half)(lambda: block(other_left, other_right))


def pair_grad_of(left, right, other_left, other_right):
    rows, width = left.shape
    cols = right.shape[1]
    step, half = 512, width // 512
    first = pl.BlockSpec((rows, step), lambda i: (0, jnp.minimum(i, half - 1)))
    second = pl.BlockSpec((rows, step), lambda i: (0, jnp.maximum(i - half, 0)))
    return pl.pallas_call(
        functools.partial(pair_grad_kernel, half),
        grid=(2 * half,),
        out_shape=jax.ShapeDtypeStruct((2, width, cols), bf16),
        in_specs=[first, in_vmem(), second, in_vmem()],
        out_specs=pl.BlockSpec((1, step, cols), lambda i: (i // half, i % half, 0)),
        compiler_params=pltpu.CompilerParams(vmem_limit_bytes=58 << 20),
        cost_estimate=LITTLE,
        name="pair_grad",
    )(left, right, other_left, other_right)


def widen_kernel(pair, up, down, square):
    part = jnp.zeros((1, 1), f32)
    for source, target, turn in ((pair.at[0], up, False), (pair.at[1], down, True)):
        value = source[...].astype(f32)
        part = part + jnp.sum(jnp.sum(value * value, axis=0, keepdims=True), axis=1, keepdims=True)
        target[...] = value.T if turn else value
    square[...] = jnp.broadcast_to(part, square.shape)


def widen(pair):
    _, cols, units = pair.shape
    shapes = ((cols, units), (units, cols), (8, HEAD))
    return pl.pallas_call(
        widen_kernel,
        out_shape=tuple(jax.ShapeDtypeStruct(s, f32) for s in shapes),
        in_specs=[in_vmem()],
        out_specs=(in_vmem(),) * 3,
        compiler_params=pltpu.CompilerParams(vmem_limit_bytes=58 << 20),
        cost_estimate=LITTLE,
        name="widen",
    )(pair)


def total_kernel(head_cols, out_t, *refs):
    pieces, (qkv, out, square) = refs[:-3], refs[-3:]
    value = out_t[...].astype(f32)
    out[...] = value.T
    part = jnp.sum(jnp.sum(value * value, axis=0, keepdims=True), axis=1, keepdims=True)
    for j in range(3):
        cut = slice(j * head_cols, (j + 1) * head_cols)
        value = pieces[0][:, cut].astype(f32)
        for piece in pieces[1:]:
            value = value + piece[:, cut].astype(f32)
        part = part + jnp.sum(jnp.sum(value * value, axis=0, keepdims=True), axis=1, keepdims=True)
        qkv[j] = value
    square[...] = jnp.broadcast_to(part, square.shape)


def total_of(pieces, out_t, head_cols):
    depth = pieces[0].shape[0]
    shapes = ((3, depth, head_cols), (head_cols, depth), (8, HEAD))
    return pl.pallas_call(
        functools.partial(total_kernel, head_cols),
        out_shape=tuple(jax.ShapeDtypeStruct(s, f32) for s in shapes),
        in_specs=[in_vmem()] * (1 + len(pieces)),
        out_specs=(in_vmem(),) * 3,
        compiler_params=pltpu.CompilerParams(vmem_limit_bytes=58 << 20),
        cost_estimate=LITTLE,
        name="total",
    )(out_t, *pieces)


ADAM_STEPS = 4


def adam_kernel(count, factor, decays, *refs):
    ins, outs = refs[: 4 * count], refs[4 * count :]
    for index in range(count):
        master, grad, first, second = (r[...] for r in ins[4 * index : 4 * index + 4])
        results = adam_update(master, grad, first, second, factor[0], decays[index])
        for target, value in zip(outs[3 * index : 3 * index + 3], results):
            target[...] = value


def adam(factor, decays, groups):
    specs, shapes, flat = ([], [], [])
    for group in groups:
        lines, cols = group[0].shape
        spec = pl.BlockSpec((lines // ADAM_STEPS, cols), lambda step: (step, 0))
        flat.extend(group)
        specs.extend([spec] * 3)
        shapes.extend([jax.ShapeDtypeStruct((lines, cols), f32)] * 3)
    in_specs = [s for spec in specs[::3] for s in [spec] * 4]
    results = pl.pallas_call(
        functools.partial(adam_kernel, len(groups)),
        grid=(ADAM_STEPS,),
        out_shape=tuple(shapes),
        in_specs=[in_smem(), in_smem()] + in_specs,
        out_specs=tuple(specs),
        compiler_params=pltpu.CompilerParams(vmem_limit_bytes=58 << 20),
        cost_estimate=LITTLE,
        name="adam",
    )(factor.reshape(1), decays, *flat)
    return [results[3 * i : 3 * i + 3] for i in range(len(groups))]


def norm_parts(rows):
    mean = jnp.mean(rows, axis=1, keepdims=True)
    centred = rows - mean
    rstd = lax.rsqrt(jnp.mean(centred * centred, axis=1, keepdims=True) + eps_norm)
    return (centred * rstd, rstd)


def norm_back(grad_out, normed, rstd, gain):
    scaled = grad_out * gain
    inner = (
        scaled
        - jnp.mean(scaled, axis=1, keepdims=True)
        - normed * jnp.mean(scaled * normed, axis=1, keepdims=True)
    )
    return (inner * rstd, jnp.sum(grad_out * normed, axis=0), jnp.sum(grad_out, axis=0))


def adam_update(master, grad, first, second, factor, decays):
    clipped = grad * factor
    first_new = beta_one * first + (1.0 - beta_one) * clipped
    second_new = beta_two * second + (1.0 - beta_two) * clipped * clipped
    fix_one = 1.0 - beta_one**step_count
    fix_two = 1.0 - beta_two**step_count
    update = first_new / fix_one / (jnp.sqrt(second_new / fix_two) + adam_eps)
    amount = learn_rate * (update + decay_rate * decays * master)
    return (amount, first_new, second_new)


def key_span(positions, seq_lengths):
    ends = jnp.cumsum(seq_lengths)
    starts = ends - seq_lengths
    inside = (positions[:, None] >= starts[None, :]) & (positions[:, None] < ends[None, :])
    begin = jnp.sum(jnp.where(inside, starts[None, :], 0), axis=1)
    end = jnp.sum(jnp.where(inside, ends[None, :], 0), axis=1)
    block = (positions - begin) // BLOCK
    return (begin, jnp.minimum(begin + (block + 1) * BLOCK, end))


def per_device(
    tokens,
    cotangent,
    w_qkv,
    w_out,
    w_up,
    w_down,
    norm_gains,
    norm_biases,
    m_qkv,
    m_out,
    m_up,
    m_down,
    m_gains,
    m_biases,
    v_qkv,
    v_out,
    v_up,
    v_down,
    v_gains,
    v_biases,
    seq_lengths,
    decay_mask,
):
    rows, width = tokens.shape
    ctx_count, tp_count = lax.axis_size("ctx"), lax.axis_size("tp")
    ctx_place = lax.axis_index("ctx").astype(jnp.int32)
    tp_place = lax.axis_index("tp").astype(jnp.int32)
    total_rows = rows * ctx_count
    part_rows = rows // tp_count
    head_cols = w_out.shape[0]
    heads = head_cols // HEAD
    units = w_up.shape[1]
    ctx_cols = w_out.shape[1]
    scale = HEAD ** (-0.5)
    my_head = lax.rem(ctx_place // 2, heads)

    place = jnp.stack((ctx_place, tp_place))

    small = jnp.concatenate((norm_gains, norm_biases), axis=0)
    small = jnp.pad(small, ((0, 12), (0, 3 * head_cols - ctx_cols)))
    qkv_pack = jnp.concatenate((w_qkv[0], w_qkv[1], w_qkv[2]), axis=1)
    qkv_pack = jnp.concatenate((qkv_pack, small), axis=0).astype(bf16)
    out_pack = w_out.T.astype(bf16)
    rest_pack = jnp.concatenate((w_up, w_down.T), axis=1).astype(bf16)

    x_slots = in_slots(tokens, tp_place, tp_count)
    c_slots = in_slots(cotangent, tp_place, tp_count)
    qkv_blocks, early = ctx_gather(qkv_pack, (out_pack, rest_pack, x_slots))
    out_pack, rest_pack, x_slots = early
    out_pack, _ = lax.optimization_barrier((out_pack, qkv_blocks[2::2]))
    out_full = lax.all_gather(out_pack, "ctx", axis=0, tiled=True)

    group = [s << 1 for s in range(heads)]
    far_bits = list(range(heads.bit_length(), ctx_count.bit_length() - 1))
    inner_rows = jnp.arange(part_rows, dtype=jnp.int32)
    positions = jnp.concatenate(
        [
            jnp.bitwise_xor(ctx_place, m) * rows + jnp.bitwise_xor(tp_place, s) * part_rows + inner_rows
            for m in group
            for s in range(tp_count)
        ]
    )
    lo, hi = key_span(positions, seq_lengths)
    span = jnp.stack((lo, hi))
    tiles = jnp.stack(
        (
            jnp.min(lo.reshape(-1, Q_TILE), axis=1) // (2 * rows),
            (jnp.max(hi.reshape(-1, Q_TILE), axis=1) + 2 * rows - 1) // (2 * rows),
        )
    )
    *pieces, a1, small = project(place, x_slots, qkv_blocks, heads, ctx_cols)
    gain_one, gain_two, bias_two = small[0], small[1], small[3]
    own_parts = [pieces[0]] + [ctx_xor(pieces[s], s << 1) for s in range(1, heads)]
    _, rest_pack = lax.optimization_barrier((pieces, rest_pack))
    rest_full = lax.all_gather(rest_pack, "ctx", axis=0, tiled=True)
    up_full, down_full = rest_full[:, :units], rest_full[:, units:]
    own = jnp.concatenate(own_parts, axis=0)
    even = own[:, HEAD:]
    for bit in far_bits:
        even = jnp.concatenate((even, ctx_xor(even, 1 << bit)), axis=0)
    odd = ctx_xor(even, 1)
    even = even if far_bits else None
    shape = (rows, tp_count, scale)
    mixed_low, mixed_t, lse = attention_forward(place, tiles, span, own, even, odd, *shape)

    back = [mixed_low[:rows]]
    for s in range(1, heads):
        back.append(ctx_xor(mixed_low[s * rows : (s + 1) * rows], s << 1))
    back = jnp.concatenate(back, axis=0)
    attn_vals = jnp.concatenate(
        [lax.dynamic_slice_in_dim(back, jnp.bitwise_xor(my_head, h) * rows, rows, 0) for h in range(heads)],
        axis=1,
    )
    attn = lax.dot_general(attn_vals, out_full, (((1,), (1,)), ((), ())), preferred_element_type=f32)
    x_own = x_slots[:part_rows].astype(f32)
    y1 = x_own + tp_scatter(attn.astype(bf16))
    normed2, rstd2 = norm_parts(y1)
    a2_own = (normed2 * gain_two + bias_two).astype(bf16)
    grad_act = jnp.dot(c_slots, down_full, preferred_element_type=f32)
    a2, grad_act = lax.optimization_barrier((tp_gather(a2_own), grad_act))
    a2 = jnp.concatenate(a2, axis=0)

    up = jnp.dot(a2, up_full, preferred_element_type=f32)
    cdf = 0.5 * (1.0 + lax.erf(up * inv_root_two))
    act = (up * cdf).astype(bf16)
    slope = cdf + up * jnp.exp(-0.5 * up * up) * inv_root_two_pi
    grad_up_in = (grad_act * slope).astype(bf16)
    grad_h2 = lax.dot_general(grad_up_in, up_full, (((1,), (1,)), ((), ())), preferred_element_type=f32).astype(bf16)
    grad_h2, act, grad_up_in = lax.optimization_barrier((grad_h2, act, grad_up_in))
    pair_grad = pair_grad_of(a2, grad_up_in, c_slots, act)
    pair_shard = lax.psum_scatter(pair_grad, "ctx", scatter_dimension=1, tiled=True)
    grad_h2 = tp_total(tp_send(grad_h2, pair_grad))

    dx2, dg2, dc2 = norm_back(grad_h2, normed2, rstd2, gain_two)
    c_own = c_slots[:part_rows].astype(f32)
    grad_y1 = c_own + dx2
    grad_attn = jnp.concatenate(tp_gather(grad_y1.astype(bf16)), axis=0)
    mixed = lax.dot_general(act, down_full, (((1,), (1,)), ((), ())), preferred_element_type=f32).astype(bf16)
    mixed, grad_attn = lax.optimization_barrier((mixed, grad_attn))
    block_out = (y1 + tp_scatter(mixed)).astype(bf16)

    grad_outw = lax.dot_general(grad_attn, attn_vals, (((0,), (0,)), ((), ())), preferred_element_type=f32)
    grad_outw = grad_outw.astype(bf16)
    grad_vals = jnp.dot(grad_attn, out_full, preferred_element_type=f32).astype(bf16)

    grads = []
    for s in range(heads):
        piece = lax.dynamic_slice_in_dim(grad_vals, jnp.bitwise_xor(my_head, s) * HEAD, HEAD, 1)
        grads.append(piece if s == 0 else ctx_xor(piece, s << 1))
    grads = jnp.concatenate(grads, axis=0)
    results = attention_backward(place, tiles, span, own, grads, mixed_t, lse, even, odd, *shape)
    grad_q, grad_kv, grad_odd = results
    got = ctx_xor(grad_odd, 1)
    for bit in reversed(far_bits):
        grad_kv = grad_kv + got.astype(f32)
        half = grad_kv.shape[0] // 2
        got = ctx_xor(grad_kv[half:].astype(bf16), 1 << bit)
        grad_kv = grad_kv[:half]
    got, block_out = lax.optimization_barrier((got, block_out))
    grad_own = merge(grad_q, grad_kv, got, heads)
    back = [grad_own[0]]
    for s in range(1, heads):
        back.append(ctx_xor(grad_own[s], s << 1))
    back = jnp.concatenate(back, axis=0)
    back, grad_outw = lax.optimization_barrier((back, grad_outw))
    by_head = [
        lax.dynamic_slice_in_dim(back, jnp.bitwise_xor(my_head, h) * rows, rows, 0) for h in range(heads)
    ]
    grad_qkv_in = jnp.concatenate(
        [by_head[h][:, j * HEAD : (j + 1) * HEAD] for j in range(3) for h in range(heads)], axis=1
    )
    chips = list(range(0, ctx_count, 2))
    sent = weight_grad(place, a1, grad_qkv_in, ctx_cols)
    sent, later, block_out = lax.optimization_barrier((sent, grad_qkv_in, tp_gather_first(block_out)))
    got = ctx_xor(sent, 1)
    grad_outw, pair_shard = lax.optimization_barrier((grad_outw, pair_shard))
    out_shard = lax.psum_scatter(grad_outw, "ctx", scatter_dimension=0, tiled=True)
    grad_h1 = input_grad(place, later, qkv_blocks, ctx_cols)
    block_out, grad_h1 = lax.optimization_barrier((tp_gather_last(block_out), grad_h1))
    summed = weight_grad(place, a1, grad_qkv_in, ctx_cols, got)
    grad_h1 = tp_send(grad_h1, summed)
    up_grad, down_grad, square = widen(pair_shard)
    arrived = [ctx_xor(summed[slot], mask) for slot, mask in enumerate(chips) if slot]
    grad_h1, _, up_grad, out_shard = lax.optimization_barrier((grad_h1, summed, up_grad, out_shard))
    grad_h1 = tp_total(grad_h1)
    block_out = slots_to_rows(block_out, tp_place)
    normed1, rstd1 = norm_parts(x_own)
    dx1, dg1, dc1 = norm_back(grad_h1, normed1, rstd1, gain_one)
    grad_tokens = (grad_y1 + dx1).astype(bf16)
    qkv_grad, out_grad, more = total_of([summed[0], *arrived], out_shard, head_cols)
    square = square[0, 0] + more[0, 0]
    lines = jnp.stack((dg1, dg2, dc1, dc2)).reshape(-1, HEAD)
    sent = jnp.concatenate((lines, jnp.full((8, HEAD), square, f32)), axis=0)
    sent, grad_tokens = lax.optimization_barrier((sent, tp_gather_first(grad_tokens)))
    total, grad_tokens = sum_over_all(sent, grad_tokens)
    grad_tokens = tp_gather_last(grad_tokens)
    small_grad = total[:-8].reshape(4, width)
    total_sq = total[-1, 0] + jnp.sum(small_grad * small_grad)
    grad_norm = jnp.sqrt(total_sq)
    factor = 1.0 / jnp.maximum(grad_norm, 1.0)
    small_own = lax.dynamic_slice_in_dim(small_grad, ctx_place * ctx_cols, ctx_cols, 1)

    flags = decay_mask.astype(f32)
    flat = lambda value: value.reshape(-1, head_cols)
    matrices = adam(
        factor,
        flags,
        (
            (flat(w_qkv), flat(qkv_grad), flat(m_qkv), flat(v_qkv)),
            (w_out, out_grad, m_out, v_out),
            (w_up, up_grad, m_up, v_up),
            (w_down, down_grad, m_down, v_down),
        ),
    )
    matrices[0] = [value.reshape(w_qkv.shape) for value in matrices[0]]
    gains_new = adam_update(norm_gains, small_own[:2], m_gains, v_gains, factor, flags[4])
    biases_new = adam_update(norm_biases, small_own[2:], m_biases, v_biases, factor, flags[5])
    grad_tokens = slots_to_rows(grad_tokens, tp_place)
    shards = (qkv_grad, out_grad, up_grad, down_grad, small_own[:2], small_own[2:])
    updates = list(zip(*matrices, gains_new, biases_new))
    return (block_out, grad_tokens, grad_norm, *shards, *updates[0], *updates[1], *updates[2])


def solution(mesh):
    small = P(None, "ctx")
    weights = (P(None, "ctx", "tp"), P("tp", "ctx"), P("ctx", "tp"), P("tp", "ctx"), small, small)
    rows = (P("ctx", None), P("ctx", None))
    return jax.shard_map(
        per_device,
        mesh=mesh,
        in_specs=(*rows, *weights, *weights, *weights, P(), P()),
        out_specs=(*rows, P(), *weights, *weights, *weights, *weights),
        check_vma=False,
    )
```
